32 devices in a mesh: walk: 2 (over core), det: 4 (over y, x), exc: 4 (over z).
Axes of the slice: x: 2, y: 2, z: 4, core: 2. Of those that a mesh axis runs over, the one named last changes fastest.
Arguments:
- inverse: bfloat16 [128, 128, 128], P(('walk', 'det', 'exc')), may hold values from -0.5 to 0.5
- virt_ref: bfloat16 [128, 128], replicated, may hold values from -6 to 6
- new_rows: bfloat16 [128, 128], P(('walk', 'det', 'exc')), may hold values from -6 to 6
- moved_electron: int32 [128], P(('walk', 'det', 'exc')), may hold values from 0 to 127
- coefficient: float32 [16384], P(('det', 'exc')), may hold values from -0.046875 to 0.046875
- occ_list: int32 [4, 16384], P(None, ('det', 'exc')), may hold values from 0 to 127
- virt_list: int32 [4, 16384], P(None, ('det', 'exc')), may hold values from 0 to 127
- exc_rank: int32 [16384], P(('det', 'exc')), may hold values from 1 to 4
Outputs:
- amplitude: float32 [128], P(('walk', 'det', 'exc'))
- ci_grad: float32 [16384], P(('det', 'exc'))
- orb_grad: float32 [128, 128], P('walk')
The draws below stay inside these ranges and needn't reach their ends.
All inputs are finite; a program needn't handle non-finite values.
Results may differ from the reference program's by a relative error of at most 0.0015.
The reference program's roundings to bfloat16 on the way count: a program that leaves them out, or rounds other values in their place, can miss the bound.
Values may be sent and summed in bfloat16 or wider, within the bound.
No kernel may reach another device: no remote copies, remote signals or barrier semaphores. Data moves between devices by JAX's collectives and lax.ppermute only.
A program may use at most 64 MiB of HBM per device.

```python
import jax
import jax.numpy as jnp
from jax import lax

N = 128
V = 128
MAXR = 4
TAB_DEV = 4
W = 128
NDET = 16384
N_DET = 4
N_EXC = 4


def plant(drawn, stream_key, low, top_value):
    place = [jax.random.randint(jax.random.fold_in(stream_key, axis), (), 0, length) for axis, length in enumerate(drawn.shape)]
    main_axis = drawn.shape.index(max(drawn.shape))
    next_to = place[:main_axis] + [(place[main_axis] + 1) % drawn.shape[main_axis]] + place[main_axis + 1:]
    return drawn.at[tuple(place)].set(low).at[tuple(next_to)].set(top_value)


def shard_levels(rng, dims, pieces, smallest, high):
    level, own = 1.0, jax.random.fold_in(rng, 6)
    for position, blocks in pieces:
        steps = jnp.exp(jax.random.uniform(jax.random.fold_in(own, position), (blocks,), jnp.float32, smallest / len(pieces), high / len(pieces)))
        level = level * jnp.repeat(steps, dims[position] // blocks).reshape([-1 if axis == position else 1 for axis in range(len(dims))])
    return level


def bell_draw(own_key, extent, width, bound, cuts=(), held_as=jnp.bfloat16):
    gain = shard_levels(own_key, extent, cuts, -0.22, 0.18) if cuts else 1.0
    values = jax.random.normal(own_key, extent, jnp.float32) * width * gain
    return jnp.minimum(jnp.maximum(values, -bound), bound).astype(held_as)


def setup_inputs(seed: int = 0) -> dict:
    splits = jax.random.split(jax.random.key(seed), 9)
    inverse = bell_draw(splits[0], (W, N, N), N ** -0.5, 0.5, ((0, 32),))
    virt_ref = bell_draw(splits[1], (N, V), 1.0, 6.0)
    new_rows = bell_draw(splits[2], (W, V), 1.0, 6.0, ((0, 32),))
    moved_electron = plant(jax.random.randint(splits[3], (W,), 0, N), jax.random.fold_in(splits[3], 1), 0, N - 1).astype(jnp.int32)
    coefficient = bell_draw(splits[4], (NDET,), NDET ** -0.5, 0.046875, ((0, 16),), jnp.float32)
    occ_list = plant(jax.random.randint(splits[5], (MAXR, NDET), 0, N), jax.random.fold_in(splits[5], 1), 0, N - 1).astype(jnp.int32)
    virt_list = plant(jax.random.randint(splits[6], (MAXR, NDET), 0, V), jax.random.fold_in(splits[6], 1), 0, V - 1).astype(jnp.int32)
    exc_rank = plant(jax.random.randint(splits[7], (NDET,), 1, MAXR + 1), jax.random.fold_in(splits[7], 1), 1, MAXR).astype(jnp.int32)
    return {"inverse": inverse, "virt_ref": virt_ref, "new_rows": new_rows, "moved_electron": moved_electron, "coefficient": coefficient, "occ_list": occ_list, "virt_list": virt_list, "exc_rank": exc_rank}


def minor_det(cells):
    top_a = cells[0] * cells[5] - cells[4] * cells[1]
    top_b = cells[0] * cells[6] - cells[4] * cells[2]
    top_c = cells[0] * cells[7] - cells[4] * cells[3]
    top_d = cells[1] * cells[6] - cells[5] * cells[2]
    top_e = cells[1] * cells[7] - cells[5] * cells[3]
    top_f = cells[2] * cells[7] - cells[6] * cells[3]
    low_f = cells[10] * cells[15] - cells[14] * cells[11]
    low_e = cells[9] * cells[15] - cells[13] * cells[11]
    low_d = cells[9] * cells[14] - cells[13] * cells[10]
    low_c = cells[8] * cells[15] - cells[12] * cells[11]
    low_b = cells[8] * cells[14] - cells[12] * cells[10]
    low_a = cells[8] * cells[13] - cells[12] * cells[9]
    return top_a * low_f - top_b * low_e + top_c * low_d + top_d * low_c - top_e * low_b + top_f * low_a

def build_minor(entries, exc_rank):
    cells = []
    for row_pos in range(4):
        for col_pos in range(4):
            inside = (exc_rank > row_pos) & (exc_rank > col_pos)
            filler = jnp.float32(1.0 if row_pos == col_pos else 0.0)
            cells.append(jnp.where(inside[None, :], entries[:, row_pos * 4 + col_pos, :], filler))
    return cells

def pair_index(occ_list, virt_list, nvirt):
    return (occ_list[:, None, :] * nvirt + virt_list[None, :, :]).reshape(16, occ_list.shape[1]).astype(jnp.int32)

def orbital_grad(weighted, pairs, nocc, nvirt):
    summed = jax.ops.segment_sum(weighted.reshape(-1), pairs.reshape(-1), num_segments=nocc * nvirt)
    return summed.reshape(nocc, nvirt)

def reference(inverse, virt_ref, new_rows, moved_electron, coefficient, occ_list, virt_list, exc_rank):
    displaced = jnp.arange(N, dtype=jnp.int32)[None, :, None] == moved_electron[:, None, None]
    basis = jnp.where(displaced, new_rows[:, None, :], virt_ref[None, :, :])
    tables = jnp.einsum('wji,wiv->wjv', inverse.astype(jnp.float32), basis.astype(jnp.float32), precision=lax.Precision.HIGHEST).astype(jnp.bfloat16)
    pairs = pair_index(occ_list, virt_list, V)
    block = TAB_DEV * N_DET * N_EXC

    def advance(running, table_block):
        grad_sum, cof_sum = running
        entries = jnp.take(table_block.reshape(block, N * V), pairs, axis=1).astype(jnp.float32)
        ratios, puller = jax.vjp(lambda values: minor_det(build_minor(values, exc_rank)), entries)
        amplitude = 1.0 + jnp.dot(ratios, coefficient, precision=lax.Precision.HIGHEST)
        weight = amplitude / (amplitude * amplitude + 1.0)
        grad_sum = grad_sum + jnp.dot(weight, ratios, precision=lax.Precision.HIGHEST)
        cofactor = puller(jnp.broadcast_to(weight[:, None], ratios.shape))[0]
        cof_sum = cof_sum + lax.optimization_barrier(jnp.sum(cofactor, axis=0))
        return ((grad_sum, cof_sum), amplitude)
    start_sums = (jnp.zeros((NDET,), jnp.float32), jnp.zeros((16, NDET), jnp.float32))
    (grad_sum, cof_sum), amplitudes = lax.scan(advance, start_sums, tables.reshape(W // block, block, N, V))
    ci_grad = grad_sum / W
    orb_grad = orbital_grad(cof_sum * coefficient[None, :] / W, pairs, N, V)
    return (amplitudes.reshape(W), ci_grad, orb_grad)
```

```python
import jax
import jax.numpy as jnp
from jax import lax
from jax.experimental import pallas as pl
from jax.experimental.pallas import tpu as pltpu
from jax.sharding import PartitionSpec as P

TILE = 256
DET_AXES = ("det", "exc")
ALL_AXES = ("walk", "det", "exc")


def pair_products(x, y):
    return (
        x[0] * y[1] - y[0] * x[1],
        x[0] * y[2] - y[0] * x[2],
        x[0] * y[3] - y[0] * x[3],
        x[1] * y[2] - y[1] * x[2],
        x[1] * y[3] - y[1] * x[3],
        x[2] * y[3] - y[2] * x[3],
    )


def cofactor_rows(x, y, q):
    qa, qb, qc, qd, qe, qf = q
    dx = (
        y[1] * qa + y[2] * qb + y[3] * qc,
        y[2] * qd + y[3] * qe - y[0] * qa,
        y[3] * qf - y[0] * qb - y[1] * qd,
        -(y[0] * qc + y[1] * qe + y[2] * qf),
    )
    dy = (
        -(x[1] * qa + x[2] * qb + x[3] * qc),
        x[0] * qa - x[2] * qd - x[3] * qe,
        x[0] * qb + x[1] * qd - x[3] * qf,
        x[0] * qc + x[1] * qe + x[2] * qf,
    )
    return dx, dy


def masked_cells(entries, rank):
    cells = []
    for a in range(4):
        row = []
        for b in range(4):
            fill = jnp.float32(1.0 if a == b else 0.0)
            row.append(jnp.where(rank > max(a, b), entries[b][a * 8 : a * 8 + 8], fill))
        cells.append(row)
    return cells


def halves(row):
    top = jnp.broadcast_to(row[:, :128], (4, 128))
    low = jnp.broadcast_to(row[:, 128:], (4, 128))
    return jnp.concatenate([top, low], axis=0)


def walker_sum(x):
    x = x + pltpu.roll(x, 1, 0)
    return x + pltpu.roll(x, 2, 0)


def kernel(
    walkers_total, moved_ref, inv_ref, virt_ref, rows_ref, pay_ref, amp_ref, ci_ref, orb_ref,
    tab, ent, rat, acc,
):
    nblk, _, width = pay_ref.shape
    per_block = width // TILE
    tiles = nblk * per_block
    iota16 = lax.broadcasted_iota(jnp.int32, (16, TILE), 0).astype(jnp.int16)
    one = jnp.ones((16, TILE), jnp.bfloat16)
    zero = jnp.zeros((16, TILE), jnp.bfloat16)

    for w in range(4):
        here = lax.broadcasted_iota(jnp.int32, (128, 128), 0) == moved_ref[w]
        basis = jnp.where(
            here,
            jnp.broadcast_to(rows_ref[w : w + 1, :].astype(jnp.float32), (128, 128)),
            virt_ref[...].astype(jnp.float32),
        ).astype(jnp.bfloat16)
        tab[w * 128 : (w + 1) * 128, :] = jnp.dot(
            inv_ref[w], basis, preferred_element_type=jnp.float32
        ).astype(jnp.bfloat16)

    def load(t):
        block = t // per_block
        lanes = pl.ds(pl.multiple_of((t % per_block) * TILE, TILE), TILE)
        rows = pay_ref[block, :, lanes]
        codes = rows[0:4].astype(jnp.int32)
        occ = jnp.right_shift(codes, 7)
        virt = jnp.bitwise_and(codes, 127)
        return occ, virt, rows[4:5], rows[5:6]

    def spread16(row):
        return jnp.broadcast_to(row, (16, TILE)).astype(jnp.int16)

    def one_hot(v16):
        parts = [jnp.where(v16 == iota16 + jnp.int16(16 * k), one, zero) for k in range(8)]
        return jnp.concatenate(parts, axis=0)

    srow = lax.broadcasted_iota(jnp.int32, (32, 512), 0)
    scol = lax.broadcasted_iota(jnp.int32, (32, 512), 1)
    pick = (jnp.right_shift(scol, 8) == (jnp.right_shift(srow, 2) & 1)) & (
        (jnp.right_shift(scol, 4) & 15) == (srow & 3) * 4 + jnp.right_shift(srow, 3)
    )
    gather_rows = jnp.where(pick, 1.0, 0.0).astype(jnp.bfloat16)

    acc[...] = jnp.zeros_like(acc)
    orb_ref[...] = jnp.zeros_like(orb_ref)

    def forward(t, total):
        occ, virt, rank, coef = load(t)
        occ16 = [spread16(occ[a : a + 1]) for a in range(4)]
        bits = [
            [(o & jnp.int16(bit)) != 0 for bit in (64, 32, 16)]
            + [(o & jnp.int16(15)) == iota16]
            for o in occ16
        ]
        entries = []
        for b in range(4):
            hot = one_hot(spread16(virt[b : b + 1]))
            picked = []
            for w in range(4):
                cols = jnp.dot(
                    tab[w * 128 : (w + 1) * 128, :], hot, preferred_element_type=jnp.float32
                ).astype(jnp.bfloat16)
                parts = [cols[16 * k : 16 * k + 16] for k in range(8)]
                for a in range(4):
                    level = parts
                    for step in range(3):
                        half = len(level) // 2
                        level = [
                            jnp.where(bits[a][step], level[k + half], level[k])
                            for k in range(half)
                        ]
                    picked.append(jnp.where(bits[a][3], level[0], zero))
            stack = jnp.concatenate(picked, axis=0)
            stack = jnp.concatenate([stack[:, :128], stack[:, 128:]], axis=0)
            got = jnp.dot(gather_rows, stack, preferred_element_type=jnp.float32)
            ent[t, b] = got
            entries.append(got)
        cells = masked_cells(entries, halves(rank))
        low = pair_products(cells[2], cells[3])
        top = pair_products(cells[0], cells[1])
        ratio = (
            top[0] * low[5]
            - top[1] * low[4]
            + top[2] * low[3]
            + top[3] * low[2]
            - top[4] * low[1]
            + top[5] * low[0]
        )
        rat[t] = ratio
        return total + ratio * halves(coef)

    total = lax.fori_loop(0, tiles, forward, jnp.zeros((8, 128), jnp.float32))
    lane_sum = jnp.broadcast_to(jnp.sum(total, axis=1, keepdims=True), (8, 128))
    amplitude = 1.0 + lane_sum + pltpu.roll(lane_sum, 4, 0)
    weight = amplitude / (amplitude * amplitude + 1.0)
    amp_ref[...] = amplitude
    weight = weight / walkers_total

    def backward(t, carry):
        occ, virt, rank_row, coef_row = load(t)
        rank = halves(rank_row)
        coef = halves(coef_row)
        summed = walker_sum(rat[t] * weight)
        block = t // per_block
        lane0 = pl.multiple_of((t % per_block) * TILE, TILE)
        ci_ref[block, :, pl.ds(lane0, 128)] = summed[3:4]
        ci_ref[block, :, pl.ds(lane0 + 128, 128)] = summed[7:8]

        cells = masked_cells([ent[t, b] for b in range(4)], rank)
        low = pair_products(cells[2], cells[3])
        top = pair_products(cells[0], cells[1])
        d0, d1 = cofactor_rows(
            cells[0], cells[1], (low[5], -low[4], low[3], low[2], -low[1], low[0])
        )
        d2, d3 = cofactor_rows(
            cells[2], cells[3], (top[5], -top[4], top[3], top[2], -top[1], top[0])
        )
        grads = [d0, d1, d2, d3]
        occ_half = [halves(occ[a : a + 1].astype(jnp.float32)) for a in range(4)]
        same = [[None] * 4 for _ in range(4)]
        for a in range(4):
            for c in range(a):
                same[a][c] = same[c][a] = occ_half[a] == occ_half[c]
        inside = [[rank > max(a, b) for b in range(4)] for a in range(4)]
        hot_occ = [spread16(occ[a : a + 1]) for a in range(4)]
        high_rows = []
        low_rows = []
        for b in range(4):
            plain = [
                jnp.where(inside[a][b], walker_sum(grads[a][b] * weight) * coef, 0.0)
                for a in range(4)
            ]
            high_rows.append([])
            low_rows.append([])
            for a in range(4):
                merged = plain[a]
                for c in range(4):
                    if c != a:
                        merged = merged + jnp.where(same[a][c], plain[c], 0.0)
                high = merged.astype(jnp.bfloat16).astype(jnp.float32)
                rest = merged - high
                for rows, value in ((high_rows[b], high), (low_rows[b], rest)):
                    wide = jnp.concatenate([value[3:4], value[7:8]], axis=1)
                    rows.append(jnp.broadcast_to(wide, (16, TILE)).astype(jnp.bfloat16))
        spread = [[[] for _ in range(4)] for _ in range(2)]
        for k in range(8):
            hits = [hot_occ[a] == iota16 + jnp.int16(16 * k) for a in range(4)]
            for b in range(4):
                for part, rows in enumerate((high_rows[b], low_rows[b])):
                    value = zero
                    for a in range(4):
                        value = jnp.where(hits[a], rows[a], value)
                    spread[part][b].append(value)
        out = None
        for b in range(4):
            left = jnp.concatenate(spread[0][b] + spread[1][b], axis=0)
            hot = one_hot(spread16(virt[b : b + 1]))
            got = lax.dot_general(
                left, hot, (((1,), (1,)), ((), ())), preferred_element_type=jnp.float32
            )
            out = got if out is None else out + got
        acc[...] += out
        return carry

    lax.fori_loop(0, tiles, backward, 0)
    orb_ref[...] = acc[0:128, :] + acc[128:256, :]


def per_device(
    inverse, virt_ref, new_rows, moved_electron, coefficient, occ_list, virt_list, exc_rank
):
    nocc = inverse.shape[1]
    nvirt = virt_ref.shape[1]
    walk_count = lax.axis_size("walk")
    blocks = lax.axis_size(DET_AXES)
    local = coefficient.shape[0]
    ndet = local * blocks
    walkers_total = inverse.shape[0] * walk_count * blocks
    payload = jnp.concatenate(
        [
            (occ_list * 128 + virt_list).astype(jnp.float32),
            exc_rank.astype(jnp.float32)[None],
            coefficient[None],
        ],
        axis=0,
    )
    gathered = lax.all_to_all(
        jnp.broadcast_to(payload[None], (blocks, 6, local)), DET_AXES, 0, 0
    )
    vmem = pl.BlockSpec(memory_space=pltpu.VMEM)
    tiles = ndet // TILE
    amp, ci_part, orb_part = pl.pallas_call(
        lambda *refs: kernel(float(walkers_total), *refs),
        out_shape=(
            jax.ShapeDtypeStruct((8, 128), jnp.float32),
            jax.ShapeDtypeStruct((blocks, 1, local), jnp.float32),
            jax.ShapeDtypeStruct((nocc, nvirt), jnp.float32),
        ),
        in_specs=[pl.BlockSpec(memory_space=pltpu.SMEM)] + [vmem] * 4,
        out_specs=(vmem, vmem, vmem),
        scratch_shapes=[
            pltpu.VMEM((512, 128), jnp.bfloat16),
            pltpu.VMEM((tiles, 4, 32, 128), jnp.float32),
            pltpu.VMEM((tiles, 8, 128), jnp.float32),
            pltpu.VMEM((256, 128), jnp.float32),
        ],
        compiler_params=pltpu.CompilerParams(vmem_limit_bytes=48 << 20),
    )(moved_electron, inverse, virt_ref, new_rows, gathered)

    ci_pieces = ci_part.reshape(blocks, walk_count, local // walk_count).transpose(1, 0, 2)
    orb_pieces = orb_part.reshape(walk_count, blocks, nocc * nvirt // (walk_count * blocks))
    pieces = jnp.concatenate([ci_pieces, orb_pieces], axis=2)
    everyone = walk_count * blocks
    pieces = pieces.reshape(everyone, pieces.shape[2])
    mine = jnp.sum(lax.all_to_all(pieces, ALL_AXES, 0, 0), axis=0)
    ci_mine = mine[: local // walk_count]
    orb_mine = mine[local // walk_count :]
    ci_grad = lax.all_gather(ci_mine, "walk", axis=0, tiled=True)
    orb_all = lax.all_to_all(
        jnp.broadcast_to(orb_mine[None], (blocks, orb_mine.shape[0])), DET_AXES, 0, 0
    )
    return (amp[:4, 0], ci_grad, orb_all.reshape(nocc // walk_count, nvirt))


def solution(mesh):
    return jax.shard_map(
        per_device,
        mesh=mesh,
        in_specs=(
            P(ALL_AXES, None, None),
            P(),
            P(ALL_AXES, None),
            P(ALL_AXES),
            P(DET_AXES),
            P(None, DET_AXES),
            P(None, DET_AXES),
            P(DET_AXES),
        ),
        out_specs=(P(ALL_AXES), P(DET_AXES), P("walk", None)),
        check_vma=False,
    )
```

```python
import jax
import jax.numpy as jnp
from jax import lax
from jax.experimental import pallas as pl
from jax.experimental.pallas import tpu as pltpu
from jax.sharding import PartitionSpec as P

TILE = 256
LANES = 128
DET_AXES = ("det", "exc")
ALL_AXES = ("walk", "det", "exc")
FINE = 64.0


def pair_products(x, y):
    return (
        x[0] * y[1] - y[0] * x[1],
        x[0] * y[2] - y[0] * x[2],
        x[0] * y[3] - y[0] * x[3],
        x[1] * y[2] - y[1] * x[2],
        x[1] * y[3] - y[1] * x[3],
        x[2] * y[3] - y[2] * x[3],
    )


def cofactor_rows(x, y, q):
    qa, qb, qc, qd, qe, qf = q
    dx = (
        y[1] * qa + y[2] * qb + y[3] * qc,
        y[2] * qd + y[3] * qe - y[0] * qa,
        y[3] * qf - y[0] * qb - y[1] * qd,
        -(y[0] * qc + y[1] * qe + y[2] * qf),
    )
    dy = (
        -(x[1] * qa + x[2] * qb + x[3] * qc),
        x[0] * qa - x[2] * qd - x[3] * qe,
        x[0] * qb + x[1] * qd - x[3] * qf,
        x[0] * qc + x[1] * qe + x[2] * qf,
    )
    return dx, dy


def masked_cells(entries, rank):
    cells = []
    for a in range(4):
        row = []
        for b in range(4):
            fill = jnp.float32(1.0 if a == b else 0.0)
            row.append(jnp.where(rank > max(a, b), entries[b][a], fill))
        cells.append(row)
    return cells


def determinant(top, low):
    return (
        top[0] * low[5]
        - top[1] * low[4]
        + top[2] * low[3]
        + top[3] * low[2]
        - top[4] * low[1]
        + top[5] * low[0]
    )


def rows8(row):
    return jnp.broadcast_to(row, (8, row.shape[1]))


def rows16(row):
    return jnp.broadcast_to(row, (16, row.shape[1])).astype(jnp.int16)


def iota16():
    return lax.broadcasted_iota(jnp.int32, (16, TILE), 0).astype(jnp.int16)


def one_hot(v16, values):
    base = iota16()
    zero = jnp.zeros((16, TILE), jnp.bfloat16)
    hits = [v16 == base + jnp.int16(16 * k) for k in range(8)]
    parts = [
        jnp.where(hit, jnp.full((16, TILE), value, jnp.bfloat16), zero)
        for value in values
        for hit in hits
    ]
    return jnp.concatenate(parts, axis=0)


def load_lists(pay_ref, t):
    per_block = pay_ref.shape[2] // TILE
    lanes = pl.ds(pl.multiple_of((t % per_block) * TILE, TILE), TILE)
    rows = pay_ref[t // per_block, :, lanes]
    codes = rows[0:4].astype(jnp.int32)
    return jnp.right_shift(codes, 7), jnp.bitwise_and(codes, 127), rows[4:5], rows[5:6]


def power_scale(top):
    scale = jnp.ones_like(top)
    back = jnp.ones_like(top)
    for k in (64, 32, 16, 8, 4, 2, 1):
        big = top >= 2.0 ** (5 + k)
        small = top < 2.0 ** (6 - k)
        up = jnp.float32(2.0**k)
        down = jnp.float32(2.0**-k)
        step = jnp.where(big, down, jnp.where(small, up, 1.0))
        undo = jnp.where(big, up, jnp.where(small, down, 1.0))
        top = top * step
        scale = scale * step
        back = back * undo
    return scale, back


def select_kernel(
    inv_ref, inv2_ref, aux_ref, aux2_ref, virt_ref, pay_ref, ent_ref, amp_ref, wide, tab
):
    nblk, _, width = pay_ref.shape
    tiles = nblk * width // TILE
    sub = lax.broadcasted_iota(jnp.int32, (8, LANES), 0)
    rows_of = lax.broadcasted_iota(jnp.int32, (128, LANES), 0).astype(jnp.float32)
    tops = jnp.zeros((8, LANES), jnp.float32)
    for w in range(8):
        inv, aux = (inv_ref, aux_ref) if w < 4 else (inv2_ref, aux2_ref)
        aux_rows = aux[...].astype(jnp.float32)
        fresh = jnp.broadcast_to(aux_rows[w % 4 : w % 4 + 1], (128, LANES))
        moved = jnp.broadcast_to(aux_rows[w % 4 + 4 : w % 4 + 5], (128, LANES))
        basis = jnp.where(rows_of == moved, fresh, virt_ref[...].astype(jnp.float32))
        table = jnp.dot(
            inv[w % 4], basis.astype(jnp.bfloat16), preferred_element_type=jnp.float32
        )
        table = table.astype(jnp.bfloat16).astype(jnp.float32)
        wide[pl.ds(w, 128, stride=8), :] = table
        tops = jnp.where(sub == w, jnp.max(jnp.abs(table)), tops)
    scale, back = power_scale(tops)
    for k in range(16):
        block = wide[64 * k : 64 * k + 64, :] * jnp.concatenate([scale] * 8, axis=0)
        coarse = block.astype(jnp.float8_e4m3fn)
        rest = (block - coarse.astype(jnp.float32)) * FINE
        tab[64 * k : 64 * k + 64, 0:128] = coarse
        tab[64 * k : 64 * k + 64, 128:256] = rest.astype(jnp.float8_e4m3fn)

    def forward(t, total):
        occ, virt, rank, coef = load_lists(pay_ref, t)
        occ16 = [rows16(occ[a : a + 1]) for a in range(4)]
        bits = [[(o & jnp.int16(bit)) != 0 for bit in (2, 4, 8, 16, 32, 64)] for o in occ16]
        odd = [(rows8(occ[a : a + 1]) & 1) != 0 for a in range(4)]
        entries = [[None] * 4 for _ in range(4)]
        for b in range(4):
            hot = one_hot(rows16(virt[b : b + 1]), (1.0, 1.0 / FINE)).astype(jnp.float8_e4m3fn)
            cols = jnp.dot(tab[...], hot, preferred_element_type=jnp.float32)
            cols = cols.astype(jnp.bfloat16)
            parts = [cols[16 * k : 16 * k + 16] for k in range(64)]
            for a in range(4):
                level = parts
                for step in range(6):
                    level = [
                        jnp.where(bits[a][step], level[2 * k + 1], level[2 * k])
                        for k in range(len(level) // 2)
                    ]
                last = level[0].astype(jnp.float32)
                last = jnp.where(odd[a], last[8:16], last[0:8])
                entries[b][a] = [
                    last[:, h * LANES : (h + 1) * LANES] * back for h in range(TILE // LANES)
                ]
        for h in range(TILE // LANES):
            lanes = slice(h * LANES, (h + 1) * LANES)
            mine = [[entries[b][a][h] for a in range(4)] for b in range(4)]
            for b in range(4):
                for a in range(0, 4, 2):
                    pair = jnp.concatenate([mine[b][a], mine[b][a + 1]], axis=0)
                    ent_ref[t * (TILE // LANES) + h, b, a // 2] = pair.astype(jnp.bfloat16)
            cells = masked_cells(mine, rows8(rank[:, lanes]))
            ratio = determinant(
                pair_products(cells[0], cells[1]), pair_products(cells[2], cells[3])
            )
            total = total + ratio * rows8(coef[:, lanes])
        return total

    total = lax.fori_loop(0, tiles, forward, jnp.zeros((8, LANES), jnp.float32))
    amp_ref[...] = jnp.broadcast_to(jnp.sum(total, axis=1, keepdims=True), (8, LANES))


def all_rows_sum(x):
    x = x + pltpu.roll(x, 4, 0)
    x = x + pltpu.roll(x, 2, 0)
    return x + pltpu.roll(x, 1, 0)


def gradient_kernel(
    walkers_total, part_ref, part2_ref, ent_ref, pay_ref, amp_ref, ci_ref, orb_ref, acc
):
    nblk, _, width = pay_ref.shape
    per_block = width // TILE
    tiles = nblk * per_block
    zero = jnp.zeros((16, TILE), jnp.bfloat16)
    amplitude = 1.0 + part_ref[...] + pltpu.roll(part2_ref[...], 4, 0)
    amp_ref[...] = amplitude
    weight = amplitude / (amplitude * amplitude + 1.0) / walkers_total
    acc[...] = jnp.zeros_like(acc)

    def backward(t, carry):
        occ, virt, rank_row, coef_row = load_lists(pay_ref, t)
        occ16 = [rows16(occ[a : a + 1]) for a in range(4)]
        high = [[[] for _ in range(4)] for _ in range(4)]
        rest = [[[] for _ in range(4)] for _ in range(4)]
        for h in range(TILE // LANES):
            lanes = slice(h * LANES, (h + 1) * LANES)
            rank = rows8(rank_row[:, lanes])
            coef = rows8(coef_row[:, lanes])
            entries = []
            for b in range(4):
                row = []
                for a in range(0, 4, 2):
                    pair = ent_ref[t * (TILE // LANES) + h, b, a // 2].astype(jnp.float32)
                    row += [pair[0:8], pair[8:16]]
                entries.append(row)
            cells = masked_cells(entries, rank)
            low = pair_products(cells[2], cells[3])
            top = pair_products(cells[0], cells[1])
            summed = all_rows_sum(determinant(top, low) * weight)
            lane0 = pl.multiple_of((t % per_block) * TILE, TILE) + h * LANES
            ci_ref[t // per_block, :, pl.ds(lane0, LANES)] = summed[0:1]
            d0, d1 = cofactor_rows(
                cells[0], cells[1], (low[5], -low[4], low[3], low[2], -low[1], low[0])
            )
            d2, d3 = cofactor_rows(
                cells[2], cells[3], (top[5], -top[4], top[3], top[2], -top[1], top[0])
            )
            grads = [d0, d1, d2, d3]
            occ8 = [rows8(occ[a : a + 1, lanes]) for a in range(4)]
            same = {(a, c): occ8[a] == occ8[c] for a in range(4) for c in range(a)}
            for b in range(4):
                plain = [
                    jnp.where(
                        rank > max(a, b), all_rows_sum(grads[a][b] * weight) * coef, 0.0
                    )
                    for a in range(4)
                ]
                for a in range(4):
                    merged = plain[a]
                    for c in range(4):
                        if c != a:
                            hit = same[max(a, c), min(a, c)]
                            merged = merged + jnp.where(hit, plain[c], 0.0)
                    both = jnp.concatenate([merged, merged], axis=0)
                    coarse = both.astype(jnp.bfloat16)
                    high[b][a].append(coarse)
                    rest[b][a].append((both - coarse.astype(jnp.float32)).astype(jnp.bfloat16))
        out = None
        for b in range(4):
            left = []
            for rows in (high[b], rest[b]):
                wide = [jnp.concatenate(rows[a], axis=1) for a in range(4)]
                for k in range(8):
                    value = zero
                    for a in range(4):
                        value = jnp.where(
                            occ16[a] == iota16() + jnp.int16(16 * k), wide[a], value
                        )
                    left.append(value)
            left = jnp.concatenate(left, axis=0)
            hot = one_hot(rows16(virt[b : b + 1]), (1.0,))
            got = lax.dot_general(
                left, hot, (((1,), (1,)), ((), ())), preferred_element_type=jnp.float32
            )
            out = got if out is None else out + got
        acc[...] += out
        return carry

    lax.fori_loop(0, tiles, backward, 0)
    orb_ref[...] = acc[0:128, :] + acc[128:256, :]


def per_device(
    inverse, virt_ref, new_rows, moved_electron, coefficient, occ_list, virt_list, exc_rank
):
    nocc = inverse.shape[1]
    nvirt = virt_ref.shape[1]
    walk_count = lax.axis_size("walk")
    blocks = lax.axis_size(DET_AXES)
    everyone = walk_count * blocks
    local = coefficient.shape[0]
    half = local // 2
    ndet = half * blocks
    walkers_total = inverse.shape[0] * everyone
    partner = [(u, u ^ 1) for u in range(walk_count)]

    aux = jnp.concatenate(
        [
            new_rows,
            jnp.broadcast_to(moved_electron[:, None], (4, nvirt)).astype(jnp.bfloat16),
        ],
        axis=0,
    )
    inverse2 = lax.ppermute(inverse, "walk", partner)
    aux2 = lax.ppermute(aux, "walk", partner)
    payload = jnp.concatenate(
        [
            (occ_list * 128 + virt_list).astype(jnp.float32),
            exc_rank.astype(jnp.float32)[None],
            coefficient[None],
        ],
        axis=0,
    )
    start = (lax.axis_index("walk") & 1) * half
    payload = lax.dynamic_slice_in_dim(payload, start, half, 1)
    gathered = lax.all_to_all(jnp.broadcast_to(payload[None], (blocks, 6, half)), DET_AXES, 0, 0)

    vmem = pl.BlockSpec(memory_space=pltpu.VMEM)
    lane_tiles = ndet // LANES
    params = pltpu.CompilerParams(vmem_limit_bytes=32 << 20)
    entries, part = pl.pallas_call(
        select_kernel,
        out_shape=(
            jax.ShapeDtypeStruct((lane_tiles, 4, 2, 16, LANES), jnp.bfloat16),
            jax.ShapeDtypeStruct((8, LANES), jnp.float32),
        ),
        in_specs=[vmem] * 6,
        out_specs=(vmem, vmem),
        scratch_shapes=[
            pltpu.VMEM((1024, LANES), jnp.float32),
            pltpu.VMEM((1024, 2 * LANES), jnp.float8_e4m3fn),
        ],
        compiler_params=params,
    )(inverse, inverse2, aux, aux2, virt_ref, gathered)
    part2 = lax.ppermute(part, "walk", partner)
    amp, ci_part, orb_part = pl.pallas_call(
        lambda *refs: gradient_kernel(float(walkers_total), *refs),
        out_shape=(
            jax.ShapeDtypeStruct((8, LANES), jnp.float32),
            jax.ShapeDtypeStruct((blocks, 1, half), jnp.float32),
            jax.ShapeDtypeStruct((nocc, nvirt), jnp.float32),
        ),
        in_specs=[vmem] * 4,
        out_specs=(vmem, vmem, vmem),
        scratch_shapes=[pltpu.VMEM((256, LANES), jnp.float32)],
        compiler_params=params,
    )(part, part2, entries, gathered)

    ci_size = half // walk_count
    orb_size = nocc * nvirt // everyone
    ci_pieces = ci_part.reshape(blocks, walk_count, ci_size).transpose(1, 0, 2)
    orb_pieces = orb_part.reshape(walk_count, blocks, orb_size)
    pieces = jnp.concatenate([orb_pieces, ci_pieces], axis=2).reshape(everyone, -1)
    pieces = lax.all_to_all(pieces, ALL_AXES, 0, 0)
    pieces = pieces.reshape(walk_count // 2, 2, blocks, -1)
    orb_mine = jnp.sum(pieces[..., :orb_size], axis=(0, 1, 2))
    ci_mine = jnp.sum(pieces[..., orb_size:], axis=(0, 2))
    orb_all = lax.all_to_all(
        jnp.broadcast_to(orb_mine[None], (blocks, orb_size)), DET_AXES, 0, 0
    )
    ci_grad = lax.all_gather(ci_mine, "walk", axis=1).reshape(local)
    return (amp[:4, 0], ci_grad, orb_all.reshape(nocc // walk_count, nvirt))


def solution(mesh):
    return jax.shard_map(
        per_device,
        mesh=mesh,
        in_specs=(
            P(ALL_AXES, None, None),
            P(),
            P(ALL_AXES, None),
            P(ALL_AXES),
            P(DET_AXES),
            P(None, DET_AXES),
            P(None, DET_AXES),
            P(DET_AXES),
        ),
        out_specs=(P(ALL_AXES), P(DET_AXES), P("walk", None)),
        check_vma=False,
    )
```

```python
import jax
import jax.numpy as jnp
from jax import lax
from jax.experimental import pallas as pl
from jax.experimental.pallas import tpu as pltpu
from jax.sharding import PartitionSpec as P

TILE = 256
LANES = 128
DET_AXES = ("det", "exc")
ALL_AXES = ("walk", "det", "exc")
FINE = 64.0


def pair_products(x, y):
    return (
        x[0] * y[1] - y[0] * x[1],
        x[0] * y[2] - y[0] * x[2],
        x[0] * y[3] - y[0] * x[3],
        x[1] * y[2] - y[1] * x[2],
        x[1] * y[3] - y[1] * x[3],
        x[2] * y[3] - y[2] * x[3],
    )


def cofactor_rows(x, y, q):
    qa, qb, qc, qd, qe, qf = q
    dx = (
        y[1] * qa + y[2] * qb + y[3] * qc,
        y[2] * qd + y[3] * qe - y[0] * qa,
        y[3] * qf - y[0] * qb - y[1] * qd,
        -(y[0] * qc + y[1] * qe + y[2] * qf),
    )
    dy = (
        -(x[1] * qa + x[2] * qb + x[3] * qc),
        x[0] * qa - x[2] * qd - x[3] * qe,
        x[0] * qb + x[1] * qd - x[3] * qf,
        x[0] * qc + x[1] * qe + x[2] * qf,
    )
    return dx, dy


def masked_cells(entries, rank):
    cells = []
    for a in range(4):
        row = []
        for b in range(4):
            fill = jnp.float32(1.0 if a == b else 0.0)
            row.append(jnp.where(rank > max(a, b), entries[b][a], fill))
        cells.append(row)
    return cells


def determinant(top, low):
    return (
        top[0] * low[5]
        - top[1] * low[4]
        + top[2] * low[3]
        + top[3] * low[2]
        - top[4] * low[1]
        + top[5] * low[0]
    )


def rows8(row):
    return jnp.broadcast_to(row, (8, row.shape[1]))


def rows16(row):
    return jnp.broadcast_to(row, (16, row.shape[1])).astype(jnp.int16)


def iota16():
    return lax.broadcasted_iota(jnp.int32, (16, TILE), 0).astype(jnp.int16)


def one_hot(v16, values):
    base = iota16()
    zero = jnp.zeros((16, TILE), jnp.bfloat16)
    hits = [v16 == base + jnp.int16(16 * k) for k in range(8)]
    parts = [
        jnp.where(hit, jnp.full((16, TILE), value, jnp.bfloat16), zero)
        for value in values
        for hit in hits
    ]
    return jnp.concatenate(parts, axis=0)


def load_lists(pay_ref, t):
    per_block = pay_ref.shape[2] // TILE
    lanes = pl.ds(pl.multiple_of((t % per_block) * TILE, TILE), TILE)
    rows = pay_ref[t // per_block, :, lanes]
    codes = rows[0:4].astype(jnp.int32)
    return jnp.right_shift(codes, 7), jnp.bitwise_and(codes, 127), rows[4:5], rows[5:6]


def power_scale(top):
    scale = jnp.ones_like(top)
    back = jnp.ones_like(top)
    for k in (64, 32, 16, 8, 4, 2, 1):
        big = top >= 2.0 ** (5 + k)
        small = top < 2.0 ** (6 - k)
        up = jnp.float32(2.0**k)
        down = jnp.float32(2.0**-k)
        step = jnp.where(big, down, jnp.where(small, up, 1.0))
        undo = jnp.where(big, up, jnp.where(small, down, 1.0))
        top = top * step
        scale = scale * step
        back = back * undo
    return scale, back


def payload_kernel(occ_ref, virt_ref, rank_ref, coef_ref, rows_ref, moved_ref, pay_ref, aux_ref):
    blocks, _, half = pay_ref.shape
    start = pl.multiple_of((lax.axis_index("walk") & 1) * half, LANES)
    lanes = pl.ds(start, half)
    codes = (occ_ref[:, lanes] * 128 + virt_ref[:, lanes]).astype(jnp.float32)
    rank = rank_ref[:, lanes].astype(jnp.float32)
    coef = coef_ref[:, lanes]
    rows = jnp.concatenate([codes, rank, coef], axis=0)
    for k in range(blocks):
        pay_ref[k] = rows
    sub = lax.broadcasted_iota(jnp.int32, (4, LANES), 0)
    moved = jnp.zeros((4, LANES), jnp.float32)
    for w in range(4):
        moved = jnp.where(sub == w, moved_ref[w].astype(jnp.float32), moved)
    aux_ref[...] = jnp.concatenate(
        [rows_ref[...].astype(jnp.float32), moved], axis=0
    ).astype(jnp.bfloat16)


def table_kernel(inv_ref, inv2_ref, aux_ref, aux2_ref, virt_ref, tab, back_ref, wide):
    sub = lax.broadcasted_iota(jnp.int32, (8, LANES), 0)
    rows_of = lax.broadcasted_iota(jnp.int32, (128, LANES), 0).astype(jnp.float32)
    tops = jnp.zeros((8, LANES), jnp.float32)
    for w in range(8):
        inv, aux = (inv_ref, aux_ref) if w < 4 else (inv2_ref, aux2_ref)
        aux_rows = aux[...].astype(jnp.float32)
        fresh = jnp.broadcast_to(aux_rows[w % 4 : w % 4 + 1], (128, LANES))
        moved = jnp.broadcast_to(aux_rows[w % 4 + 4 : w % 4 + 5], (128, LANES))
        basis = jnp.where(rows_of == moved, fresh, virt_ref[...].astype(jnp.float32))
        table = jnp.dot(
            inv[w % 4], basis.astype(jnp.bfloat16), preferred_element_type=jnp.float32
        )
        table = table.astype(jnp.bfloat16).astype(jnp.float32)
        wide[pl.ds(w, 128, stride=8), :] = table
        tops = jnp.where(sub == w, jnp.max(jnp.abs(table)), tops)
    scale, back = power_scale(tops)
    back_ref[...] = back
    for k in range(16):
        block = wide[64 * k : 64 * k + 64, :] * jnp.concatenate([scale] * 8, axis=0)
        coarse = block.astype(jnp.float8_e4m3fn)
        rest = (block - coarse.astype(jnp.float32)) * FINE
        tab[64 * k : 64 * k + 64, 0:128] = coarse
        tab[64 * k : 64 * k + 64, 128:256] = rest.astype(jnp.float8_e4m3fn)


def select_kernel(tab, back_ref, pay_ref, ent_ref, amp_ref):
    nblk, _, width = pay_ref.shape
    tiles = nblk * width // TILE
    back = back_ref[...]

    def forward(t, total):
        occ, virt, rank, coef = load_lists(pay_ref, t)
        occ16 = [rows16(occ[a : a + 1]) for a in range(4)]
        bits = [[(o & jnp.int16(bit)) != 0 for bit in (2, 4, 8, 16, 32, 64)] for o in occ16]
        odd = [(rows8(occ[a : a + 1]) & 1) != 0 for a in range(4)]
        entries = [[None] * 4 for _ in range(4)]
        for b in range(4):
            hot = one_hot(rows16(virt[b : b + 1]), (1.0, 1.0 / FINE)).astype(jnp.float8_e4m3fn)
            cols = jnp.dot(tab[...], hot, preferred_element_type=jnp.float32)
            cols = cols.astype(jnp.bfloat16)
            parts = [cols[16 * k : 16 * k + 16] for k in range(64)]
            for a in range(4):
                level = parts
                for step in range(6):
                    level = [
                        jnp.where(bits[a][step], level[2 * k + 1], level[2 * k])
                        for k in range(len(level) // 2)
                    ]
                last = level[0].astype(jnp.float32)
                last = jnp.where(odd[a], last[8:16], last[0:8])
                entries[b][a] = [
                    last[:, h * LANES : (h + 1) * LANES] * back for h in range(TILE // LANES)
                ]
        for h in range(TILE // LANES):
            lanes = slice(h * LANES, (h + 1) * LANES)
            mine = [[entries[b][a][h] for a in range(4)] for b in range(4)]
            for b in range(4):
                for a in range(0, 4, 2):
                    pair = jnp.concatenate([mine[b][a], mine[b][a + 1]], axis=0)
                    ent_ref[t * (TILE // LANES) + h, b, a // 2] = pair.astype(jnp.bfloat16)
            cells = masked_cells(mine, rows8(rank[:, lanes]))
            ratio = determinant(
                pair_products(cells[0], cells[1]), pair_products(cells[2], cells[3])
            )
            total = total + ratio * rows8(coef[:, lanes])
        return total

    total = lax.fori_loop(0, tiles, forward, jnp.zeros((8, LANES), jnp.float32), unroll=2)
    amp_ref[...] = jnp.broadcast_to(jnp.sum(total, axis=1, keepdims=True), (8, LANES))


def all_rows_sum(x):
    x = x + pltpu.roll(x, 4, 0)
    x = x + pltpu.roll(x, 2, 0)
    return x + pltpu.roll(x, 1, 0)


def fold(items, dist):
    sub = lax.broadcasted_iota(jnp.int32, (8, LANES), 0)
    first = (sub & dist) == 0
    n = len(items) // 2
    out = []
    for x, y in zip(items[:n], items[n:]):
        x = x + pltpu.roll(x, 8 - dist, 0)
        y = y + pltpu.roll(y, dist, 0)
        out.append(jnp.where(first, x, y))
    return out


def walker_sums(items):
    for dist in (4, 2, 1):
        items = fold(items, dist)
    return items[0]


def two_rows(x, y):
    top = lax.broadcasted_iota(jnp.int32, (8, LANES), 0) < 4
    return jnp.where(top, rows8(x), rows8(y))


def gradient_kernel(
    walkers_total, part_ref, part2_ref, ent_ref, pay_ref, amp_ref, ci_ref, orb_ref, acc
):
    nblk, _, width = pay_ref.shape
    per_block = width // TILE
    tiles = nblk * per_block
    packed = len(orb_ref.shape) == 3
    ci_rows = width // LANES * nblk // orb_ref.shape[0]
    zero = jnp.zeros((16, TILE), jnp.bfloat16)
    amplitude = 1.0 + part_ref[...] + pltpu.roll(part2_ref[...], 4, 0)
    amp_ref[...] = amplitude
    weight = amplitude / (amplitude * amplitude + 1.0) / walkers_total
    sub = lax.broadcasted_iota(jnp.int32, (8, LANES), 0)
    slot_b = sub & 3
    limits = [
        jnp.maximum(slot_b, jnp.right_shift(sub, 2) + 2 * g).astype(jnp.float32) for g in range(2)
    ]

    def backward(t, carry):
        occ, virt, rank_row, coef_row = load_lists(pay_ref, t)
        occ16 = [rows16(occ[a : a + 1]) for a in range(4)]
        wide = [[[] for _ in range(16)] for _ in range(2)]
        for h in range(TILE // LANES):
            lanes = slice(h * LANES, (h + 1) * LANES)
            rank = rows8(rank_row[:, lanes])
            coef = rows8(coef_row[:, lanes])
            entries = []
            for b in range(4):
                row = []
                for a in range(0, 4, 2):
                    pair = ent_ref[t * (TILE // LANES) + h, b, a // 2].astype(jnp.float32)
                    row += [pair[0:8], pair[8:16]]
                entries.append(row)
            cells = masked_cells(entries, rank)
            low = [x * weight for x in pair_products(cells[2], cells[3])]
            top = pair_products(cells[0], cells[1])
            summed = all_rows_sum(determinant(top, low))
            block = t // per_block
            lane_tile = (t % per_block) * (TILE // LANES) + h
            if packed:
                dest = lane_tile // (ci_rows) * nblk + block
                orb_ref[dest, pl.ds(4 + lane_tile % ci_rows, 1), :] = summed[0:1]
            else:
                ci_ref[block, pl.ds(lane_tile, 1), :] = summed[0:1]
            top = [x * weight for x in top]
            d0, d1 = cofactor_rows(
                cells[0], cells[1], (low[5], -low[4], low[3], low[2], -low[1], low[0])
            )
            d2, d3 = cofactor_rows(
                cells[2], cells[3], (top[5], -top[4], top[3], top[2], -top[1], top[0])
            )
            plain = [
                jnp.where(rank > limits[g], walker_sums(list(x + y)) * coef, 0.0)
                for g, (x, y) in enumerate(((d0, d1), (d2, d3)))
            ]
            turned = [pltpu.roll(x, 4, 0) for x in plain]
            occ_a = two_rows(occ[0:1, lanes], occ[1:2, lanes])
            occ_b = two_rows(occ[2:3, lanes], occ[3:4, lanes])
            turn_a = two_rows(occ[1:2, lanes], occ[0:1, lanes])
            turn_b = two_rows(occ[3:4, lanes], occ[2:3, lanes])
            straight = occ_a == occ_b
            merged = [
                plain[0]
                + jnp.where(occ_a == turn_a, turned[0], 0.0)
                + jnp.where(straight, plain[1], 0.0)
                + jnp.where(occ_a == turn_b, turned[1], 0.0),
                plain[1]
                + jnp.where(occ_b == turn_b, turned[1], 0.0)
                + jnp.where(straight, plain[0], 0.0)
                + jnp.where(occ_b == turn_a, turned[0], 0.0),
            ]
            for g in range(2):
                high = merged[g].astype(jnp.bfloat16).astype(jnp.float32)
                rest = merged[g] - high
                for part, value in enumerate((high, rest)):
                    for r in range(8):
                        one = rows8(value[r : r + 1])
                        wide[part][8 * g + r].append(
                            jnp.concatenate([one, one], axis=0).astype(jnp.bfloat16)
                        )
        wide = [[jnp.concatenate(x, axis=1) for x in rows] for rows in wide]
        left = [[None] * 16 for _ in range(4)]
        for k in range(8):
            hits = [occ16[a] == iota16() + jnp.int16(16 * k) for a in range(4)]
            for part in range(2):
                for b in range(4):
                    value = zero
                    for a in range(4):
                        value = jnp.where(hits[a], wide[part][4 * a + b], value)
                    left[b][part * 8 + k] = value
        left = jnp.concatenate([jnp.concatenate(left[b], axis=0) for b in range(4)], axis=1)
        right = jnp.concatenate(
            [one_hot(rows16(virt[b : b + 1]), (1.0,)) for b in range(4)], axis=1
        )
        acc[...] += lax.dot_general(
            left, right, (((1,), (1,)), ((), ())), preferred_element_type=jnp.float32
        )
        return carry

    acc[...] = jnp.zeros_like(acc)
    if packed:
        orb_ref[...] = jnp.zeros_like(orb_ref)
    lax.fori_loop(0, tiles, backward, 0, unroll=4)
    total = acc[0:128, :] + acc[128:256, :]
    if packed:
        for dest in range(orb_ref.shape[0]):
            orb_ref[dest, 0:4, :] = total[4 * dest : 4 * dest + 4]
    else:
        orb_ref[...] = total


def sums_kernel(pieces_ref, orb_ref, ci_ref):
    everyone = pieces_ref.shape[0]
    blocks = orb_ref.shape[0] // 4
    totals = []
    for parity in range(2):
        picked = [
            pieces_ref[s] for s in range(everyone) if (s // blocks) % 2 == parity
        ]
        while len(picked) > 1:
            picked = [x + y for x, y in zip(picked[::2], picked[1::2])]
        totals.append(picked[0])
    both = totals[0] + totals[1]
    pair = jnp.concatenate([both[0:4], both[0:4]], axis=0)
    for k in range(blocks // 2):
        orb_ref[8 * k : 8 * k + 8, :] = pair
    ci_ref[...] = jnp.concatenate([totals[0][4:6], totals[1][4:6]], axis=0)


def per_device(
    inverse, virt_ref, new_rows, moved_electron, coefficient, occ_list, virt_list, exc_rank
):
    nocc = inverse.shape[1]
    nvirt = virt_ref.shape[1]
    walk_count = lax.axis_size("walk")
    blocks = lax.axis_size(DET_AXES)
    everyone = walk_count * blocks
    local = coefficient.shape[0]
    half = local // 2
    ndet = half * blocks
    walkers_total = inverse.shape[0] * everyone
    partner = [(u, u ^ 1) for u in range(walk_count)]
    vmem = pl.BlockSpec(memory_space=pltpu.VMEM)
    smem = pl.BlockSpec(memory_space=pltpu.SMEM)
    params = pltpu.CompilerParams(vmem_limit_bytes=32 << 20)

    inverse2 = lax.ppermute(inverse, "walk", partner)
    payload, aux = pl.pallas_call(
        payload_kernel,
        out_shape=(
            jax.ShapeDtypeStruct((blocks, 6, half), jnp.float32),
            jax.ShapeDtypeStruct((8, LANES), jnp.bfloat16),
        ),
        in_specs=[vmem] * 5 + [smem],
        out_specs=(vmem, vmem),
    )(occ_list, virt_list, exc_rank[None], coefficient[None], new_rows, moved_electron)
    aux2 = lax.ppermute(aux, "walk", partner)
    gathered = lax.all_to_all(payload, DET_AXES, 0, 0)

    table, back = pl.pallas_call(
        table_kernel,
        out_shape=(
            jax.ShapeDtypeStruct((1024, 2 * LANES), jnp.float8_e4m3fn),
            jax.ShapeDtypeStruct((8, LANES), jnp.float32),
        ),
        in_specs=[vmem] * 5,
        out_specs=(vmem, vmem),
        scratch_shapes=[pltpu.VMEM((1024, LANES), jnp.float32)],
        compiler_params=params,
    )(inverse, inverse2, aux, aux2, virt_ref)
    entries, part = pl.pallas_call(
        select_kernel,
        out_shape=(
            jax.ShapeDtypeStruct((ndet // LANES, 4, 2, 16, LANES), jnp.bfloat16),
            jax.ShapeDtypeStruct((8, LANES), jnp.float32),
        ),
        in_specs=[vmem] * 3,
        out_specs=(vmem, vmem),
        compiler_params=params,
    )(table, back, gathered)
    part2 = lax.ppermute(part, "walk", partner)

    ci_size = half // walk_count
    orb_size = nocc * nvirt // everyone
    packed = orb_size == 4 * LANES and ci_size == 2 * LANES and nvirt == LANES
    orb_shape = (everyone, 8, LANES) if packed else (nocc, nvirt)
    amp, ci_part, orb_part = pl.pallas_call(
        lambda *refs: gradient_kernel(float(walkers_total), *refs),
        out_shape=(
            jax.ShapeDtypeStruct((8, LANES), jnp.float32),
            jax.ShapeDtypeStruct((blocks, half // LANES, LANES), jnp.float32),
            jax.ShapeDtypeStruct(orb_shape, jnp.float32),
        ),
        in_specs=[vmem] * 4,
        out_specs=(vmem, vmem, vmem),
        scratch_shapes=[pltpu.VMEM((256, LANES), jnp.float32)],
        compiler_params=params,
    )(part, part2, entries, gathered)

    if packed:
        pieces = lax.all_to_all(orb_part, ALL_AXES, 0, 0)
        orb_rows, ci_mine = pl.pallas_call(
            sums_kernel,
            out_shape=(
                jax.ShapeDtypeStruct((blocks * 4, LANES), jnp.float32),
                jax.ShapeDtypeStruct((4, LANES), jnp.float32),
            ),
            in_specs=[vmem],
            out_specs=(vmem, vmem),
        )(pieces)
        ci_mine = ci_mine.reshape(2, ci_size)
        orb_all = lax.all_to_all(orb_rows, DET_AXES, 0, 0, tiled=True)
    else:
        ci_pieces = ci_part.reshape(blocks, walk_count, ci_size).transpose(1, 0, 2)
        orb_pieces = orb_part.reshape(walk_count, blocks, orb_size)
        pieces = jnp.concatenate([orb_pieces, ci_pieces], axis=2).reshape(everyone, -1)
        pieces = lax.all_to_all(pieces, ALL_AXES, 0, 0)
        pieces = pieces.reshape(walk_count // 2, 2, blocks, -1)
        orb_mine = jnp.sum(pieces[..., :orb_size], axis=(0, 1, 2))
        ci_mine = jnp.sum(pieces[..., orb_size:], axis=(0, 2))
        orb_all = lax.all_to_all(
            jnp.broadcast_to(orb_mine[None], (blocks, orb_size)), DET_AXES, 0, 0
        )
    ci_grad = lax.all_gather(ci_mine, "walk", axis=1).reshape(local)
    return (amp[:4, 0], ci_grad, orb_all.reshape(nocc // walk_count, nvirt))


def solution(mesh):
    return jax.shard_map(
        per_device,
        mesh=mesh,
        in_specs=(
            P(ALL_AXES, None, None),
            P(),
            P(ALL_AXES, None),
            P(ALL_AXES),
            P(DET_AXES),
            P(None, DET_AXES),
            P(None, DET_AXES),
            P(DET_AXES),
        ),
        out_specs=(P(ALL_AXES), P(DET_AXES), P("walk", None)),
        check_vma=False,
    )
```

```python
import jax
import jax.numpy as jnp
from jax import lax
from jax.experimental import pallas as pl
from jax.experimental.pallas import tpu as pltpu
from jax.sharding import PartitionSpec as P

TILE = 256
LANES = 128
DET_AXES = ("det", "exc")
ALL_AXES = ("walk", "det", "exc")
FINE = 64.0


def pair_products(x, y):
    return (
        x[0] * y[1] - y[0] * x[1],
        x[0] * y[2] - y[0] * x[2],
        x[0] * y[3] - y[0] * x[3],
        x[1] * y[2] - y[1] * x[2],
        x[1] * y[3] - y[1] * x[3],
        x[2] * y[3] - y[2] * x[3],
    )


def cofactor_rows(x, y, q):
    qa, qb, qc, qd, qe, qf = q
    dx = (
        y[1] * qa + y[2] * qb + y[3] * qc,
        y[2] * qd + y[3] * qe - y[0] * qa,
        y[3] * qf - y[0] * qb - y[1] * qd,
        -(y[0] * qc + y[1] * qe + y[2] * qf),
    )
    dy = (
        -(x[1] * qa + x[2] * qb + x[3] * qc),
        x[0] * qa - x[2] * qd - x[3] * qe,
        x[0] * qb + x[1] * qd - x[3] * qf,
        x[0] * qc + x[1] * qe + x[2] * qf,
    )
    return dx, dy


def masked_cells(entries, rank):
    cells = []
    for a in range(4):
        row = []
        for b in range(4):
            fill = jnp.float32(1.0 if a == b else 0.0)
            row.append(jnp.where(rank > max(a, b), entries[b][a], fill))
        cells.append(row)
    return cells


def determinant(top, low):
    return (
        top[0] * low[5]
        - top[1] * low[4]
        + top[2] * low[3]
        + top[3] * low[2]
        - top[4] * low[1]
        + top[5] * low[0]
    )


def rows8(row):
    return jnp.broadcast_to(row, (8, row.shape[1]))


def rows16(row):
    return jnp.broadcast_to(row, (16, row.shape[1])).astype(jnp.int16)


def iota16():
    return lax.broadcasted_iota(jnp.int32, (16, TILE), 0).astype(jnp.int16)


def one_hot(v16, values):
    base = iota16()
    zero = jnp.zeros((16, TILE), jnp.bfloat16)
    hits = [v16 == base + jnp.int16(16 * k) for k in range(8)]
    parts = [
        jnp.where(hit, jnp.full((16, TILE), value, jnp.bfloat16), zero)
        for value in values
        for hit in hits
    ]
    return jnp.concatenate(parts, axis=0)


def load_lists(pay_ref, t):
    per_block = pay_ref.shape[2] // TILE
    lanes = pl.ds(pl.multiple_of((t % per_block) * TILE, TILE), TILE)
    rows = pay_ref[t // per_block, :, lanes]
    codes = rows[0:4].astype(jnp.int32)
    return jnp.right_shift(codes, 7), jnp.bitwise_and(codes, 127), rows[4:5], rows[5:6]


def power_scale(top):
    scale = jnp.ones_like(top)
    back = jnp.ones_like(top)
    for k in (64, 32, 16, 8, 4, 2, 1):
        big = top >= 2.0 ** (5 + k)
        small = top < 2.0 ** (6 - k)
        up = jnp.float32(2.0**k)
        down = jnp.float32(2.0**-k)
        step = jnp.where(big, down, jnp.where(small, up, 1.0))
        undo = jnp.where(big, up, jnp.where(small, down, 1.0))
        top = top * step
        scale = scale * step
        back = back * undo
    return scale, back


def payload_kernel(occ_ref, virt_ref, rank_ref, coef_ref, rows_ref, moved_ref, pay_ref, aux_ref):
    blocks, _, half = pay_ref.shape
    start = pl.multiple_of((lax.axis_index("walk") & 1) * half, LANES)
    lanes = pl.ds(start, half)
    codes = (occ_ref[:, lanes] * 128 + virt_ref[:, lanes]).astype(jnp.float32)
    rank = rank_ref[:, lanes].astype(jnp.float32)
    coef = coef_ref[:, lanes]
    rows = jnp.concatenate([codes, rank, coef], axis=0)
    for k in range(blocks):
        pay_ref[k] = rows
    sub = lax.broadcasted_iota(jnp.int32, (4, LANES), 0)
    moved = jnp.zeros((4, LANES), jnp.float32)
    for w in range(4):
        moved = jnp.where(sub == w, moved_ref[w].astype(jnp.float32), moved)
    aux_ref[...] = jnp.concatenate(
        [rows_ref[...].astype(jnp.float32), moved], axis=0
    ).astype(jnp.bfloat16)


def table_kernel(inv_ref, inv2_ref, aux_ref, aux2_ref, virt_ref, tab, back_ref, wide):
    sub = lax.broadcasted_iota(jnp.int32, (8, LANES), 0)
    rows_of = lax.broadcasted_iota(jnp.int32, (128, LANES), 0).astype(jnp.float32)
    tops = jnp.zeros((8, LANES), jnp.float32)
    for w in range(8):
        inv, aux = (inv_ref, aux_ref) if w < 4 else (inv2_ref, aux2_ref)
        aux_rows = aux[...].astype(jnp.float32)
        fresh = jnp.broadcast_to(aux_rows[w % 4 : w % 4 + 1], (128, LANES))
        moved = jnp.broadcast_to(aux_rows[w % 4 + 4 : w % 4 + 5], (128, LANES))
        basis = jnp.where(rows_of == moved, fresh, virt_ref[...].astype(jnp.float32))
        table = jnp.dot(
            inv[w % 4], basis.astype(jnp.bfloat16), preferred_element_type=jnp.float32
        )
        table = table.astype(jnp.bfloat16).astype(jnp.float32)
        wide[128 * w : 128 * w + 128, :] = table
        tops = jnp.where(sub == w, jnp.max(jnp.abs(table)), tops)
    scale, back = power_scale(tops)
    back_ref[...] = back
    for w in range(8):
        rows = slice(128 * w, 128 * w + 128)
        block = wide[rows, :] * jnp.broadcast_to(scale[w : w + 1], (128, LANES))
        coarse = block.astype(jnp.float8_e4m3fn)
        rest = (block - coarse.astype(jnp.float32)) * FINE
        tab[rows, 0:128] = coarse
        tab[rows, 128:256] = rest.astype(jnp.float8_e4m3fn)


def cell_rows(ent_ref, lane_tile):
    return [
        [ent_ref[lane_tile, b, pl.ds(a, 8, stride=4), :] for a in range(4)] for b in range(4)
    ]


def select_kernel(tab, back_ref, pay_ref, ent_ref, amp_ref):
    nblk, _, width = pay_ref.shape
    tiles = nblk * width // TILE
    parts = TILE // LANES
    upper = lax.broadcasted_iota(jnp.int32, (8, LANES), 0) < 4
    back = [
        jnp.where(upper, rows8(back_ref[2 * q : 2 * q + 1]), rows8(back_ref[2 * q + 1 : 2 * q + 2]))
        for q in range(4)
    ]

    def forward(t, total):
        occ, virt, rank, coef = load_lists(pay_ref, t)
        occ8 = jnp.concatenate([occ, occ], axis=0)
        split = [occ8[:, h * LANES : (h + 1) * LANES] for h in range(parts)]
        fine = [o & 7 for o in split]
        bits = [[(o & bit) != 0 for bit in (8, 16, 32, 64)] for o in split]
        for b in range(4):
            hot = one_hot(rows16(virt[b : b + 1]), (1.0, 1.0 / FINE)).astype(jnp.float8_e4m3fn)
            cols = jnp.dot(tab[...], hot, preferred_element_type=jnp.float32)
            for h in range(parts):
                lanes = slice(h * LANES, (h + 1) * LANES)
                for q in range(4):
                    pair = []
                    for w in (2 * q, 2 * q + 1):
                        level = [
                            jnp.take_along_axis(
                                cols[128 * w + 8 * k : 128 * w + 8 * k + 8, lanes],
                                fine[h],
                                axis=0,
                                mode="promise_in_bounds",
                            )
                            for k in range(16)
                        ]
                        for step in range(4):
                            level = [
                                jnp.where(bits[h][step], level[2 * k + 1], level[2 * k])
                                for k in range(len(level) // 2)
                            ]
                        pair.append(level[0])
                    ent_ref[t * parts + h, b, 8 * q : 8 * q + 8, :] = (
                        jnp.where(upper, pair[0], pair[1]) * back[q]
                    )
        for h in range(parts):
            lanes = slice(h * LANES, (h + 1) * LANES)
            cells = masked_cells(cell_rows(ent_ref, t * parts + h), rows8(rank[:, lanes]))
            ratio = determinant(
                pair_products(cells[0], cells[1]), pair_products(cells[2], cells[3])
            )
            total = total + ratio * rows8(coef[:, lanes])
        return total

    total = lax.fori_loop(0, tiles, forward, jnp.zeros((8, LANES), jnp.float32), unroll=2)
    amp_ref[...] = jnp.broadcast_to(jnp.sum(total, axis=1, keepdims=True), (8, LANES))


def all_rows_sum(x):
    x = x + pltpu.roll(x, 4, 0)
    x = x + pltpu.roll(x, 2, 0)
    return x + pltpu.roll(x, 1, 0)


def fold(items, dist):
    sub = lax.broadcasted_iota(jnp.int32, (8, LANES), 0)
    first = (sub & dist) == 0
    n = len(items) // 2
    out = []
    for x, y in zip(items[:n], items[n:]):
        x = x + pltpu.roll(x, 8 - dist, 0)
        y = y + pltpu.roll(y, dist, 0)
        out.append(jnp.where(first, x, y))
    return out


def walker_sums(items):
    for dist in (4, 2, 1):
        items = fold(items, dist)
    return items[0]


def two_rows(x, y):
    top = lax.broadcasted_iota(jnp.int32, (8, LANES), 0) < 4
    return jnp.where(top, rows8(x), rows8(y))


def gradient_kernel(
    walkers_total, part_ref, part2_ref, ent_ref, pay_ref, amp_ref, ci_ref, orb_ref, acc
):
    nblk, _, width = pay_ref.shape
    per_block = width // TILE
    tiles = nblk * per_block
    packed = len(orb_ref.shape) == 3
    ci_rows = width // LANES * nblk // orb_ref.shape[0]
    zero = jnp.zeros((16, TILE), jnp.bfloat16)
    amplitude = 1.0 + part_ref[...] + pltpu.roll(part2_ref[...], 4, 0)
    amp_ref[...] = amplitude
    weight = amplitude / (amplitude * amplitude + 1.0) / walkers_total
    sub = lax.broadcasted_iota(jnp.int32, (8, LANES), 0)
    slot_b = sub & 3
    limits = [
        jnp.maximum(slot_b, jnp.right_shift(sub, 2) + 2 * g).astype(jnp.float32) for g in range(2)
    ]

    def backward(t, carry):
        occ, virt, rank_row, coef_row = load_lists(pay_ref, t)
        occ16 = [rows16(occ[a : a + 1]) for a in range(4)]
        wide = [[[] for _ in range(16)] for _ in range(2)]
        for h in range(TILE // LANES):
            lanes = slice(h * LANES, (h + 1) * LANES)
            rank = rows8(rank_row[:, lanes])
            coef = rows8(coef_row[:, lanes])
            entries = cell_rows(ent_ref, t * (TILE // LANES) + h)
            cells = masked_cells(entries, rank)
            low = [x * weight for x in pair_products(cells[2], cells[3])]
            top = pair_products(cells[0], cells[1])
            summed = all_rows_sum(determinant(top, low))
            block = t // per_block
            lane_tile = (t % per_block) * (TILE // LANES) + h
            if packed:
                dest = lane_tile // (ci_rows) * nblk + block
                orb_ref[dest, pl.ds(4 + lane_tile % ci_rows, 1), :] = summed[0:1]
            else:
                ci_ref[block, pl.ds(lane_tile, 1), :] = summed[0:1]
            top = [x * weight for x in top]
            d0, d1 = cofactor_rows(
                cells[0], cells[1], (low[5], -low[4], low[3], low[2], -low[1], low[0])
            )
            d2, d3 = cofactor_rows(
                cells[2], cells[3], (top[5], -top[4], top[3], top[2], -top[1], top[0])
            )
            plain = [
                jnp.where(rank > limits[g], walker_sums(list(x + y)) * coef, 0.0)
                for g, (x, y) in enumerate(((d0, d1), (d2, d3)))
            ]
            turned = [pltpu.roll(x, 4, 0) for x in plain]
            occ_a = two_rows(occ[0:1, lanes], occ[1:2, lanes])
            occ_b = two_rows(occ[2:3, lanes], occ[3:4, lanes])
            turn_a = two_rows(occ[1:2, lanes], occ[0:1, lanes])
            turn_b = two_rows(occ[3:4, lanes], occ[2:3, lanes])
            straight = occ_a == occ_b
            merged = [
                plain[0]
                + jnp.where(occ_a == turn_a, turned[0], 0.0)
                + jnp.where(straight, plain[1], 0.0)
                + jnp.where(occ_a == turn_b, turned[1], 0.0),
                plain[1]
                + jnp.where(occ_b == turn_b, turned[1], 0.0)
                + jnp.where(straight, plain[0], 0.0)
                + jnp.where(occ_b == turn_a, turned[0], 0.0),
            ]
            for g in range(2):
                high = merged[g].astype(jnp.bfloat16).astype(jnp.float32)
                rest = merged[g] - high
                for part, value in enumerate((high, rest)):
                    for r in range(8):
                        one = rows8(value[r : r + 1])
                        wide[part][8 * g + r].append(
                            jnp.concatenate([one, one], axis=0).astype(jnp.bfloat16)
                        )
        wide = [[jnp.concatenate(x, axis=1) for x in rows] for rows in wide]
        left = [[None] * 16 for _ in range(4)]
        for k in range(8):
            hits = [occ16[a] == iota16() + jnp.int16(16 * k) for a in range(4)]
            for part in range(2):
                for b in range(4):
                    value = zero
                    for a in range(4):
                        value = jnp.where(hits[a], wide[part][4 * a + b], value)
                    left[b][part * 8 + k] = value
        left = jnp.concatenate([jnp.concatenate(left[b], axis=0) for b in range(4)], axis=1)
        right = jnp.concatenate(
            [one_hot(rows16(virt[b : b + 1]), (1.0,)) for b in range(4)], axis=1
        )
        acc[...] += lax.dot_general(
            left, right, (((1,), (1,)), ((), ())), preferred_element_type=jnp.float32
        )
        return carry

    acc[...] = jnp.zeros_like(acc)
    if packed:
        orb_ref[...] = jnp.zeros_like(orb_ref)
    lax.fori_loop(0, tiles, backward, 0, unroll=4)
    total = acc[0:128, :] + acc[128:256, :]
    if packed:
        for dest in range(orb_ref.shape[0]):
            orb_ref[dest, 0:4, :] = total[4 * dest : 4 * dest + 4]
    else:
        orb_ref[...] = total


def sums_kernel(pieces_ref, orb_ref, ci_ref):
    everyone = pieces_ref.shape[0]
    blocks = orb_ref.shape[0] // 4
    totals = []
    for parity in range(2):
        picked = [
            pieces_ref[s] for s in range(everyone) if (s // blocks) % 2 == parity
        ]
        while len(picked) > 1:
            picked = [x + y for x, y in zip(picked[::2], picked[1::2])]
        totals.append(picked[0])
    both = totals[0] + totals[1]
    pair = jnp.concatenate([both[0:4], both[0:4]], axis=0)
    for k in range(blocks // 2):
        orb_ref[8 * k : 8 * k + 8, :] = pair
    ci_ref[...] = jnp.concatenate([totals[0][4:6], totals[1][4:6]], axis=0)


def per_device(
    inverse, virt_ref, new_rows, moved_electron, coefficient, occ_list, virt_list, exc_rank
):
    nocc = inverse.shape[1]
    nvirt = virt_ref.shape[1]
    walk_count = lax.axis_size("walk")
    blocks = lax.axis_size(DET_AXES)
    everyone = walk_count * blocks
    local = coefficient.shape[0]
    half = local // 2
    ndet = half * blocks
    walkers_total = inverse.shape[0] * everyone
    partner = [(u, u ^ 1) for u in range(walk_count)]
    vmem = pl.BlockSpec(memory_space=pltpu.VMEM)
    smem = pl.BlockSpec(memory_space=pltpu.SMEM)
    params = pltpu.CompilerParams(vmem_limit_bytes=32 << 20)

    inverse2 = lax.ppermute(inverse, "walk", partner)
    payload, aux = pl.pallas_call(
        payload_kernel,
        out_shape=(
            jax.ShapeDtypeStruct((blocks, 6, half), jnp.float32),
            jax.ShapeDtypeStruct((8, LANES), jnp.bfloat16),
        ),
        in_specs=[vmem] * 5 + [smem],
        out_specs=(vmem, vmem),
    )(occ_list, virt_list, exc_rank[None], coefficient[None], new_rows, moved_electron)
    aux2 = lax.ppermute(aux, "walk", partner)
    gathered = lax.all_to_all(payload, DET_AXES, 0, 0)

    table, back = pl.pallas_call(
        table_kernel,
        out_shape=(
            jax.ShapeDtypeStruct((1024, 2 * LANES), jnp.float8_e4m3fn),
            jax.ShapeDtypeStruct((8, LANES), jnp.float32),
        ),
        in_specs=[vmem] * 5,
        out_specs=(vmem, vmem),
        scratch_shapes=[pltpu.VMEM((1024, LANES), jnp.float32)],
        compiler_params=params,
    )(inverse, inverse2, aux, aux2, virt_ref)
    entries, part = pl.pallas_call(
        select_kernel,
        out_shape=(
            jax.ShapeDtypeStruct((ndet // LANES, 4, 32, LANES), jnp.float32),
            jax.ShapeDtypeStruct((8, LANES), jnp.float32),
        ),
        in_specs=[vmem] * 3,
        out_specs=(vmem, vmem),
        compiler_params=params,
    )(table, back, gathered)
    part2 = lax.ppermute(part, "walk", partner)

    ci_size = half // walk_count
    orb_size = nocc * nvirt // everyone
    packed = orb_size == 4 * LANES and ci_size == 2 * LANES and nvirt == LANES
    orb_shape = (everyone, 8, LANES) if packed else (nocc, nvirt)
    amp, ci_part, orb_part = pl.pallas_call(
        lambda *refs: gradient_kernel(float(walkers_total), *refs),
        out_shape=(
            jax.ShapeDtypeStruct((8, LANES), jnp.float32),
            jax.ShapeDtypeStruct((blocks, half // LANES, LANES), jnp.float32),
            jax.ShapeDtypeStruct(orb_shape, jnp.float32),
        ),
        in_specs=[vmem] * 4,
        out_specs=(vmem, vmem, vmem),
        scratch_shapes=[pltpu.VMEM((256, LANES), jnp.float32)],
        compiler_params=params,
    )(part, part2, entries, gathered)

    if packed:
        pieces = lax.all_to_all(orb_part, ALL_AXES, 0, 0)
        orb_rows, ci_mine = pl.pallas_call(
            sums_kernel,
            out_shape=(
                jax.ShapeDtypeStruct((blocks * 4, LANES), jnp.float32),
                jax.ShapeDtypeStruct((4, LANES), jnp.float32),
            ),
            in_specs=[vmem],
            out_specs=(vmem, vmem),
        )(pieces)
        ci_mine = ci_mine.reshape(2, ci_size)
        orb_all = lax.all_to_all(orb_rows, DET_AXES, 0, 0, tiled=True)
    else:
        ci_pieces = ci_part.reshape(blocks, walk_count, ci_size).transpose(1, 0, 2)
        orb_pieces = orb_part.reshape(walk_count, blocks, orb_size)
        pieces = jnp.concatenate([orb_pieces, ci_pieces], axis=2).reshape(everyone, -1)
        pieces = lax.all_to_all(pieces, ALL_AXES, 0, 0)
        pieces = pieces.reshape(walk_count // 2, 2, blocks, -1)
        orb_mine = jnp.sum(pieces[..., :orb_size], axis=(0, 1, 2))
        ci_mine = jnp.sum(pieces[..., orb_size:], axis=(0, 2))
        orb_all = lax.all_to_all(
            jnp.broadcast_to(orb_mine[None], (blocks, orb_size)), DET_AXES, 0, 0
        )
    ci_grad = lax.all_gather(ci_mine, "walk", axis=1).reshape(local)
    return (amp[:4, 0], ci_grad, orb_all.reshape(nocc // walk_count, nvirt))


def solution(mesh):
    return jax.shard_map(
        per_device,
        mesh=mesh,
        in_specs=(
            P(ALL_AXES, None, None),
            P(),
            P(ALL_AXES, None),
            P(ALL_AXES),
            P(DET_AXES),
            P(None, DET_AXES),
            P(None, DET_AXES),
            P(DET_AXES),
        ),
        out_specs=(P(ALL_AXES), P(DET_AXES), P("walk", None)),
        check_vma=False,
    )
```

```python
import jax
import jax.numpy as jnp
from jax import lax
from jax.experimental import pallas as pl
from jax.experimental.pallas import tpu as pltpu
from jax.sharding import PartitionSpec as P

TILE = 256
LANES = 128
DET_AXES = ("det", "exc")
ALL_AXES = ("walk", "det", "exc")
FINE = 64.0


def pair_products(x, y):
    return (
        x[0] * y[1] - y[0] * x[1],
        x[0] * y[2] - y[0] * x[2],
        x[0] * y[3] - y[0] * x[3],
        x[1] * y[2] - y[1] * x[2],
        x[1] * y[3] - y[1] * x[3],
        x[2] * y[3] - y[2] * x[3],
    )


def cofactor_rows(x, y, q):
    qa, qb, qc, qd, qe, qf = q
    dx = (
        y[1] * qa + y[2] * qb + y[3] * qc,
        y[2] * qd + y[3] * qe - y[0] * qa,
        y[3] * qf - y[0] * qb - y[1] * qd,
        -(y[0] * qc + y[1] * qe + y[2] * qf),
    )
    dy = (
        -(x[1] * qa + x[2] * qb + x[3] * qc),
        x[0] * qa - x[2] * qd - x[3] * qe,
        x[0] * qb + x[1] * qd - x[3] * qf,
        x[0] * qc + x[1] * qe + x[2] * qf,
    )
    return dx, dy


def masked_cells(entries, rank):
    cells = []
    for a in range(4):
        row = []
        for b in range(4):
            fill = jnp.float32(1.0 if a == b else 0.0)
            row.append(jnp.where(rank > max(a, b), entries[b][a], fill))
        cells.append(row)
    return cells


def determinant(top, low):
    return (
        top[0] * low[5]
        - top[1] * low[4]
        + top[2] * low[3]
        + top[3] * low[2]
        - top[4] * low[1]
        + top[5] * low[0]
    )


ROW_GATHER = lax.GatherDimensionNumbers(
    offset_dims=(),
    collapsed_slice_dims=(0,),
    start_index_map=(0,),
    operand_batching_dims=(1,),
    start_indices_batching_dims=(1,),
)


def along_rows(x, index):
    return lax.gather(
        x,
        index[..., None],
        ROW_GATHER,
        (1, 1),
        mode=lax.GatherScatterMode.PROMISE_IN_BOUNDS,
    )


def rows8(row):
    return jnp.broadcast_to(row, (8, row.shape[1]))


def rows16(row):
    return jnp.broadcast_to(row, (16, row.shape[1])).astype(jnp.int16)


def iota16():
    return lax.broadcasted_iota(jnp.int32, (16, TILE), 0).astype(jnp.int16)


def one_hot(v16, values):
    base = iota16()
    zero = jnp.zeros((16, TILE), jnp.bfloat16)
    hits = [v16 == base + jnp.int16(16 * k) for k in range(8)]
    parts = [
        jnp.where(hit, jnp.full((16, TILE), value, jnp.bfloat16), zero)
        for value in values
        for hit in hits
    ]
    return jnp.concatenate(parts, axis=0)


def load_lists(pay_ref, t):
    per_block = pay_ref.shape[2] // TILE
    lanes = pl.ds(pl.multiple_of((t % per_block) * TILE, TILE), TILE)
    rows = pay_ref[t // per_block, :, lanes]
    codes = rows[0:4].astype(jnp.int32)
    return jnp.right_shift(codes, 7), jnp.bitwise_and(codes, 127), rows[4:5], rows[5:6]


def power_scale(top):
    scale = jnp.ones_like(top)
    back = jnp.ones_like(top)
    for k in (64, 32, 16, 8, 4, 2, 1):
        big = top >= 2.0 ** (5 + k)
        small = top < 2.0 ** (6 - k)
        up = jnp.float32(2.0**k)
        down = jnp.float32(2.0**-k)
        step = jnp.where(big, down, jnp.where(small, up, 1.0))
        undo = jnp.where(big, up, jnp.where(small, down, 1.0))
        top = top * step
        scale = scale * step
        back = back * undo
    return scale, back


def payload_kernel(occ_ref, virt_ref, rank_ref, coef_ref, pay_ref):
    blocks, _, half = pay_ref.shape
    start = pl.multiple_of((lax.axis_index("walk") & 1) * half, LANES)
    lanes = pl.ds(start, half)
    codes = (occ_ref[:, lanes] * 128 + virt_ref[:, lanes]).astype(jnp.float32)
    rank = rank_ref[:, lanes].astype(jnp.float32)
    rows = jnp.concatenate([codes, rank, coef_ref[:, lanes]], axis=0)
    for k in range(blocks):
        pay_ref[k] = rows


def aux_kernel(rows_ref, moved_ref, aux_ref):
    sub = lax.broadcasted_iota(jnp.int32, (4, LANES), 0)
    moved = jnp.zeros((4, LANES), jnp.float32)
    for w in range(4):
        moved = jnp.where(sub == w, moved_ref[w].astype(jnp.float32), moved)
    aux_ref[...] = jnp.concatenate(
        [rows_ref[...].astype(jnp.float32), moved], axis=0
    ).astype(jnp.bfloat16)


def table_kernel(inv_ref, inv2_ref, aux_ref, aux2_ref, virt_ref, tab, back_ref, wide):
    sub = lax.broadcasted_iota(jnp.int32, (8, LANES), 0)
    rows_of = lax.broadcasted_iota(jnp.int32, (128, LANES), 0).astype(jnp.float32)
    tops = jnp.zeros((8, LANES), jnp.float32)
    for w in range(8):
        inv, aux = (inv_ref, aux_ref) if w < 4 else (inv2_ref, aux2_ref)
        aux_rows = aux[...].astype(jnp.float32)
        fresh = jnp.broadcast_to(aux_rows[w % 4 : w % 4 + 1], (128, LANES))
        moved = jnp.broadcast_to(aux_rows[w % 4 + 4 : w % 4 + 5], (128, LANES))
        basis = jnp.where(rows_of == moved, fresh, virt_ref[...].astype(jnp.float32))
        table = jnp.dot(
            inv[w % 4], basis.astype(jnp.bfloat16), preferred_element_type=jnp.float32
        )
        table = table.astype(jnp.bfloat16).astype(jnp.float32)
        wide[128 * w : 128 * w + 128, :] = table
        tops = jnp.where(sub == w, jnp.max(jnp.abs(table)), tops)
    scale, back = power_scale(tops)
    back_ref[...] = back
    for w in range(8):
        rows = slice(128 * w, 128 * w + 128)
        block = wide[rows, :] * jnp.broadcast_to(scale[w : w + 1], (128, LANES))
        coarse = block.astype(jnp.float8_e4m3fn)
        rest = (block - coarse.astype(jnp.float32)) * FINE
        tab[rows, 0:128] = coarse
        tab[rows, 128:256] = rest.astype(jnp.float8_e4m3fn)


def cell_rows(ent_ref, lane_tile):
    return [
        [ent_ref[lane_tile, b, pl.ds(a, 8, stride=4), :] for a in range(4)] for b in range(4)
    ]


def select_kernel(tab, back_ref, pay_ref, ent_ref, amp_ref):
    nblk, _, width = pay_ref.shape
    tiles = nblk * width // TILE
    parts = TILE // LANES
    upper = lax.broadcasted_iota(jnp.int32, (8, LANES), 0) < 4
    back = [
        jnp.where(upper, rows8(back_ref[2 * q : 2 * q + 1]), rows8(back_ref[2 * q + 1 : 2 * q + 2]))
        for q in range(4)
    ]

    def forward(t, total):
        occ, virt, rank, coef = load_lists(pay_ref, t)
        occ8 = jnp.concatenate([occ, occ], axis=0)
        split = [occ8[:, h * LANES : (h + 1) * LANES] for h in range(parts)]
        fine = [o & 7 for o in split]
        bits = [[(o & bit) != 0 for bit in (8, 16, 32, 64)] for o in split]
        for b in range(4):
            hot = one_hot(rows16(virt[b : b + 1]), (1.0, 1.0 / FINE)).astype(jnp.float8_e4m3fn)
            cols = jnp.dot(tab[...], hot, preferred_element_type=jnp.float32)
            for h in range(parts):
                lanes = slice(h * LANES, (h + 1) * LANES)
                for q in range(4):
                    pair = []
                    for w in (2 * q, 2 * q + 1):
                        level = [
                            along_rows(
                                cols[128 * w + 8 * k : 128 * w + 8 * k + 8, lanes], fine[h]
                            )
                            for k in range(16)
                        ]
                        for step in range(4):
                            level = [
                                jnp.where(bits[h][step], level[2 * k + 1], level[2 * k])
                                for k in range(len(level) // 2)
                            ]
                        pair.append(level[0])
                    ent_ref[t * parts + h, b, 8 * q : 8 * q + 8, :] = (
                        jnp.where(upper, pair[0], pair[1]) * back[q]
                    )
        for h in range(parts):
            lanes = slice(h * LANES, (h + 1) * LANES)
            cells = masked_cells(cell_rows(ent_ref, t * parts + h), rows8(rank[:, lanes]))
            ratio = determinant(
                pair_products(cells[0], cells[1]), pair_products(cells[2], cells[3])
            )
            total = total + ratio * rows8(coef[:, lanes])
        return total

    total = lax.fori_loop(0, tiles, forward, jnp.zeros((8, LANES), jnp.float32), unroll=4)
    amp_ref[...] = jnp.broadcast_to(jnp.sum(total, axis=1, keepdims=True), (8, LANES))


def all_rows_sum(x):
    x = x + pltpu.roll(x, 4, 0)
    x = x + pltpu.roll(x, 2, 0)
    return x + pltpu.roll(x, 1, 0)


def fold(items, dist):
    sub = lax.broadcasted_iota(jnp.int32, (8, LANES), 0)
    first = (sub & dist) == 0
    n = len(items) // 2
    out = []
    for x, y in zip(items[:n], items[n:]):
        x = x + pltpu.roll(x, 8 - dist, 0)
        y = y + pltpu.roll(y, dist, 0)
        out.append(jnp.where(first, x, y))
    return out


def walker_sums(items):
    for dist in (4, 2, 1):
        items = fold(items, dist)
    return items[0]


def gradient_kernel(
    walkers_total, part_ref, part2_ref, ent_ref, pay_ref, amp_ref, ci_ref, orb_ref, acc
):
    nblk, _, width = pay_ref.shape
    per_block = width // TILE
    tiles = nblk * per_block
    packed = len(orb_ref.shape) == 3
    ci_rows = width // LANES * nblk // orb_ref.shape[0]
    amplitude = 1.0 + part_ref[...] + pltpu.roll(part2_ref[...], 4, 0)
    amp_ref[...] = amplitude
    weight = amplitude / (amplitude * amplitude + 1.0) / walkers_total
    sub = lax.broadcasted_iota(jnp.int32, (8, LANES), 0)
    slot = sub & 3
    upper = sub < 4
    limits = [
        jnp.maximum(slot, jnp.right_shift(sub, 2) + 2 * g).astype(jnp.float32) for g in range(2)
    ]
    others = [(sub & 4) + ((slot + shift) & 3) for shift in (1, 2, 3)]

    def backward(t, carry):
        occ, virt, rank_row, coef_row = load_lists(pay_ref, t)
        left = [[[] for _ in range(16)] for _ in range(4)]
        for h in range(TILE // LANES):
            lanes = slice(h * LANES, (h + 1) * LANES)
            rank = rows8(rank_row[:, lanes])
            coef = rows8(coef_row[:, lanes])
            entries = cell_rows(ent_ref, t * (TILE // LANES) + h)
            cells = masked_cells(entries, rank)
            low = [x * weight for x in pair_products(cells[2], cells[3])]
            top = pair_products(cells[0], cells[1])
            summed = all_rows_sum(determinant(top, low))
            source = t // per_block
            lane_tile = (t % per_block) * (TILE // LANES) + h
            if packed:
                dest = lane_tile // ci_rows * nblk + source
                orb_ref[dest, pl.ds(4 + lane_tile % ci_rows, 1), :] = summed[0:1]
            else:
                ci_ref[source, pl.ds(lane_tile, 1), :] = summed[0:1]
            top = [x * weight for x in top]
            d0, d1 = cofactor_rows(
                cells[0], cells[1], (low[5], -low[4], low[3], low[2], -low[1], low[0])
            )
            d2, d3 = cofactor_rows(
                cells[2], cells[3], (top[5], -top[4], top[3], top[2], -top[1], top[0])
            )
            grads = [d0, d1, d2, d3]
            occ_rows = jnp.concatenate([occ[:, lanes], occ[:, lanes]], axis=0)
            same = [occ_rows == along_rows(occ_rows, other) for other in others]
            sources = []
            for g in range(2):
                items = [grads[a][b] for b in (2 * g, 2 * g + 1) for a in range(4)]
                plain = jnp.where(rank > limits[g], walker_sums(items) * coef, 0.0)
                merged = plain
                for hit, other in zip(same, others):
                    merged = merged + jnp.where(hit, along_rows(plain, other), 0.0)
                high = merged.astype(jnp.bfloat16).astype(jnp.float32)
                both = (high, merged - high)
                sources.append([jnp.where(upper, x, 0.0) for x in both])
                sources.append([jnp.where(upper, pltpu.roll(x, 4, 0), 0.0) for x in both])
            slots = [rows8(occ[a : a + 1, lanes]) for a in range(4)]
            for k in range(8):
                index = []
                for block in (2 * k, 2 * k + 1):
                    place = sub + 8 * block
                    found = jnp.full((8, LANES), 4, jnp.int32)
                    for a in range(4):
                        found = jnp.where(slots[a] == place, a, found)
                    index.append(found)
                for b in range(4):
                    for part in range(2):
                        rows = [along_rows(sources[b][part], x) for x in index]
                        left[b][8 * part + k].append(
                            jnp.concatenate(rows, axis=0).astype(jnp.bfloat16)
                        )
        left = [[jnp.concatenate(x, axis=1) for x in left[b]] for b in range(4)]
        left = jnp.concatenate([jnp.concatenate(left[b], axis=0) for b in range(4)], axis=1)
        right = jnp.concatenate(
            [one_hot(rows16(virt[b : b + 1]), (1.0,)) for b in range(4)], axis=1
        )
        acc[...] += lax.dot_general(
            left, right, (((1,), (1,)), ((), ())), preferred_element_type=jnp.float32
        )
        return carry

    acc[...] = jnp.zeros_like(acc)
    if packed:
        orb_ref[...] = jnp.zeros_like(orb_ref)
    lax.fori_loop(0, tiles, backward, 0, unroll=8)
    total = acc[0:128, :] + acc[128:256, :]
    if packed:
        for dest in range(orb_ref.shape[0]):
            orb_ref[dest, 0:4, :] = total[4 * dest : 4 * dest + 4]
    else:
        orb_ref[...] = total


def sums_kernel(pieces_ref, orb_ref, ci_ref):
    everyone = pieces_ref.shape[0]
    blocks = orb_ref.shape[0] // 4
    totals = []
    for parity in range(2):
        picked = [
            pieces_ref[s] for s in range(everyone) if (s // blocks) % 2 == parity
        ]
        while len(picked) > 1:
            picked = [x + y for x, y in zip(picked[::2], picked[1::2])]
        totals.append(picked[0])
    both = totals[0] + totals[1]
    pair = jnp.concatenate([both[0:4], both[0:4]], axis=0)
    for k in range(blocks // 2):
        orb_ref[8 * k : 8 * k + 8, :] = pair
    ci_ref[...] = jnp.concatenate([totals[0][4:6], totals[1][4:6]], axis=0)


def per_device(
    inverse, virt_ref, new_rows, moved_electron, coefficient, occ_list, virt_list, exc_rank
):
    nocc = inverse.shape[1]
    nvirt = virt_ref.shape[1]
    walk_count = lax.axis_size("walk")
    blocks = lax.axis_size(DET_AXES)
    everyone = walk_count * blocks
    local = coefficient.shape[0]
    half = local // 2
    ndet = half * blocks
    walkers_total = inverse.shape[0] * everyone
    partner = [(u, u ^ 1) for u in range(walk_count)]
    vmem = pl.BlockSpec(memory_space=pltpu.VMEM)
    smem = pl.BlockSpec(memory_space=pltpu.SMEM)
    params = pltpu.CompilerParams(vmem_limit_bytes=32 << 20)

    inverse2 = lax.ppermute(inverse, "walk", partner)
    payload = pl.pallas_call(
        payload_kernel,
        out_shape=jax.ShapeDtypeStruct((blocks, 6, half), jnp.float32),
        in_specs=[vmem] * 4,
        out_specs=vmem,
    )(occ_list, virt_list, exc_rank[None], coefficient[None])
    aux = pl.pallas_call(
        aux_kernel,
        out_shape=jax.ShapeDtypeStruct((8, LANES), jnp.bfloat16),
        in_specs=[vmem, smem],
        out_specs=vmem,
    )(new_rows, moved_electron)
    aux2 = lax.ppermute(aux, "walk", partner)
    gathered = lax.all_to_all(payload, DET_AXES, 0, 0)

    table, back = pl.pallas_call(
        table_kernel,
        out_shape=(
            jax.ShapeDtypeStruct((1024, 2 * LANES), jnp.float8_e4m3fn),
            jax.ShapeDtypeStruct((8, LANES), jnp.float32),
        ),
        in_specs=[vmem] * 5,
        out_specs=(vmem, vmem),
        scratch_shapes=[pltpu.VMEM((1024, LANES), jnp.float32)],
        compiler_params=params,
    )(inverse, inverse2, aux, aux2, virt_ref)
    entries, part = pl.pallas_call(
        select_kernel,
        out_shape=(
            jax.ShapeDtypeStruct((ndet // LANES, 4, 32, LANES), jnp.float32),
            jax.ShapeDtypeStruct((8, LANES), jnp.float32),
        ),
        in_specs=[vmem] * 3,
        out_specs=(vmem, vmem),
        compiler_params=params,
    )(table, back, gathered)
    part2 = lax.ppermute(part, "walk", partner)

    ci_size = half // walk_count
    orb_size = nocc * nvirt // everyone
    packed = orb_size == 4 * LANES and ci_size == 2 * LANES and nvirt == LANES
    orb_shape = (everyone, 8, LANES) if packed else (nocc, nvirt)
    amp, ci_part, orb_part = pl.pallas_call(
        lambda *refs: gradient_kernel(float(walkers_total), *refs),
        out_shape=(
            jax.ShapeDtypeStruct((8, LANES), jnp.float32),
            jax.ShapeDtypeStruct((blocks, half // LANES, LANES), jnp.float32),
            jax.ShapeDtypeStruct(orb_shape, jnp.float32),
        ),
        in_specs=[vmem] * 4,
        out_specs=(vmem, vmem, vmem),
        scratch_shapes=[pltpu.VMEM((256, LANES), jnp.float32)],
        compiler_params=params,
    )(part, part2, entries, gathered)

    if packed:
        pieces = lax.all_to_all(orb_part, ALL_AXES, 0, 0)
        orb_rows, ci_mine = pl.pallas_call(
            sums_kernel,
            out_shape=(
                jax.ShapeDtypeStruct((blocks * 4, LANES), jnp.float32),
                jax.ShapeDtypeStruct((4, LANES), jnp.float32),
            ),
            in_specs=[vmem],
            out_specs=(vmem, vmem),
        )(pieces)
        ci_mine = ci_mine.reshape(2, ci_size)
        orb_all = lax.all_to_all(orb_rows, DET_AXES, 0, 0, tiled=True)
    else:
        ci_pieces = ci_part.reshape(blocks, walk_count, ci_size).transpose(1, 0, 2)
        orb_pieces = orb_part.reshape(walk_count, blocks, orb_size)
        pieces = jnp.concatenate([orb_pieces, ci_pieces], axis=2).reshape(everyone, -1)
        pieces = lax.all_to_all(pieces, ALL_AXES, 0, 0)
        pieces = pieces.reshape(walk_count // 2, 2, blocks, -1)
        orb_mine = jnp.sum(pieces[..., :orb_size], axis=(0, 1, 2))
        ci_mine = jnp.sum(pieces[..., orb_size:], axis=(0, 2))
        orb_all = lax.all_to_all(
            jnp.broadcast_to(orb_mine[None], (blocks, orb_size)), DET_AXES, 0, 0
        )
    ci_grad = lax.all_gather(ci_mine, "walk", axis=1).reshape(local)
    return (amp[:4, 0], ci_grad, orb_all.reshape(nocc // walk_count, nvirt))


def solution(mesh):
    return jax.shard_map(
        per_device,
        mesh=mesh,
        in_specs=(
            P(ALL_AXES, None, None),
            P(),
            P(ALL_AXES, None),
            P(ALL_AXES),
            P(DET_AXES),
            P(None, DET_AXES),
            P(None, DET_AXES),
            P(DET_AXES),
        ),
        out_specs=(P(ALL_AXES), P(DET_AXES), P("walk", None)),
        check_vma=False,
    )
```

```python
import jax
import jax.numpy as jnp
from jax import lax
from jax.experimental import pallas as pl
from jax.experimental.pallas import tpu as pltpu
from jax.sharding import PartitionSpec as P

TILE = 256
LANES = 128
DET_AXES = ("det", "exc")
ALL_AXES = ("walk", "det", "exc")
FINE = 64.0


def pair_products(x, y):
    return (
        x[0] * y[1] - y[0] * x[1],
        x[0] * y[2] - y[0] * x[2],
        x[0] * y[3] - y[0] * x[3],
        x[1] * y[2] - y[1] * x[2],
        x[1] * y[3] - y[1] * x[3],
        x[2] * y[3] - y[2] * x[3],
    )


def cofactor_rows(x, y, q):
    qa, qb, qc, qd, qe, qf = q
    dx = (
        y[1] * qa + y[2] * qb + y[3] * qc,
        y[2] * qd + y[3] * qe - y[0] * qa,
        y[3] * qf - y[0] * qb - y[1] * qd,
        -(y[0] * qc + y[1] * qe + y[2] * qf),
    )
    dy = (
        -(x[1] * qa + x[2] * qb + x[3] * qc),
        x[0] * qa - x[2] * qd - x[3] * qe,
        x[0] * qb + x[1] * qd - x[3] * qf,
        x[0] * qc + x[1] * qe + x[2] * qf,
    )
    return dx, dy


def masked_cells(entries, rank):
    cells = []
    for a in range(4):
        row = []
        for b in range(4):
            fill = jnp.float32(1.0 if a == b else 0.0)
            row.append(jnp.where(rank > max(a, b), entries[b][a], fill))
        cells.append(row)
    return cells


def determinant(top, low):
    return (
        top[0] * low[5]
        - top[1] * low[4]
        + top[2] * low[3]
        + top[3] * low[2]
        - top[4] * low[1]
        + top[5] * low[0]
    )


ROW_GATHER = lax.GatherDimensionNumbers(
    offset_dims=(),
    collapsed_slice_dims=(0,),
    start_index_map=(0,),
    operand_batching_dims=(1,),
    start_indices_batching_dims=(1,),
)


def along_rows(x, index):
    return lax.gather(
        x,
        index[..., None],
        ROW_GATHER,
        (1, 1),
        mode=lax.GatherScatterMode.PROMISE_IN_BOUNDS,
    )


def rows8(row):
    return jnp.broadcast_to(row, (8, row.shape[1]))


def rows16(row):
    return jnp.broadcast_to(row, (16, row.shape[1])).astype(jnp.int16)


def iota16():
    return lax.broadcasted_iota(jnp.int32, (16, TILE), 0).astype(jnp.int16)


def one_hot(v16, values):
    base = iota16()
    zero = jnp.zeros((16, TILE), jnp.bfloat16)
    hits = [v16 == base + jnp.int16(16 * k) for k in range(8)]
    parts = [
        jnp.where(hit, jnp.full((16, TILE), value, jnp.bfloat16), zero)
        for value in values
        for hit in hits
    ]
    return jnp.concatenate(parts, axis=0)


def one_hot8(row, values):
    kind = jnp.float8_e4m3fn
    shape = (32, row.shape[1])
    v8 = jnp.broadcast_to(row, shape).astype(jnp.int8)
    base = lax.broadcasted_iota(jnp.int32, shape, 0)
    hits = [v8 == (base + 32 * k).astype(jnp.int8) for k in range(4)]
    zero = jnp.zeros(shape, kind)
    parts = [jnp.where(hit, jnp.full(shape, x, kind), zero) for x in values for hit in hits]
    return jnp.concatenate(parts, axis=0)


def load_lists(pay_ref, t):
    per_block = pay_ref.shape[2] // TILE
    lanes = pl.ds(pl.multiple_of((t % per_block) * TILE, TILE), TILE)
    rows = pay_ref[t // per_block, :, lanes]
    codes = rows[0:4].astype(jnp.int32)
    return jnp.right_shift(codes, 7), jnp.bitwise_and(codes, 127), rows[4:5], rows[5:6]


def power_scale(top):
    scale = jnp.ones_like(top)
    back = jnp.ones_like(top)
    for k in (64, 32, 16, 8, 4, 2, 1):
        big = top >= 2.0 ** (5 + k)
        small = top < 2.0 ** (6 - k)
        up = jnp.float32(2.0**k)
        down = jnp.float32(2.0**-k)
        step = jnp.where(big, down, jnp.where(small, up, 1.0))
        undo = jnp.where(big, up, jnp.where(small, down, 1.0))
        top = top * step
        scale = scale * step
        back = back * undo
    return scale, back


def payload_kernel(occ_ref, virt_ref, rank_ref, coef_ref, pay_ref):
    blocks, _, half = pay_ref.shape
    start = pl.multiple_of((lax.axis_index("walk") & 1) * half, LANES)
    lanes = pl.ds(start, half)
    codes = (occ_ref[:, lanes] * 128 + virt_ref[:, lanes]).astype(jnp.float32)
    rank = rank_ref[:, lanes].astype(jnp.float32)
    rows = jnp.concatenate([codes, rank, coef_ref[:, lanes]], axis=0)
    for k in range(blocks):
        pay_ref[k] = rows


def table_kernel(moved_ref, inv_ref, rows_ref, virt_ref, tab):
    rows_of = lax.broadcasted_iota(jnp.int32, (128, LANES), 0)
    fresh = rows_ref[...].astype(jnp.float32)
    for w in range(4):
        basis = jnp.where(
            rows_of == moved_ref[w],
            jnp.broadcast_to(fresh[w : w + 1], (128, LANES)),
            virt_ref[...].astype(jnp.float32),
        )
        tab[w] = jnp.dot(
            inv_ref[w], basis.astype(jnp.bfloat16), preferred_element_type=jnp.float32
        ).astype(jnp.bfloat16)


def code_kernel(mine_ref, theirs_ref, code_ref, back_ref):
    sub = lax.broadcasted_iota(jnp.int32, (8, LANES), 0)
    tables = [
        (mine_ref if w < 4 else theirs_ref)[w % 4].astype(jnp.float32) for w in range(8)
    ]
    tops = jnp.zeros((8, LANES), jnp.float32)
    for w in range(8):
        top = jnp.max(jnp.max(jnp.abs(tables[w]), axis=0, keepdims=True), axis=1, keepdims=True)
        tops = jnp.where(sub == w, jnp.broadcast_to(top, (8, LANES)), tops)
    scale, back = power_scale(tops)
    back_ref[...] = back
    for w in range(8):
        rows = slice(128 * w, 128 * w + 128)
        block = tables[w] * jnp.broadcast_to(scale[w : w + 1], (128, LANES))
        coarse = block.astype(jnp.float8_e4m3fn)
        rest = (block - coarse.astype(jnp.float32)) * FINE
        code_ref[rows, 0:128] = coarse
        code_ref[rows, 128:256] = rest.astype(jnp.float8_e4m3fn)


def cell_rows(ent_ref, lane_tile):
    return [
        [ent_ref[lane_tile, b, pl.ds(a, 8, stride=4), :] for a in range(4)] for b in range(4)
    ]


def select_kernel(tab, back_ref, pay_ref, ent_ref, amp_ref):
    nblk, _, width = pay_ref.shape
    tiles = nblk * width // TILE
    parts = TILE // LANES
    upper = lax.broadcasted_iota(jnp.int32, (8, LANES), 0) < 4
    back = [
        jnp.where(upper, rows8(back_ref[2 * q : 2 * q + 1]), rows8(back_ref[2 * q + 1 : 2 * q + 2]))
        for q in range(4)
    ]

    def forward(t, total):
        occ, virt, rank, coef = load_lists(pay_ref, t)
        occ8 = jnp.concatenate([occ, occ], axis=0)
        split = [occ8[:, h * LANES : (h + 1) * LANES] for h in range(parts)]
        fine = [o & 7 for o in split]
        bits = [[(o & bit) != 0 for bit in (8, 16, 32, 64)] for o in split]
        for b in range(4):
            hot = one_hot8(virt[b : b + 1], (1.0, 1.0 / FINE))
            cols = jnp.dot(tab[...], hot, preferred_element_type=jnp.float32)
            for h in range(parts):
                lanes = slice(h * LANES, (h + 1) * LANES)
                for q in range(4):
                    pair = []
                    for w in (2 * q, 2 * q + 1):
                        level = [
                            along_rows(
                                cols[128 * w + 8 * k : 128 * w + 8 * k + 8, lanes], fine[h]
                            )
                            for k in range(16)
                        ]
                        for step in range(4):
                            level = [
                                jnp.where(bits[h][step], level[2 * k + 1], level[2 * k])
                                for k in range(len(level) // 2)
                            ]
                        pair.append(level[0])
                    ent_ref[t * parts + h, b, 8 * q : 8 * q + 8, :] = (
                        jnp.where(upper, pair[0], pair[1]) * back[q]
                    )
        for h in range(parts):
            lanes = slice(h * LANES, (h + 1) * LANES)
            cells = masked_cells(cell_rows(ent_ref, t * parts + h), rows8(rank[:, lanes]))
            ratio = determinant(
                pair_products(cells[0], cells[1]), pair_products(cells[2], cells[3])
            )
            total = total + ratio * rows8(coef[:, lanes])
        return total

    total = lax.fori_loop(0, tiles, forward, jnp.zeros((8, LANES), jnp.float32), unroll=4)
    amp_ref[...] = jnp.broadcast_to(jnp.sum(total, axis=1, keepdims=True), (8, LANES))


def all_rows_sum(x):
    x = x + pltpu.roll(x, 4, 0)
    x = x + pltpu.roll(x, 2, 0)
    return x + pltpu.roll(x, 1, 0)


def fold(items, dist):
    sub = lax.broadcasted_iota(jnp.int32, (8, LANES), 0)
    first = (sub & dist) == 0
    n = len(items) // 2
    out = []
    for x, y in zip(items[:n], items[n:]):
        x = x + pltpu.roll(x, 8 - dist, 0)
        y = y + pltpu.roll(y, dist, 0)
        out.append(jnp.where(first, x, y))
    return out


def walker_sums(items):
    for dist in (4, 2, 1):
        items = fold(items, dist)
    return items[0]


def gradient_kernel(
    walkers_total, part_ref, part2_ref, ent_ref, pay_ref, amp_ref, ci_ref, orb_ref, acc
):
    nblk, _, width = pay_ref.shape
    per_block = width // TILE
    tiles = nblk * per_block
    packed = len(orb_ref.shape) == 3
    ci_rows = width // LANES * nblk // orb_ref.shape[0]
    amplitude = 1.0 + part_ref[...] + pltpu.roll(part2_ref[...], 4, 0)
    amp_ref[...] = amplitude
    weight = amplitude / (amplitude * amplitude + 1.0) / walkers_total
    sub = lax.broadcasted_iota(jnp.int32, (8, LANES), 0)
    slot = sub & 3
    upper = sub < 4
    limits = [
        jnp.maximum(slot, jnp.right_shift(sub, 2) + 2 * g).astype(jnp.float32) for g in range(2)
    ]
    others = [(sub & 4) + ((slot + shift) & 3) for shift in (1, 2, 3)]

    def backward(t, carry):
        occ, virt, rank_row, coef_row = load_lists(pay_ref, t)
        left = [[[] for _ in range(16)] for _ in range(4)]
        for h in range(TILE // LANES):
            lanes = slice(h * LANES, (h + 1) * LANES)
            rank = rows8(rank_row[:, lanes])
            coef = rows8(coef_row[:, lanes])
            entries = cell_rows(ent_ref, t * (TILE // LANES) + h)
            cells = masked_cells(entries, rank)
            low = [x * weight for x in pair_products(cells[2], cells[3])]
            top = pair_products(cells[0], cells[1])
            summed = all_rows_sum(determinant(top, low))
            source = t // per_block
            lane_tile = (t % per_block) * (TILE // LANES) + h
            if packed:
                dest = lane_tile // ci_rows * nblk + source
                orb_ref[dest, pl.ds(4 + lane_tile % ci_rows, 1), :] = summed[0:1]
            else:
                ci_ref[source, pl.ds(lane_tile, 1), :] = summed[0:1]
            top = [x * weight for x in top]
            d0, d1 = cofactor_rows(
                cells[0], cells[1], (low[5], -low[4], low[3], low[2], -low[1], low[0])
            )
            d2, d3 = cofactor_rows(
                cells[2], cells[3], (top[5], -top[4], top[3], top[2], -top[1], top[0])
            )
            grads = [d0, d1, d2, d3]
            occ_rows = jnp.concatenate([occ[:, lanes], occ[:, lanes]], axis=0)
            same = [occ_rows == along_rows(occ_rows, other) for other in others]
            sources = []
            for g in range(2):
                items = [grads[a][b] for b in (2 * g, 2 * g + 1) for a in range(4)]
                plain = jnp.where(rank > limits[g], walker_sums(items) * coef, 0.0)
                merged = plain
                for hit, other in zip(same, others):
                    merged = merged + jnp.where(hit, along_rows(plain, other), 0.0)
                high = merged.astype(jnp.bfloat16).astype(jnp.float32)
                both = (high, merged - high)
                sources.append([jnp.where(upper, x, 0.0) for x in both])
                sources.append([jnp.where(upper, pltpu.roll(x, 4, 0), 0.0) for x in both])
            slots = [rows8(occ[a : a + 1, lanes]) for a in range(4)]
            for k in range(8):
                index = []
                for block in (2 * k, 2 * k + 1):
                    place = sub + 8 * block
                    found = jnp.full((8, LANES), 4, jnp.int32)
                    for a in range(4):
                        found = jnp.where(slots[a] == place, a, found)
                    index.append(found)
                for b in range(4):
                    for part in range(2):
                        rows = [along_rows(sources[b][part], x) for x in index]
                        left[b][8 * part + k].append(
                            jnp.concatenate(rows, axis=0).astype(jnp.bfloat16)
                        )
        left = [[jnp.concatenate(x, axis=1) for x in left[b]] for b in range(4)]
        left = jnp.concatenate([jnp.concatenate(left[b], axis=0) for b in range(4)], axis=1)
        right = jnp.concatenate(
            [one_hot(rows16(virt[b : b + 1]), (1.0,)) for b in range(4)], axis=1
        )
        acc[...] += lax.dot_general(
            left, right, (((1,), (1,)), ((), ())), preferred_element_type=jnp.float32
        )
        return carry

    acc[...] = jnp.zeros_like(acc)
    if packed:
        orb_ref[...] = jnp.zeros_like(orb_ref)
    lax.fori_loop(0, tiles, backward, 0, unroll=8)
    total = acc[0:128, :] + acc[128:256, :]
    if packed:
        for dest in range(orb_ref.shape[0]):
            orb_ref[dest, 0:4, :] = total[4 * dest : 4 * dest + 4]
    else:
        orb_ref[...] = total


def sums_kernel(pieces_ref, orb_ref, ci_ref):
    everyone = pieces_ref.shape[0]
    blocks = orb_ref.shape[0] // 4
    totals = []
    for parity in range(2):
        picked = [
            pieces_ref[s] for s in range(everyone) if (s // blocks) % 2 == parity
        ]
        while len(picked) > 1:
            picked = [x + y for x, y in zip(picked[::2], picked[1::2])]
        totals.append(picked[0])
    both = totals[0] + totals[1]
    pair = jnp.concatenate([both[0:4], both[0:4]], axis=0)
    for k in range(blocks // 2):
        orb_ref[8 * k : 8 * k + 8, :] = pair
    ci_ref[...] = jnp.concatenate([totals[0][4:6], totals[1][4:6]], axis=0)


def per_device(
    inverse, virt_ref, new_rows, moved_electron, coefficient, occ_list, virt_list, exc_rank
):
    nocc = inverse.shape[1]
    nvirt = virt_ref.shape[1]
    walk_count = lax.axis_size("walk")
    blocks = lax.axis_size(DET_AXES)
    everyone = walk_count * blocks
    local = coefficient.shape[0]
    half = local // 2
    ndet = half * blocks
    walkers_total = inverse.shape[0] * everyone
    partner = [(u, u ^ 1) for u in range(walk_count)]
    vmem = pl.BlockSpec(memory_space=pltpu.VMEM)
    smem = pl.BlockSpec(memory_space=pltpu.SMEM)
    params = pltpu.CompilerParams(vmem_limit_bytes=32 << 20)

    payload = pl.pallas_call(
        payload_kernel,
        out_shape=jax.ShapeDtypeStruct((blocks, 6, half), jnp.float32),
        in_specs=[vmem] * 4,
        out_specs=vmem,
    )(occ_list, virt_list, exc_rank[None], coefficient[None])
    gathered = lax.all_to_all(payload, DET_AXES, 0, 0)
    mine = pl.pallas_call(
        table_kernel,
        out_shape=jax.ShapeDtypeStruct(inverse.shape, jnp.bfloat16),
        in_specs=[smem] + [vmem] * 3,
        out_specs=vmem,
    )(moved_electron, inverse, new_rows, virt_ref)
    theirs = lax.ppermute(mine, "walk", partner)
    table, back = pl.pallas_call(
        code_kernel,
        out_shape=(
            jax.ShapeDtypeStruct((1024, 2 * LANES), jnp.float8_e4m3fn),
            jax.ShapeDtypeStruct((8, LANES), jnp.float32),
        ),
        in_specs=[vmem] * 2,
        out_specs=(vmem, vmem),
        compiler_params=params,
    )(mine, theirs)
    entries, part = pl.pallas_call(
        select_kernel,
        out_shape=(
            jax.ShapeDtypeStruct((ndet // LANES, 4, 32, LANES), jnp.float32),
            jax.ShapeDtypeStruct((8, LANES), jnp.float32),
        ),
        in_specs=[vmem] * 3,
        out_specs=(vmem, vmem),
        compiler_params=params,
    )(table, back, gathered)
    part2 = lax.ppermute(part, "walk", partner)

    ci_size = half // walk_count
    orb_size = nocc * nvirt // everyone
    packed = orb_size == 4 * LANES and ci_size == 2 * LANES and nvirt == LANES
    orb_shape = (everyone, 8, LANES) if packed else (nocc, nvirt)
    amp, ci_part, orb_part = pl.pallas_call(
        lambda *refs: gradient_kernel(float(walkers_total), *refs),
        out_shape=(
            jax.ShapeDtypeStruct((8, LANES), jnp.float32),
            jax.ShapeDtypeStruct((blocks, half // LANES, LANES), jnp.float32),
            jax.ShapeDtypeStruct(orb_shape, jnp.float32),
        ),
        in_specs=[vmem] * 4,
        out_specs=(vmem, vmem, vmem),
        scratch_shapes=[pltpu.VMEM((256, LANES), jnp.float32)],
        compiler_params=params,
    )(part, part2, entries, gathered)

    if packed:
        pieces = lax.all_to_all(orb_part, ALL_AXES, 0, 0)
        orb_rows, ci_mine = pl.pallas_call(
            sums_kernel,
            out_shape=(
                jax.ShapeDtypeStruct((blocks * 4, LANES), jnp.float32),
                jax.ShapeDtypeStruct((4, LANES), jnp.float32),
            ),
            in_specs=[vmem],
            out_specs=(vmem, vmem),
        )(pieces)
        ci_mine = ci_mine.reshape(2, ci_size)
        orb_all = lax.all_to_all(orb_rows, DET_AXES, 0, 0, tiled=True)
    else:
        ci_pieces = ci_part.reshape(blocks, walk_count, ci_size).transpose(1, 0, 2)
        orb_pieces = orb_part.reshape(walk_count, blocks, orb_size)
        pieces = jnp.concatenate([orb_pieces, ci_pieces], axis=2).reshape(everyone, -1)
        pieces = lax.all_to_all(pieces, ALL_AXES, 0, 0)
        pieces = pieces.reshape(walk_count // 2, 2, blocks, -1)
        orb_mine = jnp.sum(pieces[..., :orb_size], axis=(0, 1, 2))
        ci_mine = jnp.sum(pieces[..., orb_size:], axis=(0, 2))
        orb_all = lax.all_to_all(
            jnp.broadcast_to(orb_mine[None], (blocks, orb_size)), DET_AXES, 0, 0
        )
    ci_grad = lax.all_gather(ci_mine, "walk", axis=1).reshape(local)
    return (amp[:4, 0], ci_grad, orb_all.reshape(nocc // walk_count, nvirt))


def solution(mesh):
    return jax.shard_map(
        per_device,
        mesh=mesh,
        in_specs=(
            P(ALL_AXES, None, None),
            P(),
            P(ALL_AXES, None),
            P(ALL_AXES),
            P(DET_AXES),
            P(None, DET_AXES),
            P(None, DET_AXES),
            P(DET_AXES),
        ),
        out_specs=(P(ALL_AXES), P(DET_AXES), P("walk", None)),
        check_vma=False,
    )
```

```python
import jax
import jax.numpy as jnp
from jax import lax
from jax.experimental import pallas as pl
from jax.experimental.pallas import tpu as pltpu
from jax.sharding import PartitionSpec as P

TILE = 256
LANES = 128
FIELDS = 6
DET_AXES = ("det", "exc")
ALL_AXES = ("walk", "det", "exc")
FINE = 64.0


def pair_products(x, y):
    return (
        x[0] * y[1] - y[0] * x[1],
        x[0] * y[2] - y[0] * x[2],
        x[0] * y[3] - y[0] * x[3],
        x[1] * y[2] - y[1] * x[2],
        x[1] * y[3] - y[1] * x[3],
        x[2] * y[3] - y[2] * x[3],
    )


def cofactor_rows(x, y, q):
    qa, qb, qc, qd, qe, qf = q
    dx = (
        y[1] * qa + y[2] * qb + y[3] * qc,
        y[2] * qd + y[3] * qe - y[0] * qa,
        y[3] * qf - y[0] * qb - y[1] * qd,
        -(y[0] * qc + y[1] * qe + y[2] * qf),
    )
    dy = (
        -(x[1] * qa + x[2] * qb + x[3] * qc),
        x[0] * qa - x[2] * qd - x[3] * qe,
        x[0] * qb + x[1] * qd - x[3] * qf,
        x[0] * qc + x[1] * qe + x[2] * qf,
    )
    return dx, dy


def masked_cells(entries, rank):
    cells = []
    for a in range(4):
        row = []
        for b in range(4):
            fill = jnp.float32(1.0 if a == b else 0.0)
            row.append(jnp.where(rank > max(a, b), entries[b][a], fill))
        cells.append(row)
    return cells


def determinant(top, low):
    return (
        top[0] * low[5]
        - top[1] * low[4]
        + top[2] * low[3]
        + top[3] * low[2]
        - top[4] * low[1]
        + top[5] * low[0]
    )


ROW_GATHER = lax.GatherDimensionNumbers(
    offset_dims=(),
    collapsed_slice_dims=(0,),
    start_index_map=(0,),
    operand_batching_dims=(1,),
    start_indices_batching_dims=(1,),
)


def along_rows(x, index):
    return lax.gather(
        x,
        index[..., None],
        ROW_GATHER,
        (1, 1),
        mode=lax.GatherScatterMode.PROMISE_IN_BOUNDS,
    )


def rows8(row):
    return jnp.broadcast_to(row, (8, row.shape[1]))


def rows16(row):
    return jnp.broadcast_to(row, (16, row.shape[1])).astype(jnp.int16)


def iota16():
    return lax.broadcasted_iota(jnp.int32, (16, TILE), 0).astype(jnp.int16)


def one_hot(v16, values):
    base = iota16()
    zero = jnp.zeros((16, TILE), jnp.bfloat16)
    hits = [v16 == base + jnp.int16(16 * k) for k in range(8)]
    parts = [
        jnp.where(hit, jnp.full((16, TILE), value, jnp.bfloat16), zero)
        for value in values
        for hit in hits
    ]
    return jnp.concatenate(parts, axis=0)


def one_hot8(row, values):
    kind = jnp.float8_e4m3fn
    shape = (32, row.shape[1])
    v8 = jnp.broadcast_to(row, shape).astype(jnp.int8)
    base = lax.broadcasted_iota(jnp.int32, shape, 0)
    hits = [v8 == (base + 32 * k).astype(jnp.int8) for k in range(4)]
    zero = jnp.zeros(shape, kind)
    parts = [jnp.where(hit, jnp.full(shape, x, kind), zero) for x in values for hit in hits]
    return jnp.concatenate(parts, axis=0)


def unpack_lists(packed_ref, pay_ref):
    for block in range(pay_ref.shape[0]):
        for x in range(pay_ref.shape[2] // LANES):
            lanes = slice(x * LANES, (x + 1) * LANES)
            pay_ref[block, 0:FIELDS, lanes] = packed_ref[block, FIELDS * x : FIELDS * (x + 1), :]


def load_lists(pay_ref, t):
    per_block = pay_ref.shape[2] // TILE
    lanes = pl.ds(pl.multiple_of((t % per_block) * TILE, TILE), TILE)
    rows = pay_ref[t // per_block, :, lanes]
    codes = rows[0:4].astype(jnp.int32)
    return jnp.right_shift(codes, 7), jnp.bitwise_and(codes, 127), rows[4:5], rows[5:6]


def power_scale(top):
    scale = jnp.ones_like(top)
    back = jnp.ones_like(top)
    for k in (64, 32, 16, 8, 4, 2, 1):
        big = top >= 2.0 ** (5 + k)
        small = top < 2.0 ** (6 - k)
        up = jnp.float32(2.0**k)
        down = jnp.float32(2.0**-k)
        step = jnp.where(big, down, jnp.where(small, up, 1.0))
        undo = jnp.where(big, up, jnp.where(small, down, 1.0))
        top = top * step
        scale = scale * step
        back = back * undo
    return scale, back


def payload_kernel(occ_ref, virt_ref, rank_ref, coef_ref, pay_ref):
    blocks, depth, _ = pay_ref.shape
    half = depth // FIELDS * LANES
    start = pl.multiple_of((lax.axis_index("walk") & 1) * half, LANES)
    lanes = pl.ds(start, half)
    codes = (occ_ref[:, lanes] * 128 + virt_ref[:, lanes]).astype(jnp.float32)
    rank = rank_ref[:, lanes].astype(jnp.float32)
    rows = jnp.concatenate([codes, rank, coef_ref[:, lanes]], axis=0)
    rows = jnp.concatenate(
        [rows[:, x : x + LANES] for x in range(0, half, LANES)], axis=0
    )
    for k in range(blocks):
        pay_ref[k] = rows


def table_kernel(moved_ref, inv_ref, rows_ref, virt_ref, tab):
    rows_of = lax.broadcasted_iota(jnp.int32, (128, LANES), 0)
    fresh = rows_ref[...].astype(jnp.float32)
    for w in range(4):
        basis = jnp.where(
            rows_of == moved_ref[w],
            jnp.broadcast_to(fresh[w : w + 1], (128, LANES)),
            virt_ref[...].astype(jnp.float32),
        )
        tab[w] = jnp.dot(
            inv_ref[w], basis.astype(jnp.bfloat16), preferred_element_type=jnp.float32
        ).astype(jnp.bfloat16)


def code_kernel(mine_ref, theirs_ref, code_ref, back_ref):
    sub = lax.broadcasted_iota(jnp.int32, (8, LANES), 0)
    tables = [
        (mine_ref if w < 4 else theirs_ref)[w % 4].astype(jnp.float32) for w in range(8)
    ]
    tops = jnp.zeros((8, LANES), jnp.float32)
    for w in range(8):
        top = jnp.max(jnp.max(jnp.abs(tables[w]), axis=0, keepdims=True), axis=1, keepdims=True)
        tops = jnp.where(sub == w, jnp.broadcast_to(top, (8, LANES)), tops)
    scale, back = power_scale(tops)
    back_ref[...] = back
    for w in range(8):
        rows = slice(128 * w, 128 * w + 128)
        block = tables[w] * jnp.broadcast_to(scale[w : w + 1], (128, LANES))
        coarse = block.astype(jnp.float8_e4m3fn)
        rest = (block - coarse.astype(jnp.float32)) * FINE
        code_ref[rows, 0:128] = coarse
        code_ref[rows, 128:256] = rest.astype(jnp.float8_e4m3fn)


def cell_rows(ent_ref, lane_tile):
    return [
        [ent_ref[lane_tile, b, pl.ds(a, 8, stride=4), :] for a in range(4)] for b in range(4)
    ]


def select_kernel(tab, back_ref, packed_ref, ent_ref, amp_ref, pay_ref):
    unpack_lists(packed_ref, pay_ref)
    nblk, _, width = pay_ref.shape
    tiles = nblk * width // TILE
    parts = TILE // LANES
    upper = lax.broadcasted_iota(jnp.int32, (8, LANES), 0) < 4
    back = [
        jnp.where(upper, rows8(back_ref[2 * q : 2 * q + 1]), rows8(back_ref[2 * q + 1 : 2 * q + 2]))
        for q in range(4)
    ]

    def forward(t, total):
        occ, virt, rank, coef = load_lists(pay_ref, t)
        occ8 = jnp.concatenate([occ, occ], axis=0)
        split = [occ8[:, h * LANES : (h + 1) * LANES] for h in range(parts)]
        fine = [o & 7 for o in split]
        bits = [[(o & bit) != 0 for bit in (8, 16, 32, 64)] for o in split]
        for b in range(4):
            hot = one_hot8(virt[b : b + 1], (1.0, 1.0 / FINE))
            cols = jnp.dot(tab[...], hot, preferred_element_type=jnp.float32)
            for h in range(parts):
                lanes = slice(h * LANES, (h + 1) * LANES)
                for q in range(4):
                    pair = []
                    for w in (2 * q, 2 * q + 1):
                        level = [
                            along_rows(
                                cols[128 * w + 8 * k : 128 * w + 8 * k + 8, lanes], fine[h]
                            )
                            for k in range(16)
                        ]
                        for step in range(4):
                            level = [
                                jnp.where(bits[h][step], level[2 * k + 1], level[2 * k])
                                for k in range(len(level) // 2)
                            ]
                        pair.append(level[0])
                    ent_ref[t * parts + h, b, 8 * q : 8 * q + 8, :] = (
                        jnp.where(upper, pair[0], pair[1]) * back[q]
                    )
        for h in range(parts):
            lanes = slice(h * LANES, (h + 1) * LANES)
            cells = masked_cells(cell_rows(ent_ref, t * parts + h), rows8(rank[:, lanes]))
            ratio = determinant(
                pair_products(cells[0], cells[1]), pair_products(cells[2], cells[3])
            )
            total = total + ratio * rows8(coef[:, lanes])
        return total

    total = lax.fori_loop(0, tiles, forward, jnp.zeros((8, LANES), jnp.float32), unroll=4)
    amp_ref[...] = jnp.broadcast_to(jnp.sum(total, axis=1, keepdims=True), (8, LANES))


def all_rows_sum(x):
    x = x + pltpu.roll(x, 4, 0)
    x = x + pltpu.roll(x, 2, 0)
    return x + pltpu.roll(x, 1, 0)


def fold(items, dist):
    sub = lax.broadcasted_iota(jnp.int32, (8, LANES), 0)
    first = (sub & dist) == 0
    n = len(items) // 2
    out = []
    for x, y in zip(items[:n], items[n:]):
        x = x + pltpu.roll(x, 8 - dist, 0)
        y = y + pltpu.roll(y, dist, 0)
        out.append(jnp.where(first, x, y))
    return out


def walker_sums(items):
    for dist in (4, 2, 1):
        items = fold(items, dist)
    return items[0]


def gradient_kernel(
    walkers_total, part_ref, part2_ref, ent_ref, packed_ref, amp_ref, ci_ref, orb_ref, acc, pay_ref
):
    unpack_lists(packed_ref, pay_ref)
    nblk, _, width = pay_ref.shape
    per_block = width // TILE
    tiles = nblk * per_block
    packed = len(orb_ref.shape) == 3
    ci_rows = width // LANES * nblk // orb_ref.shape[0]
    amplitude = 1.0 + part_ref[...] + pltpu.roll(part2_ref[...], 4, 0)
    amp_ref[...] = amplitude
    weight = amplitude / (amplitude * amplitude + 1.0) / walkers_total
    sub = lax.broadcasted_iota(jnp.int32, (8, LANES), 0)
    slot = sub & 3
    upper = sub < 4
    limits = [
        jnp.maximum(slot, jnp.right_shift(sub, 2) + 2 * g).astype(jnp.float32) for g in range(2)
    ]
    others = [(sub & 4) + ((slot + shift) & 3) for shift in (1, 2, 3)]

    def backward(t, carry):
        occ, virt, rank_row, coef_row = load_lists(pay_ref, t)
        left = [[[] for _ in range(16)] for _ in range(4)]
        for h in range(TILE // LANES):
            lanes = slice(h * LANES, (h + 1) * LANES)
            rank = rows8(rank_row[:, lanes])
            coef = rows8(coef_row[:, lanes])
            entries = cell_rows(ent_ref, t * (TILE // LANES) + h)
            cells = masked_cells(entries, rank)
            low = [x * weight for x in pair_products(cells[2], cells[3])]
            top = pair_products(cells[0], cells[1])
            summed = all_rows_sum(determinant(top, low))
            source = t // per_block
            lane_tile = (t % per_block) * (TILE // LANES) + h
            if packed:
                dest = lane_tile // ci_rows * nblk + source
                orb_ref[dest, pl.ds(4 + lane_tile % ci_rows, 1), :] = summed[0:1]
            else:
                ci_ref[source, pl.ds(lane_tile, 1), :] = summed[0:1]
            top = [x * weight for x in top]
            d0, d1 = cofactor_rows(
                cells[0], cells[1], (low[5], -low[4], low[3], low[2], -low[1], low[0])
            )
            d2, d3 = cofactor_rows(
                cells[2], cells[3], (top[5], -top[4], top[3], top[2], -top[1], top[0])
            )
            grads = [d0, d1, d2, d3]
            occ_rows = jnp.concatenate([occ[:, lanes], occ[:, lanes]], axis=0)
            same = [occ_rows == along_rows(occ_rows, other) for other in others]
            sources = []
            for g in range(2):
                items = [grads[a][b] for b in (2 * g, 2 * g + 1) for a in range(4)]
                plain = jnp.where(rank > limits[g], walker_sums(items) * coef, 0.0)
                merged = plain
                for hit, other in zip(same, others):
                    merged = merged + jnp.where(hit, along_rows(plain, other), 0.0)
                high = merged.astype(jnp.bfloat16).astype(jnp.float32)
                both = (high, merged - high)
                sources.append([jnp.where(upper, x, 0.0) for x in both])
                sources.append([jnp.where(upper, pltpu.roll(x, 4, 0), 0.0) for x in both])
            slots = [rows8(occ[a : a + 1, lanes]) for a in range(4)]
            for k in range(8):
                index = []
                for block in (2 * k, 2 * k + 1):
                    place = sub + 8 * block
                    found = jnp.full((8, LANES), 4, jnp.int32)
                    for a in range(4):
                        found = jnp.where(slots[a] == place, a, found)
                    index.append(found)
                for b in range(4):
                    for part in range(2):
                        rows = [along_rows(sources[b][part], x) for x in index]
                        left[b][8 * part + k].append(
                            jnp.concatenate(rows, axis=0).astype(jnp.bfloat16)
                        )
        left = [[jnp.concatenate(x, axis=1) for x in left[b]] for b in range(4)]
        left = jnp.concatenate([jnp.concatenate(left[b], axis=0) for b in range(4)], axis=1)
        right = jnp.concatenate(
            [one_hot(rows16(virt[b : b + 1]), (1.0,)) for b in range(4)], axis=1
        )
        acc[...] += lax.dot_general(
            left, right, (((1,), (1,)), ((), ())), preferred_element_type=jnp.float32
        )
        return carry

    acc[...] = jnp.zeros_like(acc)
    if packed:
        orb_ref[...] = jnp.zeros_like(orb_ref)
    lax.fori_loop(0, tiles, backward, 0, unroll=8)
    total = acc[0:128, :] + acc[128:256, :]
    if packed:
        for dest in range(orb_ref.shape[0]):
            orb_ref[dest, 0:4, :] = total[4 * dest : 4 * dest + 4]
    else:
        orb_ref[...] = total


def sums_kernel(pieces_ref, orb_ref, ci_ref):
    everyone = pieces_ref.shape[0]
    blocks = orb_ref.shape[0] // 4
    totals = []
    for parity in range(2):
        picked = [
            pieces_ref[s] for s in range(everyone) if (s // blocks) % 2 == parity
        ]
        while len(picked) > 1:
            picked = [x + y for x, y in zip(picked[::2], picked[1::2])]
        totals.append(picked[0])
    both = totals[0] + totals[1]
    pair = jnp.concatenate([both[0:4], both[0:4]], axis=0)
    for k in range(blocks // 2):
        orb_ref[8 * k : 8 * k + 8, :] = pair
    ci_ref[...] = jnp.concatenate([totals[0][4:6], totals[1][4:6]], axis=0)


def per_device(
    inverse, virt_ref, new_rows, moved_electron, coefficient, occ_list, virt_list, exc_rank
):
    nocc = inverse.shape[1]
    nvirt = virt_ref.shape[1]
    walk_count = lax.axis_size("walk")
    blocks = lax.axis_size(DET_AXES)
    everyone = walk_count * blocks
    local = coefficient.shape[0]
    half = local // 2
    ndet = half * blocks
    walkers_total = inverse.shape[0] * everyone
    partner = [(u, u ^ 1) for u in range(walk_count)]
    vmem = pl.BlockSpec(memory_space=pltpu.VMEM)
    smem = pl.BlockSpec(memory_space=pltpu.SMEM)
    lists = pltpu.VMEM((blocks, 8, half), jnp.float32)
    params = pltpu.CompilerParams(vmem_limit_bytes=32 << 20)

    payload = pl.pallas_call(
        payload_kernel,
        out_shape=jax.ShapeDtypeStruct((blocks, FIELDS * half // LANES, LANES), jnp.float32),
        in_specs=[vmem] * 4,
        out_specs=vmem,
    )(occ_list, virt_list, exc_rank[None], coefficient[None])
    gathered = lax.all_to_all(payload, DET_AXES, 0, 0)
    mine = pl.pallas_call(
        table_kernel,
        out_shape=jax.ShapeDtypeStruct(inverse.shape, jnp.bfloat16),
        in_specs=[smem] + [vmem] * 3,
        out_specs=vmem,
    )(moved_electron, inverse, new_rows, virt_ref)
    theirs = lax.ppermute(mine, "walk", partner)
    table, back = pl.pallas_call(
        code_kernel,
        out_shape=(
            jax.ShapeDtypeStruct((1024, 2 * LANES), jnp.float8_e4m3fn),
            jax.ShapeDtypeStruct((8, LANES), jnp.float32),
        ),
        in_specs=[vmem] * 2,
        out_specs=(vmem, vmem),
        compiler_params=params,
    )(mine, theirs)
    entries, part = pl.pallas_call(
        select_kernel,
        out_shape=(
            jax.ShapeDtypeStruct((ndet // LANES, 4, 32, LANES), jnp.float32),
            jax.ShapeDtypeStruct((8, LANES), jnp.float32),
        ),
        in_specs=[vmem] * 3,
        out_specs=(vmem, vmem),
        scratch_shapes=[lists],
        compiler_params=params,
    )(table, back, gathered)
    part2 = lax.ppermute(part, "walk", partner)

    ci_size = half // walk_count
    orb_size = nocc * nvirt // everyone
    packed = orb_size == 4 * LANES and ci_size == 2 * LANES and nvirt == LANES
    orb_shape = (everyone, 8, LANES) if packed else (nocc, nvirt)
    amp, ci_part, orb_part = pl.pallas_call(
        lambda *refs: gradient_kernel(float(walkers_total), *refs),
        out_shape=(
            jax.ShapeDtypeStruct((8, LANES), jnp.float32),
            jax.ShapeDtypeStruct((blocks, half // LANES, LANES), jnp.float32),
            jax.ShapeDtypeStruct(orb_shape, jnp.float32),
        ),
        in_specs=[vmem] * 4,
        out_specs=(vmem, vmem, vmem),
        scratch_shapes=[pltpu.VMEM((256, LANES), jnp.float32), lists],
        compiler_params=params,
    )(part, part2, entries, gathered)

    if packed:
        pieces = lax.all_to_all(orb_part, ALL_AXES, 0, 0)
        orb_rows, ci_mine = pl.pallas_call(
            sums_kernel,
            out_shape=(
                jax.ShapeDtypeStruct((blocks * 4, LANES), jnp.float32),
                jax.ShapeDtypeStruct((4, LANES), jnp.float32),
            ),
            in_specs=[vmem],
            out_specs=(vmem, vmem),
        )(pieces)
        ci_mine = ci_mine.reshape(2, ci_size)
        orb_all = lax.all_to_all(orb_rows, DET_AXES, 0, 0, tiled=True)
    else:
        ci_pieces = ci_part.reshape(blocks, walk_count, ci_size).transpose(1, 0, 2)
        orb_pieces = orb_part.reshape(walk_count, blocks, orb_size)
        pieces = jnp.concatenate([orb_pieces, ci_pieces], axis=2).reshape(everyone, -1)
        pieces = lax.all_to_all(pieces, ALL_AXES, 0, 0)
        pieces = pieces.reshape(walk_count // 2, 2, blocks, -1)
        orb_mine = jnp.sum(pieces[..., :orb_size], axis=(0, 1, 2))
        ci_mine = jnp.sum(pieces[..., orb_size:], axis=(0, 2))
        orb_all = lax.all_to_all(
            jnp.broadcast_to(orb_mine[None], (blocks, orb_size)), DET_AXES, 0, 0
        )
    ci_grad = lax.all_gather(ci_mine, "walk", axis=1).reshape(local)
    return (amp[:4, 0], ci_grad, orb_all.reshape(nocc // walk_count, nvirt))


def solution(mesh):
    return jax.shard_map(
        per_device,
        mesh=mesh,
        in_specs=(
            P(ALL_AXES, None, None),
            P(),
            P(ALL_AXES, None),
            P(ALL_AXES),
            P(DET_AXES),
            P(None, DET_AXES),
            P(None, DET_AXES),
            P(DET_AXES),
        ),
        out_specs=(P(ALL_AXES), P(DET_AXES), P("walk", None)),
        check_vma=False,
    )
```

```python
import jax
import jax.numpy as jnp
from jax import lax
from jax.experimental import pallas as pl
from jax.experimental.pallas import tpu as pltpu
from jax.sharding import PartitionSpec as P

TILE = 256
LANES = 128
FIELDS = 6
DET_AXES = ("det", "exc")
ALL_AXES = ("walk", "det", "exc")
FINE = 64.0


def pair_products(x, y):
    return (
        x[0] * y[1] - y[0] * x[1],
        x[0] * y[2] - y[0] * x[2],
        x[0] * y[3] - y[0] * x[3],
        x[1] * y[2] - y[1] * x[2],
        x[1] * y[3] - y[1] * x[3],
        x[2] * y[3] - y[2] * x[3],
    )


def cofactor_rows(x, y, q):
    qa, qb, qc, qd, qe, qf = q
    dx = (
        y[1] * qa + y[2] * qb + y[3] * qc,
        y[2] * qd + y[3] * qe - y[0] * qa,
        y[3] * qf - y[0] * qb - y[1] * qd,
        -(y[0] * qc + y[1] * qe + y[2] * qf),
    )
    dy = (
        -(x[1] * qa + x[2] * qb + x[3] * qc),
        x[0] * qa - x[2] * qd - x[3] * qe,
        x[0] * qb + x[1] * qd - x[3] * qf,
        x[0] * qc + x[1] * qe + x[2] * qf,
    )
    return dx, dy


def masked_cells(entries, rank):
    cells = []
    for a in range(4):
        row = []
        for b in range(4):
            fill = jnp.float32(1.0 if a == b else 0.0)
            row.append(jnp.where(rank > max(a, b), entries[b][a], fill))
        cells.append(row)
    return cells


def determinant(top, low):
    return (
        top[0] * low[5]
        - top[1] * low[4]
        + top[2] * low[3]
        + top[3] * low[2]
        - top[4] * low[1]
        + top[5] * low[0]
    )


ROW_GATHER = lax.GatherDimensionNumbers(
    offset_dims=(),
    collapsed_slice_dims=(0,),
    start_index_map=(0,),
    operand_batching_dims=(1,),
    start_indices_batching_dims=(1,),
)


def along_rows(x, index):
    return lax.gather(
        x,
        index[..., None],
        ROW_GATHER,
        (1, 1),
        mode=lax.GatherScatterMode.PROMISE_IN_BOUNDS,
    )


def rows8(row):
    return jnp.broadcast_to(row, (8, row.shape[1]))


def rows16(row):
    return jnp.broadcast_to(row, (16, row.shape[1])).astype(jnp.int16)


def iota16():
    return lax.broadcasted_iota(jnp.int32, (16, TILE), 0).astype(jnp.int16)


def one_hot(v16, values):
    base = iota16()
    zero = jnp.zeros((16, TILE), jnp.bfloat16)
    hits = [v16 == base + jnp.int16(16 * k) for k in range(8)]
    parts = [
        jnp.where(hit, jnp.full((16, TILE), value, jnp.bfloat16), zero)
        for value in values
        for hit in hits
    ]
    return jnp.concatenate(parts, axis=0)


def one_hot8(row, values):
    kind = jnp.float8_e4m3fn
    shape = (32, row.shape[1])
    v8 = jnp.broadcast_to(row, shape).astype(jnp.int8)
    base = lax.broadcasted_iota(jnp.int32, shape, 0)
    hits = [v8 == (base + 32 * k).astype(jnp.int8) for k in range(4)]
    zero = jnp.zeros(shape, kind)
    parts = [jnp.where(hit, jnp.full(shape, x, kind), zero) for x in values for hit in hits]
    return jnp.concatenate(parts, axis=0)


def unpack_lists(packed_ref, pay_ref):
    for block in range(pay_ref.shape[0]):
        for x in range(pay_ref.shape[2] // LANES):
            lanes = slice(x * LANES, (x + 1) * LANES)
            pay_ref[block, 0:FIELDS, lanes] = packed_ref[block, FIELDS * x : FIELDS * (x + 1), :]


def load_lists(pay_ref, t):
    per_block = pay_ref.shape[2] // TILE
    lanes = pl.ds(pl.multiple_of((t % per_block) * TILE, TILE), TILE)
    rows = pay_ref[t // per_block, :, lanes]
    codes = rows[0:4].astype(jnp.int32)
    return jnp.right_shift(codes, 7), jnp.bitwise_and(codes, 127), rows[4:5], rows[5:6]


def power_scale(top):
    scale = jnp.ones_like(top)
    back = jnp.ones_like(top)
    for k in (64, 32, 16, 8, 4, 2, 1):
        big = top >= 2.0 ** (5 + k)
        small = top < 2.0 ** (6 - k)
        up = jnp.float32(2.0**k)
        down = jnp.float32(2.0**-k)
        step = jnp.where(big, down, jnp.where(small, up, 1.0))
        undo = jnp.where(big, up, jnp.where(small, down, 1.0))
        top = top * step
        scale = scale * step
        back = back * undo
    return scale, back


def payload_kernel(occ_ref, virt_ref, rank_ref, coef_ref, pay_ref):
    blocks, depth, _ = pay_ref.shape
    half = depth // FIELDS * LANES
    start = pl.multiple_of((lax.axis_index("walk") & 1) * half, LANES)
    lanes = pl.ds(start, half)
    codes = (occ_ref[:, lanes] * 128 + virt_ref[:, lanes]).astype(jnp.float32)
    rank = rank_ref[:, lanes].astype(jnp.float32)
    rows = jnp.concatenate([codes, rank, coef_ref[:, lanes]], axis=0)
    rows = jnp.concatenate(
        [rows[:, x : x + LANES] for x in range(0, half, LANES)], axis=0
    )
    for k in range(blocks):
        pay_ref[k] = rows


def table_kernel(moved_ref, inv_ref, rows_ref, virt_ref, tab):
    rows_of = lax.broadcasted_iota(jnp.int32, (128, LANES), 0)
    fresh = rows_ref[...].astype(jnp.float32)
    for w in range(4):
        basis = jnp.where(
            rows_of == moved_ref[w],
            jnp.broadcast_to(fresh[w : w + 1], (128, LANES)),
            virt_ref[...].astype(jnp.float32),
        )
        tab[w] = jnp.dot(
            inv_ref[w], basis.astype(jnp.bfloat16), preferred_element_type=jnp.float32
        ).astype(jnp.bfloat16)


def code_kernel(mine_ref, theirs_ref, code_ref, back_ref):
    sub = lax.broadcasted_iota(jnp.int32, (8, LANES), 0)
    tables = [
        (mine_ref if w < 4 else theirs_ref)[w % 4].astype(jnp.float32) for w in range(8)
    ]
    tops = jnp.zeros((8, LANES), jnp.float32)
    for w in range(8):
        top = jnp.max(jnp.max(jnp.abs(tables[w]), axis=0, keepdims=True), axis=1, keepdims=True)
        tops = jnp.where(sub == w, jnp.broadcast_to(top, (8, LANES)), tops)
    scale, back = power_scale(tops)
    back_ref[...] = back
    for w in range(8):
        rows = slice(128 * w, 128 * w + 128)
        block = tables[w] * jnp.broadcast_to(scale[w : w + 1], (128, LANES))
        coarse = block.astype(jnp.float8_e4m3fn)
        rest = (block - coarse.astype(jnp.float32)) * FINE
        code_ref[rows, 0:128] = coarse
        code_ref[rows, 128:256] = rest.astype(jnp.float8_e4m3fn)


def cell_rows(ent_ref, lane_tile):
    return [
        [ent_ref[lane_tile, b, pl.ds(a, 8, stride=4), :] for a in range(4)] for b in range(4)
    ]


def select_kernel(tab, back_ref, packed_ref, ent_ref, amp_ref, pay_ref):
    unpack_lists(packed_ref, pay_ref)
    nblk, _, width = pay_ref.shape
    tiles = nblk * width // TILE
    parts = TILE // LANES
    upper = lax.broadcasted_iota(jnp.int32, (8, LANES), 0) < 4
    back = [
        jnp.where(upper, rows8(back_ref[2 * q : 2 * q + 1]), rows8(back_ref[2 * q + 1 : 2 * q + 2]))
        for q in range(4)
    ]

    def forward(t, total):
        occ, virt, rank, coef = load_lists(pay_ref, t)
        occ8 = jnp.concatenate([occ, occ], axis=0)
        split = [occ8[:, h * LANES : (h + 1) * LANES] for h in range(parts)]
        fine = [o & 7 for o in split]
        bits = [[(o & bit) != 0 for bit in (8, 16, 32, 64)] for o in split]
        for b in range(4):
            hot = one_hot8(virt[b : b + 1], (1.0, 1.0 / FINE))
            cols = jnp.dot(tab[...], hot, preferred_element_type=jnp.float32)
            for h in range(parts):
                lanes = slice(h * LANES, (h + 1) * LANES)
                for q in range(4):
                    pair = []
                    for w in (2 * q, 2 * q + 1):
                        level = [
                            along_rows(
                                cols[128 * w + 8 * k : 128 * w + 8 * k + 8, lanes], fine[h]
                            )
                            for k in range(16)
                        ]
                        for step in range(4):
                            level = [
                                jnp.where(bits[h][step], level[2 * k + 1], level[2 * k])
                                for k in range(len(level) // 2)
                            ]
                        pair.append(level[0])
                    ent_ref[t * parts + h, b, 8 * q : 8 * q + 8, :] = (
                        jnp.where(upper, pair[0], pair[1]) * back[q]
                    )
        for h in range(parts):
            lanes = slice(h * LANES, (h + 1) * LANES)
            cells = masked_cells(cell_rows(ent_ref, t * parts + h), rows8(rank[:, lanes]))
            ratio = determinant(
                pair_products(cells[0], cells[1]), pair_products(cells[2], cells[3])
            )
            total = total + ratio * rows8(coef[:, lanes])
        return total

    total = lax.fori_loop(0, tiles, forward, jnp.zeros((8, LANES), jnp.float32), unroll=4)
    amp_ref[...] = jnp.broadcast_to(jnp.sum(total, axis=1, keepdims=True), (8, LANES))


def all_rows_sum(x):
    x = x + pltpu.roll(x, 4, 0)
    x = x + pltpu.roll(x, 2, 0)
    return x + pltpu.roll(x, 1, 0)


def fold(items, dist):
    sub = lax.broadcasted_iota(jnp.int32, (8, LANES), 0)
    first = (sub & dist) == 0
    n = len(items) // 2
    out = []
    for x, y in zip(items[:n], items[n:]):
        x = x + pltpu.roll(x, 8 - dist, 0)
        y = y + pltpu.roll(y, dist, 0)
        out.append(jnp.where(first, x, y))
    return out


def walker_sums(items):
    for dist in (4, 2, 1):
        items = fold(items, dist)
    return items[0]


def gradient_kernel(
    walkers_total, part_ref, part2_ref, ent_ref, packed_ref, amp_ref, ci_ref, orb_ref, acc, pay_ref
):
    unpack_lists(packed_ref, pay_ref)
    nblk, _, width = pay_ref.shape
    per_block = width // TILE
    tiles = nblk * per_block
    packed = len(orb_ref.shape) == 3
    ci_rows = width // LANES * nblk // orb_ref.shape[0]
    amplitude = 1.0 + part_ref[...] + pltpu.roll(part2_ref[...], 4, 0)
    amp_ref[...] = amplitude
    weight = amplitude / (amplitude * amplitude + 1.0) / walkers_total
    sub = lax.broadcasted_iota(jnp.int32, (8, LANES), 0)
    slot = sub & 3
    upper = sub < 4
    limits = [
        jnp.maximum(slot, jnp.right_shift(sub, 2) + 2 * g).astype(jnp.float32) for g in range(2)
    ]
    others = [(sub & 4) + ((slot + shift) & 3) for shift in (1, 2, 3)]

    def backward(t, carry):
        occ, virt, rank_row, coef_row = load_lists(pay_ref, t)
        left = [[[] for _ in range(16)] for _ in range(4)]
        for h in range(TILE // LANES):
            lanes = slice(h * LANES, (h + 1) * LANES)
            rank = rows8(rank_row[:, lanes])
            coef = rows8(coef_row[:, lanes])
            entries = cell_rows(ent_ref, t * (TILE // LANES) + h)
            cells = masked_cells(entries, rank)
            low = [x * weight for x in pair_products(cells[2], cells[3])]
            top = pair_products(cells[0], cells[1])
            summed = all_rows_sum(determinant(top, low))
            source = t // per_block
            lane_tile = (t % per_block) * (TILE // LANES) + h
            if packed:
                dest = lane_tile // ci_rows * nblk + source
                orb_ref[dest, pl.ds(4 + lane_tile % ci_rows, 1), :] = summed[0:1]
            else:
                ci_ref[source, pl.ds(lane_tile, 1), :] = summed[0:1]
            top = [x * weight for x in top]
            d0, d1 = cofactor_rows(
                cells[0], cells[1], (low[5], -low[4], low[3], low[2], -low[1], low[0])
            )
            d2, d3 = cofactor_rows(
                cells[2], cells[3], (top[5], -top[4], top[3], top[2], -top[1], top[0])
            )
            grads = [d0, d1, d2, d3]
            occ_rows = jnp.concatenate([occ[:, lanes], occ[:, lanes]], axis=0)
            same = [occ_rows == along_rows(occ_rows, other) for other in others]
            sources = []
            for g in range(2):
                items = [grads[a][b] for b in (2 * g, 2 * g + 1) for a in range(4)]
                plain = jnp.where(rank > limits[g], walker_sums(items) * coef, 0.0)
                merged = plain
                for hit, other in zip(same, others):
                    merged = merged + jnp.where(hit, along_rows(plain, other), 0.0)
                high = merged.astype(jnp.bfloat16).astype(jnp.float32)
                both = (high, merged - high)
                sources.append([jnp.where(upper, x, 0.0) for x in both])
                sources.append([jnp.where(upper, pltpu.roll(x, 4, 0), 0.0) for x in both])
            slots = [rows8(occ[a : a + 1, lanes]) for a in range(4)]
            for k in range(8):
                index = []
                for block in (2 * k, 2 * k + 1):
                    place = sub + 8 * block
                    found = jnp.full((8, LANES), 4, jnp.int32)
                    for a in range(4):
                        found = jnp.where(slots[a] == place, a, found)
                    index.append(found)
                for b in range(4):
                    for part in range(2):
                        rows = [along_rows(sources[b][part], x) for x in index]
                        left[b][8 * part + k].append(
                            jnp.concatenate(rows, axis=0).astype(jnp.bfloat16)
                        )
        left = [[jnp.concatenate(x, axis=1) for x in left[b]] for b in range(4)]
        left = jnp.concatenate([jnp.concatenate(left[b], axis=0) for b in range(4)], axis=1)
        right = jnp.concatenate(
            [one_hot(rows16(virt[b : b + 1]), (1.0,)) for b in range(4)], axis=1
        )
        acc[...] += lax.dot_general(
            left, right, (((1,), (1,)), ((), ())), preferred_element_type=jnp.float32
        )
        return carry

    acc[...] = jnp.zeros_like(acc)
    if packed:
        orb_ref[...] = jnp.zeros_like(orb_ref)
    lax.fori_loop(0, tiles, backward, 0, unroll=8)
    total = acc[0:128, :] + acc[128:256, :]
    if packed:
        for dest in range(orb_ref.shape[0]):
            orb_ref[dest, 0:4, :] = total[4 * dest : 4 * dest + 4]
    else:
        orb_ref[...] = total


def sums_kernel(pieces_ref, orb_ref, ci_ref):
    everyone = pieces_ref.shape[0]
    blocks = orb_ref.shape[0] // 4
    totals = []
    for parity in range(2):
        picked = [
            pieces_ref[s] for s in range(everyone) if (s // blocks) % 2 == parity
        ]
        while len(picked) > 1:
            picked = [x + y for x, y in zip(picked[::2], picked[1::2])]
        totals.append(picked[0])
    both = totals[0] + totals[1]
    pair = jnp.concatenate([both[0:4], both[0:4]], axis=0)
    for k in range(blocks // 2):
        orb_ref[8 * k : 8 * k + 8, :] = pair
    ci_ref[...] = jnp.concatenate([totals[0][4:6], totals[1][4:6]], axis=0)


def per_device(
    inverse, virt_ref, new_rows, moved_electron, coefficient, occ_list, virt_list, exc_rank
):
    nocc = inverse.shape[1]
    nvirt = virt_ref.shape[1]
    walk_count = lax.axis_size("walk")
    blocks = lax.axis_size(DET_AXES)
    everyone = walk_count * blocks
    local = coefficient.shape[0]
    half = local // 2
    ndet = half * blocks
    walkers_total = inverse.shape[0] * everyone
    partner = [(u, u ^ 1) for u in range(walk_count)]
    vmem = pl.BlockSpec(memory_space=pltpu.VMEM)
    smem = pl.BlockSpec(memory_space=pltpu.SMEM)
    lists = pltpu.VMEM((blocks, 8, half), jnp.float32)
    params = pltpu.CompilerParams(vmem_limit_bytes=32 << 20)
    small = pltpu.CompilerParams(vmem_limit_bytes=8 << 20)

    payload = pl.pallas_call(
        payload_kernel,
        out_shape=jax.ShapeDtypeStruct((blocks, FIELDS * half // LANES, LANES), jnp.float32),
        in_specs=[vmem] * 4,
        out_specs=vmem,
    )(occ_list, virt_list, exc_rank[None], coefficient[None])
    gathered = lax.all_to_all(payload, DET_AXES, 0, 0)
    mine = pl.pallas_call(
        table_kernel,
        out_shape=jax.ShapeDtypeStruct(inverse.shape, jnp.bfloat16),
        in_specs=[smem] + [vmem] * 3,
        out_specs=vmem,
    )(moved_electron, inverse, new_rows, virt_ref)
    theirs = lax.ppermute(mine, "walk", partner)
    table, back = pl.pallas_call(
        code_kernel,
        out_shape=(
            jax.ShapeDtypeStruct((1024, 2 * LANES), jnp.float8_e4m3fn),
            jax.ShapeDtypeStruct((8, LANES), jnp.float32),
        ),
        in_specs=[vmem] * 2,
        out_specs=(vmem, vmem),
        compiler_params=params,
    )(mine, theirs)
    entries, part = pl.pallas_call(
        select_kernel,
        out_shape=(
            jax.ShapeDtypeStruct((ndet // LANES, 4, 32, LANES), jnp.float32),
            jax.ShapeDtypeStruct((8, LANES), jnp.float32),
        ),
        in_specs=[vmem] * 3,
        out_specs=(vmem, vmem),
        scratch_shapes=[lists],
        compiler_params=params,
    )(table, back, gathered)
    part2 = lax.ppermute(part, "walk", partner)

    ci_size = half // walk_count
    orb_size = nocc * nvirt // everyone
    packed = orb_size == 4 * LANES and ci_size == 2 * LANES and nvirt == LANES
    orb_shape = (everyone, 8, LANES) if packed else (nocc, nvirt)
    amp, ci_part, orb_part = pl.pallas_call(
        lambda *refs: gradient_kernel(float(walkers_total), *refs),
        out_shape=(
            jax.ShapeDtypeStruct((8, LANES), jnp.float32),
            jax.ShapeDtypeStruct((blocks, half // LANES, LANES), jnp.float32),
            jax.ShapeDtypeStruct(orb_shape, jnp.float32),
        ),
        in_specs=[vmem] * 4,
        out_specs=(vmem, vmem, vmem),
        scratch_shapes=[pltpu.VMEM((256, LANES), jnp.float32), lists],
        compiler_params=params,
    )(part, part2, entries, gathered)

    amplitude = amp[:4, 0]
    if packed:
        pieces = lax.all_to_all(orb_part, ALL_AXES, 0, 0)
        pieces, amplitude = lax.optimization_barrier((pieces, amplitude))
        orb_rows, ci_mine = pl.pallas_call(
            sums_kernel,
            out_shape=(
                jax.ShapeDtypeStruct((blocks * 4, LANES), jnp.float32),
                jax.ShapeDtypeStruct((4, LANES), jnp.float32),
            ),
            in_specs=[vmem],
            out_specs=(vmem, vmem),
            compiler_params=small,
        )(pieces)
        ci_mine = ci_mine.reshape(2, ci_size)
        orb_all = lax.all_to_all(orb_rows, DET_AXES, 0, 0, tiled=True)
    else:
        ci_pieces = ci_part.reshape(blocks, walk_count, ci_size).transpose(1, 0, 2)
        orb_pieces = orb_part.reshape(walk_count, blocks, orb_size)
        pieces = jnp.concatenate([orb_pieces, ci_pieces], axis=2).reshape(everyone, -1)
        pieces = lax.all_to_all(pieces, ALL_AXES, 0, 0)
        pieces = pieces.reshape(walk_count // 2, 2, blocks, -1)
        orb_mine = jnp.sum(pieces[..., :orb_size], axis=(0, 1, 2))
        ci_mine = jnp.sum(pieces[..., orb_size:], axis=(0, 2))
        orb_all = lax.all_to_all(
            jnp.broadcast_to(orb_mine[None], (blocks, orb_size)), DET_AXES, 0, 0
        )
    ci_grad = lax.all_gather(ci_mine, "walk", axis=1).reshape(local)
    return (amplitude, ci_grad, orb_all.reshape(nocc // walk_count, nvirt))


def solution(mesh):
    return jax.shard_map(
        per_device,
        mesh=mesh,
        in_specs=(
            P(ALL_AXES, None, None),
            P(),
            P(ALL_AXES, None),
            P(ALL_AXES),
            P(DET_AXES),
            P(None, DET_AXES),
            P(None, DET_AXES),
            P(DET_AXES),
        ),
        out_specs=(P(ALL_AXES), P(DET_AXES), P("walk", None)),
        check_vma=False,
    )
```

```python
import jax
import jax.numpy as jnp
from jax import lax
from jax.experimental import pallas as pl
from jax.experimental.pallas import tpu as pltpu
from jax.sharding import PartitionSpec as P

TILE = 256
LANES = 128
FIELDS = 6
DET_AXES = ("det", "exc")
ALL_AXES = ("walk", "det", "exc")
FINE = 64.0


def pair_products(x, y):
    return (
        x[0] * y[1] - y[0] * x[1],
        x[0] * y[2] - y[0] * x[2],
        x[0] * y[3] - y[0] * x[3],
        x[1] * y[2] - y[1] * x[2],
        x[1] * y[3] - y[1] * x[3],
        x[2] * y[3] - y[2] * x[3],
    )


def cofactor_rows(x, y, q):
    qa, qb, qc, qd, qe, qf = q
    dx = (
        y[1] * qa + y[2] * qb + y[3] * qc,
        y[2] * qd + y[3] * qe - y[0] * qa,
        y[3] * qf - y[0] * qb - y[1] * qd,
        -(y[0] * qc + y[1] * qe + y[2] * qf),
    )
    dy = (
        -(x[1] * qa + x[2] * qb + x[3] * qc),
        x[0] * qa - x[2] * qd - x[3] * qe,
        x[0] * qb + x[1] * qd - x[3] * qf,
        x[0] * qc + x[1] * qe + x[2] * qf,
    )
    return dx, dy


def masked_cells(entries, rank):
    cells = []
    for a in range(4):
        row = []
        for b in range(4):
            fill = jnp.float32(1.0 if a == b else 0.0)
            row.append(jnp.where(rank > max(a, b), entries[b][a], fill))
        cells.append(row)
    return cells


def determinant(top, low):
    return (
        top[0] * low[5]
        - top[1] * low[4]
        + top[2] * low[3]
        + top[3] * low[2]
        - top[4] * low[1]
        + top[5] * low[0]
    )


ROW_GATHER = lax.GatherDimensionNumbers(
    offset_dims=(),
    collapsed_slice_dims=(0,),
    start_index_map=(0,),
    operand_batching_dims=(1,),
    start_indices_batching_dims=(1,),
)


def along_rows(x, index):
    return lax.gather(
        x,
        index[..., None],
        ROW_GATHER,
        (1, 1),
        mode=lax.GatherScatterMode.PROMISE_IN_BOUNDS,
    )


def rows8(row):
    return jnp.broadcast_to(row, (8, row.shape[1]))


def rows16(row):
    return jnp.broadcast_to(row, (16, row.shape[1])).astype(jnp.int16)


def iota16():
    return lax.broadcasted_iota(jnp.int32, (16, TILE), 0).astype(jnp.int16)


def one_hot(v16, values):
    base = iota16()
    zero = jnp.zeros((16, TILE), jnp.bfloat16)
    hits = [v16 == base + jnp.int16(16 * k) for k in range(8)]
    parts = [
        jnp.where(hit, jnp.full((16, TILE), value, jnp.bfloat16), zero)
        for value in values
        for hit in hits
    ]
    return jnp.concatenate(parts, axis=0)


def one_hot8(row, values):
    kind = jnp.float8_e4m3fn
    shape = (32, row.shape[1])
    v8 = jnp.broadcast_to(row, shape).astype(jnp.int8)
    base = lax.broadcasted_iota(jnp.int32, shape, 0)
    hits = [v8 == (base + 32 * k).astype(jnp.int8) for k in range(4)]
    zero = jnp.zeros(shape, kind)
    parts = [jnp.where(hit, jnp.full(shape, x, kind), zero) for x in values for hit in hits]
    return jnp.concatenate(parts, axis=0)


def unpack_lists(packed_ref, pay_ref):
    for block in range(pay_ref.shape[0]):
        for x in range(pay_ref.shape[2] // LANES):
            lanes = slice(x * LANES, (x + 1) * LANES)
            pay_ref[block, 0:FIELDS, lanes] = packed_ref[block, FIELDS * x : FIELDS * (x + 1), :]


def load_lists(pay_ref, t):
    per_block = pay_ref.shape[2] // TILE
    lanes = pl.ds(pl.multiple_of((t % per_block) * TILE, TILE), TILE)
    rows = pay_ref[t // per_block, :, lanes]
    codes = rows[0:4].astype(jnp.int32)
    return jnp.right_shift(codes, 7), jnp.bitwise_and(codes, 127), rows[4:5], rows[5:6]


def power_scale(top):
    scale = jnp.ones_like(top)
    back = jnp.ones_like(top)
    for k in (64, 32, 16, 8, 4, 2, 1):
        big = top >= 2.0 ** (5 + k)
        small = top < 2.0 ** (6 - k)
        up = jnp.float32(2.0**k)
        down = jnp.float32(2.0**-k)
        step = jnp.where(big, down, jnp.where(small, up, 1.0))
        undo = jnp.where(big, up, jnp.where(small, down, 1.0))
        top = top * step
        scale = scale * step
        back = back * undo
    return scale, back


def payload_kernel(occ_ref, virt_ref, rank_ref, coef_ref, pay_ref):
    blocks, depth, _ = pay_ref.shape
    half = depth // FIELDS * LANES
    start = pl.multiple_of((lax.axis_index("walk") & 1) * half, LANES)
    lanes = pl.ds(start, half)
    codes = (occ_ref[:, lanes] * 128 + virt_ref[:, lanes]).astype(jnp.float32)
    rank = rank_ref[:, lanes].astype(jnp.float32)
    rows = jnp.concatenate([codes, rank, coef_ref[:, lanes]], axis=0)
    rows = jnp.concatenate(
        [rows[:, x : x + LANES] for x in range(0, half, LANES)], axis=0
    )
    for k in range(blocks):
        pay_ref[k] = rows


def table_kernel(moved_ref, inv_ref, rows_ref, virt_ref, tab):
    rows_of = lax.broadcasted_iota(jnp.int32, (128, LANES), 0)
    fresh = rows_ref[...].astype(jnp.float32)
    for w in range(4):
        basis = jnp.where(
            rows_of == moved_ref[w],
            jnp.broadcast_to(fresh[w : w + 1], (128, LANES)),
            virt_ref[...].astype(jnp.float32),
        )
        tab[w] = jnp.dot(
            inv_ref[w], basis.astype(jnp.bfloat16), preferred_element_type=jnp.float32
        ).astype(jnp.bfloat16)


def code_kernel(mine_ref, theirs_ref, code_ref, back_ref):
    sub = lax.broadcasted_iota(jnp.int32, (8, LANES), 0)
    tables = [
        (mine_ref if w < 4 else theirs_ref)[w % 4].astype(jnp.float32) for w in range(8)
    ]
    tops = jnp.zeros((8, LANES), jnp.float32)
    for w in range(8):
        top = jnp.max(jnp.max(jnp.abs(tables[w]), axis=0, keepdims=True), axis=1, keepdims=True)
        tops = jnp.where(sub == w, jnp.broadcast_to(top, (8, LANES)), tops)
    scale, back = power_scale(tops)
    back_ref[...] = back
    for w in range(8):
        rows = slice(128 * w, 128 * w + 128)
        block = tables[w] * jnp.broadcast_to(scale[w : w + 1], (128, LANES))
        coarse = block.astype(jnp.float8_e4m3fn)
        rest = (block - coarse.astype(jnp.float32)) * FINE
        code_ref[rows, 0:128] = coarse
        code_ref[rows, 128:256] = rest.astype(jnp.float8_e4m3fn)


def cell_rows(ent_ref, lane_tile):
    return [
        [ent_ref[lane_tile, b, pl.ds(a, 8, stride=4), :] for a in range(4)] for b in range(4)
    ]


def select_kernel(tab, back_ref, packed_ref, ent_ref, amp_ref, pay_ref):
    unpack_lists(packed_ref, pay_ref)
    nblk, _, width = pay_ref.shape
    tiles = nblk * width // TILE
    parts = TILE // LANES
    upper = lax.broadcasted_iota(jnp.int32, (8, LANES), 0) < 4
    back = [
        jnp.where(upper, rows8(back_ref[2 * q : 2 * q + 1]), rows8(back_ref[2 * q + 1 : 2 * q + 2]))
        for q in range(4)
    ]

    def forward(t, total):
        occ, virt, rank, coef = load_lists(pay_ref, t)
        occ8 = jnp.concatenate([occ, occ], axis=0)
        split = [occ8[:, h * LANES : (h + 1) * LANES] for h in range(parts)]
        fine = [o & 7 for o in split]
        bits = [[(o & bit) != 0 for bit in (8, 16, 32, 64)] for o in split]
        for b in range(4):
            hot = one_hot8(virt[b : b + 1], (1.0, 1.0 / FINE))
            cols = jnp.dot(tab[...], hot, preferred_element_type=jnp.float32)
            for h in range(parts):
                lanes = slice(h * LANES, (h + 1) * LANES)
                for q in range(4):
                    pair = []
                    for w in (2 * q, 2 * q + 1):
                        level = [
                            along_rows(
                                cols[128 * w + 8 * k : 128 * w + 8 * k + 8, lanes], fine[h]
                            )
                            for k in range(16)
                        ]
                        for step in range(4):
                            level = [
                                jnp.where(bits[h][step], level[2 * k + 1], level[2 * k])
                                for k in range(len(level) // 2)
                            ]
                        pair.append(level[0])
                    ent_ref[t * parts + h, b, 8 * q : 8 * q + 8, :] = (
                        jnp.where(upper, pair[0], pair[1]) * back[q]
                    )
        for h in range(parts):
            lanes = slice(h * LANES, (h + 1) * LANES)
            cells = masked_cells(cell_rows(ent_ref, t * parts + h), rows8(rank[:, lanes]))
            ratio = determinant(
                pair_products(cells[0], cells[1]), pair_products(cells[2], cells[3])
            )
            total = total + ratio * rows8(coef[:, lanes])
        return total

    total = lax.fori_loop(0, tiles, forward, jnp.zeros((8, LANES), jnp.float32), unroll=8)
    amp_ref[...] = jnp.broadcast_to(jnp.sum(total, axis=1, keepdims=True), (8, LANES))


def all_rows_sum(x):
    x = x + pltpu.roll(x, 4, 0)
    x = x + pltpu.roll(x, 2, 0)
    return x + pltpu.roll(x, 1, 0)


def fold(items, dist):
    sub = lax.broadcasted_iota(jnp.int32, (8, LANES), 0)
    first = (sub & dist) == 0
    n = len(items) // 2
    out = []
    for x, y in zip(items[:n], items[n:]):
        x = x + pltpu.roll(x, 8 - dist, 0)
        y = y + pltpu.roll(y, dist, 0)
        out.append(jnp.where(first, x, y))
    return out


def walker_sums(items):
    for dist in (4, 2, 1):
        items = fold(items, dist)
    return items[0]


def gradient_kernel(
    walkers_total, part_ref, part2_ref, ent_ref, packed_ref, amp_ref, ci_ref, orb_ref, acc, pay_ref
):
    unpack_lists(packed_ref, pay_ref)
    nblk, _, width = pay_ref.shape
    per_block = width // TILE
    tiles = nblk * per_block
    packed = len(orb_ref.shape) == 3
    ci_rows = width // LANES * nblk // orb_ref.shape[0]
    amplitude = 1.0 + part_ref[...] + pltpu.roll(part2_ref[...], 4, 0)
    amp_ref[...] = amplitude
    weight = amplitude / (amplitude * amplitude + 1.0) / walkers_total
    sub = lax.broadcasted_iota(jnp.int32, (8, LANES), 0)
    slot = sub & 3
    upper = sub < 4
    limits = [
        jnp.maximum(slot, jnp.right_shift(sub, 2) + 2 * g).astype(jnp.float32) for g in range(2)
    ]
    others = [(sub & 4) + ((slot + shift) & 3) for shift in (1, 2, 3)]

    def backward(t, carry):
        occ, virt, rank_row, coef_row = load_lists(pay_ref, t)
        left = [[[] for _ in range(16)] for _ in range(4)]
        for h in range(TILE // LANES):
            lanes = slice(h * LANES, (h + 1) * LANES)
            rank = rows8(rank_row[:, lanes])
            coef = rows8(coef_row[:, lanes])
            entries = cell_rows(ent_ref, t * (TILE // LANES) + h)
            cells = masked_cells(entries, rank)
            low = [x * weight for x in pair_products(cells[2], cells[3])]
            top = pair_products(cells[0], cells[1])
            summed = all_rows_sum(determinant(top, low))
            source = t // per_block
            lane_tile = (t % per_block) * (TILE // LANES) + h
            if packed:
                dest = lane_tile // ci_rows * nblk + source
                orb_ref[dest, pl.ds(4 + lane_tile % ci_rows, 1), :] = summed[0:1]
            else:
                ci_ref[source, pl.ds(lane_tile, 1), :] = summed[0:1]
            top = [x * weight for x in top]
            d0, d1 = cofactor_rows(
                cells[0], cells[1], (low[5], -low[4], low[3], low[2], -low[1], low[0])
            )
            d2, d3 = cofactor_rows(
                cells[2], cells[3], (top[5], -top[4], top[3], top[2], -top[1], top[0])
            )
            grads = [d0, d1, d2, d3]
            occ_rows = jnp.concatenate([occ[:, lanes], occ[:, lanes]], axis=0)
            same = [occ_rows == along_rows(occ_rows, other) for other in others]
            sources = []
            for g in range(2):
                items = [grads[a][b] for b in (2 * g, 2 * g + 1) for a in range(4)]
                plain = jnp.where(rank > limits[g], walker_sums(items) * coef, 0.0)
                merged = plain
                for hit, other in zip(same, others):
                    merged = merged + jnp.where(hit, along_rows(plain, other), 0.0)
                high = merged.astype(jnp.bfloat16).astype(jnp.float32)
                both = (high, merged - high)
                sources.append([jnp.where(upper, x, 0.0) for x in both])
                sources.append([jnp.where(upper, pltpu.roll(x, 4, 0), 0.0) for x in both])
            slots = [rows8(occ[a : a + 1, lanes]) for a in range(4)]
            for k in range(8):
                index = []
                for block in (2 * k, 2 * k + 1):
                    place = sub + 8 * block
                    found = jnp.full((8, LANES), 4, jnp.int32)
                    for a in range(4):
                        found = jnp.where(slots[a] == place, a, found)
                    index.append(found)
                for b in range(4):
                    for part in range(2):
                        rows = [along_rows(sources[b][part], x) for x in index]
                        left[b][8 * part + k].append(
                            jnp.concatenate(rows, axis=0).astype(jnp.bfloat16)
                        )
        left = [[jnp.concatenate(x, axis=1) for x in left[b]] for b in range(4)]
        left = jnp.concatenate([jnp.concatenate(left[b], axis=0) for b in range(4)], axis=1)
        right = jnp.concatenate(
            [one_hot(rows16(virt[b : b + 1]), (1.0,)) for b in range(4)], axis=1
        )
        acc[...] += lax.dot_general(
            left, right, (((1,), (1,)), ((), ())), preferred_element_type=jnp.float32
        )
        return carry

    acc[...] = jnp.zeros_like(acc)
    if packed:
        orb_ref[...] = jnp.zeros_like(orb_ref)
    lax.fori_loop(0, tiles, backward, 0, unroll=32)
    total = acc[0:128, :] + acc[128:256, :]
    if packed:
        for dest in range(orb_ref.shape[0]):
            orb_ref[dest, 0:4, :] = total[4 * dest : 4 * dest + 4]
    else:
        orb_ref[...] = total


def sums_kernel(pieces_ref, orb_ref, ci_ref):
    everyone = pieces_ref.shape[0]
    blocks = orb_ref.shape[0] // 4
    totals = []
    for parity in range(2):
        picked = [
            pieces_ref[s] for s in range(everyone) if (s // blocks) % 2 == parity
        ]
        while len(picked) > 1:
            picked = [x + y for x, y in zip(picked[::2], picked[1::2])]
        totals.append(picked[0])
    both = totals[0] + totals[1]
    pair = jnp.concatenate([both[0:4], both[0:4]], axis=0)
    for k in range(blocks // 2):
        orb_ref[8 * k : 8 * k + 8, :] = pair
    ci_ref[...] = jnp.concatenate([totals[0][4:6], totals[1][4:6]], axis=0)


def per_device(
    inverse, virt_ref, new_rows, moved_electron, coefficient, occ_list, virt_list, exc_rank
):
    nocc = inverse.shape[1]
    nvirt = virt_ref.shape[1]
    walk_count = lax.axis_size("walk")
    blocks = lax.axis_size(DET_AXES)
    everyone = walk_count * blocks
    local = coefficient.shape[0]
    half = local // 2
    ndet = half * blocks
    walkers_total = inverse.shape[0] * everyone
    partner = [(u, u ^ 1) for u in range(walk_count)]
    vmem = pl.BlockSpec(memory_space=pltpu.VMEM)
    smem = pl.BlockSpec(memory_space=pltpu.SMEM)
    lists = pltpu.VMEM((blocks, 8, half), jnp.float32)
    params = pltpu.CompilerParams(vmem_limit_bytes=32 << 20)

    payload = pl.pallas_call(
        payload_kernel,
        out_shape=jax.ShapeDtypeStruct((blocks, FIELDS * half // LANES, LANES), jnp.float32),
        in_specs=[vmem] * 4,
        out_specs=vmem,
    )(occ_list, virt_list, exc_rank[None], coefficient[None])
    gathered = lax.all_to_all(payload, DET_AXES, 0, 0)
    mine = pl.pallas_call(
        table_kernel,
        out_shape=jax.ShapeDtypeStruct(inverse.shape, jnp.bfloat16),
        in_specs=[smem] + [vmem] * 3,
        out_specs=vmem,
    )(moved_electron, inverse, new_rows, virt_ref)
    theirs = lax.ppermute(mine, "walk", partner)
    table, back = pl.pallas_call(
        code_kernel,
        out_shape=(
            jax.ShapeDtypeStruct((1024, 2 * LANES), jnp.float8_e4m3fn),
            jax.ShapeDtypeStruct((8, LANES), jnp.float32),
        ),
        in_specs=[vmem] * 2,
        out_specs=(vmem, vmem),
        compiler_params=params,
    )(mine, theirs)
    entries, part = pl.pallas_call(
        select_kernel,
        out_shape=(
            jax.ShapeDtypeStruct((ndet // LANES, 4, 32, LANES), jnp.float32),
            jax.ShapeDtypeStruct((8, LANES), jnp.float32),
        ),
        in_specs=[vmem] * 3,
        out_specs=(vmem, vmem),
        scratch_shapes=[lists],
        compiler_params=params,
    )(table, back, gathered)
    part2 = lax.ppermute(part, "walk", partner)

    ci_size = half // walk_count
    orb_size = nocc * nvirt // everyone
    packed = orb_size == 4 * LANES and ci_size == 2 * LANES and nvirt == LANES
    orb_shape = (everyone, 8, LANES) if packed else (nocc, nvirt)
    amp, ci_part, orb_part = pl.pallas_call(
        lambda *refs: gradient_kernel(float(walkers_total), *refs),
        out_shape=(
            jax.ShapeDtypeStruct((8, LANES), jnp.float32),
            jax.ShapeDtypeStruct((blocks, half // LANES, LANES), jnp.float32),
            jax.ShapeDtypeStruct(orb_shape, jnp.float32),
        ),
        in_specs=[vmem] * 4,
        out_specs=(vmem, vmem, vmem),
        scratch_shapes=[pltpu.VMEM((256, LANES), jnp.float32), lists],
        compiler_params=params,
    )(part, part2, entries, gathered)

    if packed:
        pieces = lax.all_to_all(orb_part, ALL_AXES, 0, 0)
        orb_rows, ci_mine = pl.pallas_call(
            sums_kernel,
            out_shape=(
                jax.ShapeDtypeStruct((blocks * 4, LANES), jnp.float32),
                jax.ShapeDtypeStruct((4, LANES), jnp.float32),
            ),
            in_specs=[vmem],
            out_specs=(vmem, vmem),
        )(pieces)
        ci_mine = ci_mine.reshape(2, ci_size)
        orb_all = lax.all_to_all(orb_rows, DET_AXES, 0, 0, tiled=True)
    else:
        ci_pieces = ci_part.reshape(blocks, walk_count, ci_size).transpose(1, 0, 2)
        orb_pieces = orb_part.reshape(walk_count, blocks, orb_size)
        pieces = jnp.concatenate([orb_pieces, ci_pieces], axis=2).reshape(everyone, -1)
        pieces = lax.all_to_all(pieces, ALL_AXES, 0, 0)
        pieces = pieces.reshape(walk_count // 2, 2, blocks, -1)
        orb_mine = jnp.sum(pieces[..., :orb_size], axis=(0, 1, 2))
        ci_mine = jnp.sum(pieces[..., orb_size:], axis=(0, 2))
        orb_all = lax.all_to_all(
            jnp.broadcast_to(orb_mine[None], (blocks, orb_size)), DET_AXES, 0, 0
        )
    ci_grad = lax.all_gather(ci_mine, "walk", axis=1).reshape(local)
    return (amp[:4, 0], ci_grad, orb_all.reshape(nocc // walk_count, nvirt))


def solution(mesh):
    return jax.shard_map(
        per_device,
        mesh=mesh,
        in_specs=(
            P(ALL_AXES, None, None),
            P(),
            P(ALL_AXES, None),
            P(ALL_AXES),
            P(DET_AXES),
            P(None, DET_AXES),
            P(None, DET_AXES),
            P(DET_AXES),
        ),
        out_specs=(P(ALL_AXES), P(DET_AXES), P("walk", None)),
        check_vma=False,
    )
```

```python
import jax
import jax.numpy as jnp
from jax import lax
from jax.experimental import pallas as pl
from jax.experimental.pallas import tpu as pltpu
from jax.sharding import PartitionSpec as P

TILE = 256
LANES = 128
FIELDS = 6
DET_AXES = ("det", "exc")
ALL_AXES = ("walk", "det", "exc")
FINE = 64.0


def pair_products(x, y):
    return (
        x[0] * y[1] - y[0] * x[1],
        x[0] * y[2] - y[0] * x[2],
        x[0] * y[3] - y[0] * x[3],
        x[1] * y[2] - y[1] * x[2],
        x[1] * y[3] - y[1] * x[3],
        x[2] * y[3] - y[2] * x[3],
    )


def cofactor_rows(x, y, q):
    qa, qb, qc, qd, qe, qf = q
    dx = (
        y[1] * qa + y[2] * qb + y[3] * qc,
        y[2] * qd + y[3] * qe - y[0] * qa,
        y[3] * qf - y[0] * qb - y[1] * qd,
        -(y[0] * qc + y[1] * qe + y[2] * qf),
    )
    dy = (
        -(x[1] * qa + x[2] * qb + x[3] * qc),
        x[0] * qa - x[2] * qd - x[3] * qe,
        x[0] * qb + x[1] * qd - x[3] * qf,
        x[0] * qc + x[1] * qe + x[2] * qf,
    )
    return dx, dy


def masked_cells(entries, rank):
    cells = []
    for a in range(4):
        row = []
        for b in range(4):
            fill = jnp.float32(1.0 if a == b else 0.0)
            row.append(jnp.where(rank > max(a, b), entries[b][a], fill))
        cells.append(row)
    return cells


def determinant(top, low):
    return (
        top[0] * low[5]
        - top[1] * low[4]
        + top[2] * low[3]
        + top[3] * low[2]
        - top[4] * low[1]
        + top[5] * low[0]
    )


ROW_GATHER = lax.GatherDimensionNumbers(
    offset_dims=(),
    collapsed_slice_dims=(0,),
    start_index_map=(0,),
    operand_batching_dims=(1,),
    start_indices_batching_dims=(1,),
)


def along_rows(x, index):
    return lax.gather(
        x,
        index[..., None],
        ROW_GATHER,
        (1, 1),
        mode=lax.GatherScatterMode.PROMISE_IN_BOUNDS,
    )


def rows8(row):
    return jnp.broadcast_to(row, (8, row.shape[1]))


def rows16(row):
    return jnp.broadcast_to(row, (16, row.shape[1])).astype(jnp.int16)


def iota16():
    return lax.broadcasted_iota(jnp.int32, (16, TILE), 0).astype(jnp.int16)


def one_hot(v16, values):
    base = iota16()
    zero = jnp.zeros((16, TILE), jnp.bfloat16)
    hits = [v16 == base + jnp.int16(16 * k) for k in range(8)]
    parts = [
        jnp.where(hit, jnp.full((16, TILE), value, jnp.bfloat16), zero)
        for value in values
        for hit in hits
    ]
    return jnp.concatenate(parts, axis=0)


def one_hot8(row, values):
    kind = jnp.float8_e4m3fn
    shape = (32, row.shape[1])
    v8 = jnp.broadcast_to(row, shape).astype(jnp.int8)
    base = lax.broadcasted_iota(jnp.int32, shape, 0)
    hits = [v8 == (base + 32 * k).astype(jnp.int8) for k in range(4)]
    zero = jnp.zeros(shape, kind)
    parts = [jnp.where(hit, jnp.full(shape, x, kind), zero) for x in values for hit in hits]
    return jnp.concatenate(parts, axis=0)


def unpack_lists(packed_ref, pay_ref):
    for block in range(pay_ref.shape[0]):
        for x in range(pay_ref.shape[2] // LANES):
            lanes = slice(x * LANES, (x + 1) * LANES)
            pay_ref[block, 0:FIELDS, lanes] = packed_ref[block, FIELDS * x : FIELDS * (x + 1), :]


def load_lists(pay_ref, t):
    per_block = pay_ref.shape[2] // TILE
    lanes = pl.ds(pl.multiple_of((t % per_block) * TILE, TILE), TILE)
    rows = pay_ref[t // per_block, :, lanes]
    codes = rows[0:4].astype(jnp.int32)
    return jnp.right_shift(codes, 7), jnp.bitwise_and(codes, 127), rows[4:5], rows[5:6]


def power_scale(top):
    scale = jnp.ones_like(top)
    back = jnp.ones_like(top)
    for k in (64, 32, 16, 8, 4, 2, 1):
        big = top >= 2.0 ** (5 + k)
        small = top < 2.0 ** (6 - k)
        up = jnp.float32(2.0**k)
        down = jnp.float32(2.0**-k)
        step = jnp.where(big, down, jnp.where(small, up, 1.0))
        undo = jnp.where(big, up, jnp.where(small, down, 1.0))
        top = top * step
        scale = scale * step
        back = back * undo
    return scale, back


def payload_kernel(occ_ref, virt_ref, rank_ref, coef_ref, pay_ref):
    blocks, depth, _ = pay_ref.shape
    half = depth // FIELDS * LANES
    start = pl.multiple_of((lax.axis_index("walk") & 1) * half, LANES)
    lanes = pl.ds(start, half)
    codes = (occ_ref[:, lanes] * 128 + virt_ref[:, lanes]).astype(jnp.float32)
    rank = rank_ref[:, lanes].astype(jnp.float32)
    rows = jnp.concatenate([codes, rank, coef_ref[:, lanes]], axis=0)
    rows = jnp.concatenate(
        [rows[:, x : x + LANES] for x in range(0, half, LANES)], axis=0
    )
    for k in range(blocks):
        pay_ref[k] = rows


def table_kernel(moved_ref, inv_ref, rows_ref, virt_ref, tab):
    rows_of = lax.broadcasted_iota(jnp.int32, (128, LANES), 0)
    fresh = rows_ref[...].astype(jnp.float32)
    for w in range(4):
        basis = jnp.where(
            rows_of == moved_ref[w],
            jnp.broadcast_to(fresh[w : w + 1], (128, LANES)),
            virt_ref[...].astype(jnp.float32),
        )
        tab[w] = jnp.dot(
            inv_ref[w], basis.astype(jnp.bfloat16), preferred_element_type=jnp.float32
        ).astype(jnp.bfloat16)


def code_kernel(mine_ref, theirs_ref, code_ref, back_ref):
    sub = lax.broadcasted_iota(jnp.int32, (8, LANES), 0)
    tables = [
        (mine_ref if w < 4 else theirs_ref)[w % 4].astype(jnp.float32) for w in range(8)
    ]
    tops = jnp.zeros((8, LANES), jnp.float32)
    for w in range(8):
        top = jnp.max(jnp.max(jnp.abs(tables[w]), axis=0, keepdims=True), axis=1, keepdims=True)
        tops = jnp.where(sub == w, jnp.broadcast_to(top, (8, LANES)), tops)
    scale, back = power_scale(tops)
    back_ref[...] = back
    for w in range(8):
        rows = slice(128 * w, 128 * w + 128)
        block = tables[w] * jnp.broadcast_to(scale[w : w + 1], (128, LANES))
        coarse = block.astype(jnp.float8_e4m3fn)
        rest = (block - coarse.astype(jnp.float32)) * FINE
        code_ref[rows, 0:128] = coarse
        code_ref[rows, 128:256] = rest.astype(jnp.float8_e4m3fn)


def cell_rows(ent_ref, lane_tile):
    return [
        [ent_ref[lane_tile, b, pl.ds(a, 8, stride=4), :] for a in range(4)] for b in range(4)
    ]


def select_kernel(tab, back_ref, packed_ref, ent_ref, amp_ref, pay_ref):
    unpack_lists(packed_ref, pay_ref)
    nblk, _, width = pay_ref.shape
    tiles = nblk * width // TILE
    parts = TILE // LANES
    upper = lax.broadcasted_iota(jnp.int32, (8, LANES), 0) < 4
    back = [
        jnp.where(upper, rows8(back_ref[2 * q : 2 * q + 1]), rows8(back_ref[2 * q + 1 : 2 * q + 2]))
        for q in range(4)
    ]

    def forward(t, total):
        occ, virt, rank, coef = load_lists(pay_ref, t)
        occ8 = jnp.concatenate([occ, occ], axis=0)
        split = [occ8[:, h * LANES : (h + 1) * LANES] for h in range(parts)]
        fine = [o & 7 for o in split]
        bits = [[(o & bit) != 0 for bit in (8, 16, 32, 64)] for o in split]
        for b in range(4):
            hot = one_hot8(virt[b : b + 1], (1.0, 1.0 / FINE))
            cols = jnp.dot(tab[...], hot, preferred_element_type=jnp.float32)
            for h in range(parts):
                lanes = slice(h * LANES, (h + 1) * LANES)
                for q in range(4):
                    pair = []
                    for w in (2 * q, 2 * q + 1):
                        level = [
                            along_rows(
                                cols[128 * w + 8 * k : 128 * w + 8 * k + 8, lanes], fine[h]
                            )
                            for k in range(16)
                        ]
                        for step in range(4):
                            level = [
                                jnp.where(bits[h][step], level[2 * k + 1], level[2 * k])
                                for k in range(len(level) // 2)
                            ]
                        pair.append(level[0])
                    ent_ref[t * parts + h, b, 8 * q : 8 * q + 8, :] = (
                        jnp.where(upper, pair[0], pair[1]) * back[q]
                    )
        for h in range(parts):
            lanes = slice(h * LANES, (h + 1) * LANES)
            cells = masked_cells(cell_rows(ent_ref, t * parts + h), rows8(rank[:, lanes]))
            ratio = determinant(
                pair_products(cells[0], cells[1]), pair_products(cells[2], cells[3])
            )
            total = total + ratio * rows8(coef[:, lanes])
        return total

    total = lax.fori_loop(0, tiles, forward, jnp.zeros((8, LANES), jnp.float32), unroll=8)
    amp_ref[...] = jnp.broadcast_to(jnp.sum(total, axis=1, keepdims=True), (8, LANES))


def all_rows_sum(x):
    x = x + pltpu.roll(x, 4, 0)
    x = x + pltpu.roll(x, 2, 0)
    return x + pltpu.roll(x, 1, 0)


def fold(items, dist):
    sub = lax.broadcasted_iota(jnp.int32, (8, LANES), 0)
    first = (sub & dist) == 0
    n = len(items) // 2
    out = []
    for x, y in zip(items[:n], items[n:]):
        x = x + pltpu.roll(x, 8 - dist, 0)
        y = y + pltpu.roll(y, dist, 0)
        out.append(jnp.where(first, x, y))
    return out


def walker_sums(items):
    for dist in (4, 2, 1):
        items = fold(items, dist)
    return items[0]


def gradient_kernel(
    walkers_total, part_ref, part2_ref, ent_ref, packed_ref, amp_ref, ci_ref, orb_ref, acc, pay_ref
):
    unpack_lists(packed_ref, pay_ref)
    nblk, _, width = pay_ref.shape
    per_block = width // TILE
    tiles = nblk * per_block
    packed = len(orb_ref.shape) == 3
    ci_rows = width // LANES * nblk // orb_ref.shape[0]
    amplitude = 1.0 + part_ref[...] + pltpu.roll(part2_ref[...], 4, 0)
    amp_ref[...] = amplitude
    weight = amplitude / (amplitude * amplitude + 1.0) / walkers_total
    sub = lax.broadcasted_iota(jnp.int32, (8, LANES), 0)
    slot = sub & 3
    upper = sub < 4
    limits = [
        jnp.maximum(slot, jnp.right_shift(sub, 2) + 2 * g).astype(jnp.float32) for g in range(2)
    ]
    others = [(sub & 4) + ((slot + shift) & 3) for shift in (1, 2, 3)]

    def backward(t, carry):
        occ, virt, rank_row, coef_row = load_lists(pay_ref, t)
        left = [[[] for _ in range(16)] for _ in range(4)]
        for h in range(TILE // LANES):
            lanes = slice(h * LANES, (h + 1) * LANES)
            rank = rows8(rank_row[:, lanes])
            coef = rows8(coef_row[:, lanes])
            entries = cell_rows(ent_ref, t * (TILE // LANES) + h)
            cells = masked_cells(entries, rank)
            low = [x * weight for x in pair_products(cells[2], cells[3])]
            top = pair_products(cells[0], cells[1])
            summed = all_rows_sum(determinant(top, low))
            source = t // per_block
            lane_tile = (t % per_block) * (TILE // LANES) + h
            if packed:
                dest = lane_tile // ci_rows * nblk + source
                orb_ref[dest, pl.ds(4 + lane_tile % ci_rows, 1), :] = summed[0:1]
            else:
                ci_ref[source, pl.ds(lane_tile, 1), :] = summed[0:1]
            top = [x * weight for x in top]
            d0, d1 = cofactor_rows(
                cells[0], cells[1], (low[5], -low[4], low[3], low[2], -low[1], low[0])
            )
            d2, d3 = cofactor_rows(
                cells[2], cells[3], (top[5], -top[4], top[3], top[2], -top[1], top[0])
            )
            grads = [d0, d1, d2, d3]
            occ_rows = jnp.concatenate([occ[:, lanes], occ[:, lanes]], axis=0)
            same = [occ_rows == along_rows(occ_rows, other) for other in others]
            sources = []
            for g in range(2):
                items = [grads[a][b] for b in (2 * g, 2 * g + 1) for a in range(4)]
                plain = jnp.where(rank > limits[g], walker_sums(items) * coef, 0.0)
                merged = plain
                for hit, other in zip(same, others):
                    merged = merged + jnp.where(hit, along_rows(plain, other), 0.0)
                high = merged.astype(jnp.bfloat16).astype(jnp.float32)
                both = (high, merged - high)
                sources.append([jnp.where(upper, x, 0.0) for x in both])
                sources.append([jnp.where(upper, pltpu.roll(x, 4, 0), 0.0) for x in both])
            slots = [rows8(occ[a : a + 1, lanes]) for a in range(4)]
            for k in range(8):
                index = []
                for block in (2 * k, 2 * k + 1):
                    place = sub + 8 * block
                    found = jnp.full((8, LANES), 4, jnp.int32)
                    for a in range(4):
                        found = jnp.where(slots[a] == place, a, found)
                    index.append(found)
                for b in range(4):
                    for part in range(2):
                        rows = [along_rows(sources[b][part], x) for x in index]
                        left[b][8 * part + k].append(
                            jnp.concatenate(rows, axis=0).astype(jnp.bfloat16)
                        )
        left = [[jnp.concatenate(x, axis=1) for x in left[b]] for b in range(4)]
        left = jnp.concatenate([jnp.concatenate(left[b], axis=0) for b in range(4)], axis=1)
        right = jnp.concatenate(
            [one_hot(rows16(virt[b : b + 1]), (1.0,)) for b in range(4)], axis=1
        )
        acc[...] += lax.dot_general(
            left, right, (((1,), (1,)), ((), ())), preferred_element_type=jnp.float32
        )
        return carry

    acc[...] = jnp.zeros_like(acc)
    if packed:
        orb_ref[...] = jnp.zeros_like(orb_ref)
    lax.fori_loop(0, tiles, backward, 0, unroll=32)
    total = acc[0:128, :] + acc[128:256, :]
    if packed:
        for dest in range(orb_ref.shape[0]):
            orb_ref[dest, 0:4, :] = total[4 * dest : 4 * dest + 4]
    else:
        orb_ref[...] = total


def sums_kernel(pieces_ref, orb_ref, ci_ref):
    everyone = pieces_ref.shape[0]
    blocks = orb_ref.shape[0] // 4
    totals = []
    for parity in range(2):
        picked = [
            pieces_ref[s] for s in range(everyone) if (s // blocks) % 2 == parity
        ]
        while len(picked) > 1:
            picked = [x + y for x, y in zip(picked[::2], picked[1::2])]
        totals.append(picked[0])
    both = totals[0] + totals[1]
    pair = jnp.concatenate([both[0:4], both[0:4]], axis=0)
    for k in range(blocks // 2):
        orb_ref[8 * k : 8 * k + 8, :] = pair
    ci_ref[...] = jnp.concatenate([totals[0][4:6], totals[1][4:6]], axis=0)


def per_device(
    inverse, virt_ref, new_rows, moved_electron, coefficient, occ_list, virt_list, exc_rank
):
    nocc = inverse.shape[1]
    nvirt = virt_ref.shape[1]
    walk_count = lax.axis_size("walk")
    blocks = lax.axis_size(DET_AXES)
    everyone = walk_count * blocks
    local = coefficient.shape[0]
    half = local // 2
    ndet = half * blocks
    walkers_total = inverse.shape[0] * everyone
    partner = [(u, u ^ 1) for u in range(walk_count)]
    vmem = pl.BlockSpec(memory_space=pltpu.VMEM)
    smem = pl.BlockSpec(memory_space=pltpu.SMEM)
    lists = pltpu.VMEM((blocks, 8, half), jnp.float32)
    params = pltpu.CompilerParams(vmem_limit_bytes=32 << 20)
    small = pltpu.CompilerParams(vmem_limit_bytes=8 << 20)

    payload = pl.pallas_call(
        payload_kernel,
        out_shape=jax.ShapeDtypeStruct((blocks, FIELDS * half // LANES, LANES), jnp.float32),
        in_specs=[vmem] * 4,
        out_specs=vmem,
    )(occ_list, virt_list, exc_rank[None], coefficient[None])
    gathered = lax.all_to_all(payload, DET_AXES, 0, 0)
    mine = pl.pallas_call(
        table_kernel,
        out_shape=jax.ShapeDtypeStruct(inverse.shape, jnp.bfloat16),
        in_specs=[smem] + [vmem] * 3,
        out_specs=vmem,
    )(moved_electron, inverse, new_rows, virt_ref)
    theirs = lax.ppermute(mine, "walk", partner)
    table, back = pl.pallas_call(
        code_kernel,
        out_shape=(
            jax.ShapeDtypeStruct((1024, 2 * LANES), jnp.float8_e4m3fn),
            jax.ShapeDtypeStruct((8, LANES), jnp.float32),
        ),
        in_specs=[vmem] * 2,
        out_specs=(vmem, vmem),
        compiler_params=params,
    )(mine, theirs)
    entries, part = pl.pallas_call(
        select_kernel,
        out_shape=(
            jax.ShapeDtypeStruct((ndet // LANES, 4, 32, LANES), jnp.float32),
            jax.ShapeDtypeStruct((8, LANES), jnp.float32),
        ),
        in_specs=[vmem] * 3,
        out_specs=(vmem, vmem),
        scratch_shapes=[lists],
        compiler_params=params,
    )(table, back, gathered)
    part2 = lax.ppermute(part, "walk", partner)

    ci_size = half // walk_count
    orb_size = nocc * nvirt // everyone
    packed = orb_size == 4 * LANES and ci_size == 2 * LANES and nvirt == LANES
    orb_shape = (everyone, 8, LANES) if packed else (nocc, nvirt)
    amp, ci_part, orb_part = pl.pallas_call(
        lambda *refs: gradient_kernel(float(walkers_total), *refs),
        out_shape=(
            jax.ShapeDtypeStruct((8, LANES), jnp.float32),
            jax.ShapeDtypeStruct((blocks, half // LANES, LANES), jnp.float32),
            jax.ShapeDtypeStruct(orb_shape, jnp.float32),
        ),
        in_specs=[vmem] * 4,
        out_specs=(vmem, vmem, vmem),
        scratch_shapes=[pltpu.VMEM((256, LANES), jnp.float32), lists],
        compiler_params=params,
    )(part, part2, entries, gathered)

    if packed:
        pieces = lax.all_to_all(orb_part, ALL_AXES, 0, 0)
        orb_rows, ci_mine = pl.pallas_call(
            sums_kernel,
            out_shape=(
                jax.ShapeDtypeStruct((blocks * 4, LANES), jnp.float32),
                jax.ShapeDtypeStruct((4, LANES), jnp.float32),
            ),
            in_specs=[vmem],
            out_specs=(vmem, vmem),
            compiler_params=small,
        )(pieces)
        ci_mine = ci_mine.reshape(2, ci_size)
        orb_all = lax.all_to_all(orb_rows, DET_AXES, 0, 0, tiled=True)
    else:
        ci_pieces = ci_part.reshape(blocks, walk_count, ci_size).transpose(1, 0, 2)
        orb_pieces = orb_part.reshape(walk_count, blocks, orb_size)
        pieces = jnp.concatenate([orb_pieces, ci_pieces], axis=2).reshape(everyone, -1)
        pieces = lax.all_to_all(pieces, ALL_AXES, 0, 0)
        pieces = pieces.reshape(walk_count // 2, 2, blocks, -1)
        orb_mine = jnp.sum(pieces[..., :orb_size], axis=(0, 1, 2))
        ci_mine = jnp.sum(pieces[..., orb_size:], axis=(0, 2))
        orb_all = lax.all_to_all(
            jnp.broadcast_to(orb_mine[None], (blocks, orb_size)), DET_AXES, 0, 0
        )
    ci_grad = lax.all_gather(ci_mine, "walk", axis=1).reshape(local)
    return (amp[:4, 0], ci_grad, orb_all.reshape(nocc // walk_count, nvirt))


def solution(mesh):
    return jax.shard_map(
        per_device,
        mesh=mesh,
        in_specs=(
            P(ALL_AXES, None, None),
            P(),
            P(ALL_AXES, None),
            P(ALL_AXES),
            P(DET_AXES),
            P(None, DET_AXES),
            P(None, DET_AXES),
            P(DET_AXES),
        ),
        out_specs=(P(ALL_AXES), P(DET_AXES), P("walk", None)),
        check_vma=False,
    )
```

```python
import jax
import jax.numpy as jnp
from jax import lax
from jax.experimental import pallas as pl
from jax.experimental.pallas import tpu as pltpu
from jax.sharding import PartitionSpec as P

TILE = 256
LANES = 128
FIELDS = 6
DET_AXES = ("det", "exc")
ALL_AXES = ("walk", "det", "exc")
FINE = 64.0


def pair_products(x, y):
    return (
        x[0] * y[1] - y[0] * x[1],
        x[0] * y[2] - y[0] * x[2],
        x[0] * y[3] - y[0] * x[3],
        x[1] * y[2] - y[1] * x[2],
        x[1] * y[3] - y[1] * x[3],
        x[2] * y[3] - y[2] * x[3],
    )


def cofactor_rows(x, y, q):
    qa, qb, qc, qd, qe, qf = q
    dx = (
        y[1] * qa + y[2] * qb + y[3] * qc,
        y[2] * qd + y[3] * qe - y[0] * qa,
        y[3] * qf - y[0] * qb - y[1] * qd,
        -(y[0] * qc + y[1] * qe + y[2] * qf),
    )
    dy = (
        -(x[1] * qa + x[2] * qb + x[3] * qc),
        x[0] * qa - x[2] * qd - x[3] * qe,
        x[0] * qb + x[1] * qd - x[3] * qf,
        x[0] * qc + x[1] * qe + x[2] * qf,
    )
    return dx, dy


def masked_cells(entries, rank):
    cells = []
    for a in range(4):
        row = []
        for b in range(4):
            fill = jnp.float32(1.0 if a == b else 0.0)
            row.append(jnp.where(rank > max(a, b), entries[b][a], fill))
        cells.append(row)
    return cells


def determinant(top, low):
    return (
        top[0] * low[5]
        - top[1] * low[4]
        + top[2] * low[3]
        + top[3] * low[2]
        - top[4] * low[1]
        + top[5] * low[0]
    )


ROW_GATHER = lax.GatherDimensionNumbers(
    offset_dims=(),
    collapsed_slice_dims=(0,),
    start_index_map=(0,),
    operand_batching_dims=(1,),
    start_indices_batching_dims=(1,),
)


def along_rows(x, index):
    return lax.gather(
        x,
        index[..., None],
        ROW_GATHER,
        (1, 1),
        mode=lax.GatherScatterMode.PROMISE_IN_BOUNDS,
    )


def rows8(row):
    return jnp.broadcast_to(row, (8, row.shape[1]))


def rows16(row):
    return jnp.broadcast_to(row, (16, row.shape[1])).astype(jnp.int16)


def iota16():
    return lax.broadcasted_iota(jnp.int32, (16, TILE), 0).astype(jnp.int16)


def one_hot(v16, values):
    base = iota16()
    zero = jnp.zeros((16, TILE), jnp.bfloat16)
    hits = [v16 == base + jnp.int16(16 * k) for k in range(8)]
    parts = [
        jnp.where(hit, jnp.full((16, TILE), value, jnp.bfloat16), zero)
        for value in values
        for hit in hits
    ]
    return jnp.concatenate(parts, axis=0)


def one_hot8(row, values):
    kind = jnp.float8_e4m3fn
    shape = (32, row.shape[1])
    v8 = jnp.broadcast_to(row, shape).astype(jnp.int8)
    base = lax.broadcasted_iota(jnp.int32, shape, 0)
    hits = [v8 == (base + 32 * k).astype(jnp.int8) for k in range(4)]
    zero = jnp.zeros(shape, kind)
    parts = [jnp.where(hit, jnp.full(shape, x, kind), zero) for x in values for hit in hits]
    return jnp.concatenate(parts, axis=0)


def unpack_lists(packed_ref, pay_ref):
    for block in range(pay_ref.shape[0]):
        for x in range(pay_ref.shape[2] // LANES):
            lanes = slice(x * LANES, (x + 1) * LANES)
            pay_ref[block, 0:FIELDS, lanes] = packed_ref[block, FIELDS * x : FIELDS * (x + 1), :]


def load_lists(pay_ref, t):
    per_block = pay_ref.shape[2] // TILE
    lanes = pl.ds(pl.multiple_of((t % per_block) * TILE, TILE), TILE)
    rows = pay_ref[t // per_block, :, lanes]
    codes = rows[0:4].astype(jnp.int32)
    return jnp.right_shift(codes, 7), jnp.bitwise_and(codes, 127), rows[4:5], rows[5:6]


def power_scale(top):
    scale = jnp.ones_like(top)
    back = jnp.ones_like(top)
    for k in (64, 32, 16, 8, 4, 2, 1):
        big = top >= 2.0 ** (5 + k)
        small = top < 2.0 ** (6 - k)
        up = jnp.float32(2.0**k)
        down = jnp.float32(2.0**-k)
        step = jnp.where(big, down, jnp.where(small, up, 1.0))
        undo = jnp.where(big, up, jnp.where(small, down, 1.0))
        top = top * step
        scale = scale * step
        back = back * undo
    return scale, back


def payload_kernel(occ_ref, virt_ref, rank_ref, coef_ref, pay_ref):
    blocks, depth, _ = pay_ref.shape
    half = depth // FIELDS * LANES
    start = pl.multiple_of((lax.axis_index("walk") & 1) * half, LANES)
    lanes = pl.ds(start, half)
    codes = (occ_ref[:, lanes] * 128 + virt_ref[:, lanes]).astype(jnp.float32)
    rank = rank_ref[:, lanes].astype(jnp.float32)
    rows = jnp.concatenate([codes, rank, coef_ref[:, lanes]], axis=0)
    rows = jnp.concatenate(
        [rows[:, x : x + LANES] for x in range(0, half, LANES)], axis=0
    )
    for k in range(blocks):
        pay_ref[k] = rows


def table_kernel(moved_ref, inv_ref, rows_ref, virt_ref, tab):
    rows_of = lax.broadcasted_iota(jnp.int32, (128, LANES), 0)
    fresh = rows_ref[...].astype(jnp.float32)
    for w in range(4):
        basis = jnp.where(
            rows_of == moved_ref[w],
            jnp.broadcast_to(fresh[w : w + 1], (128, LANES)),
            virt_ref[...].astype(jnp.float32),
        )
        tab[w] = jnp.dot(
            inv_ref[w], basis.astype(jnp.bfloat16), preferred_element_type=jnp.float32
        ).astype(jnp.bfloat16)


def code_kernel(mine_ref, theirs_ref, code_ref, back_ref):
    sub = lax.broadcasted_iota(jnp.int32, (8, LANES), 0)
    tables = [
        (mine_ref if w < 4 else theirs_ref)[w % 4].astype(jnp.float32) for w in range(8)
    ]
    tops = jnp.zeros((8, LANES), jnp.float32)
    for w in range(8):
        top = jnp.max(jnp.max(jnp.abs(tables[w]), axis=0, keepdims=True), axis=1, keepdims=True)
        tops = jnp.where(sub == w, jnp.broadcast_to(top, (8, LANES)), tops)
    scale, back = power_scale(tops)
    back_ref[...] = back
    for w in range(8):
        rows = slice(128 * w, 128 * w + 128)
        block = tables[w] * jnp.broadcast_to(scale[w : w + 1], (128, LANES))
        coarse = block.astype(jnp.float8_e4m3fn)
        rest = (block - coarse.astype(jnp.float32)) * FINE
        code_ref[rows, 0:128] = coarse
        code_ref[rows, 128:256] = rest.astype(jnp.float8_e4m3fn)


def cell_rows(ent_ref, lane_tile):
    return [
        [ent_ref[lane_tile, b, pl.ds(a, 8, stride=4), :] for a in range(4)] for b in range(4)
    ]


def select_kernel(tab, back_ref, packed_ref, ent_ref, amp_ref, pay_ref):
    unpack_lists(packed_ref, pay_ref)
    nblk, _, width = pay_ref.shape
    tiles = nblk * width // TILE
    parts = TILE // LANES
    upper = lax.broadcasted_iota(jnp.int32, (8, LANES), 0) < 4
    back = [
        jnp.where(upper, rows8(back_ref[2 * q : 2 * q + 1]), rows8(back_ref[2 * q + 1 : 2 * q + 2]))
        for q in range(4)
    ]

    def forward(t, total):
        occ, virt, rank, coef = load_lists(pay_ref, t)
        occ8 = jnp.concatenate([occ, occ], axis=0)
        split = [occ8[:, h * LANES : (h + 1) * LANES] for h in range(parts)]
        fine = [o & 7 for o in split]
        bits = [[(o & bit) != 0 for bit in (8, 16, 32, 64)] for o in split]
        for b in range(4):
            hot = one_hot8(virt[b : b + 1], (1.0, 1.0 / FINE))
            cols = jnp.dot(tab[...], hot, preferred_element_type=jnp.float32)
            for h in range(parts):
                lanes = slice(h * LANES, (h + 1) * LANES)
                for q in range(4):
                    pair = []
                    for w in (2 * q, 2 * q + 1):
                        level = [
                            along_rows(
                                cols[128 * w + 8 * k : 128 * w + 8 * k + 8, lanes], fine[h]
                            )
                            for k in range(16)
                        ]
                        for step in range(4):
                            level = [
                                jnp.where(bits[h][step], level[2 * k + 1], level[2 * k])
                                for k in range(len(level) // 2)
                            ]
                        pair.append(level[0])
                    ent_ref[t * parts + h, b, 8 * q : 8 * q + 8, :] = (
                        jnp.where(upper, pair[0], pair[1]) * back[q]
                    )
        for h in range(parts):
            lanes = slice(h * LANES, (h + 1) * LANES)
            cells = masked_cells(cell_rows(ent_ref, t * parts + h), rows8(rank[:, lanes]))
            ratio = determinant(
                pair_products(cells[0], cells[1]), pair_products(cells[2], cells[3])
            )
            total = total + ratio * rows8(coef[:, lanes])
        return total

    total = lax.fori_loop(0, tiles, forward, jnp.zeros((8, LANES), jnp.float32), unroll=8)
    amp_ref[...] = jnp.broadcast_to(jnp.sum(total, axis=1, keepdims=True), (8, LANES))


def all_rows_sum(x):
    x = x + pltpu.roll(x, 4, 0)
    x = x + pltpu.roll(x, 2, 0)
    return x + pltpu.roll(x, 1, 0)


def fold(items, dist):
    sub = lax.broadcasted_iota(jnp.int32, (8, LANES), 0)
    first = (sub & dist) == 0
    n = len(items) // 2
    out = []
    for x, y in zip(items[:n], items[n:]):
        out.append(jnp.where(first, x, y) + along_rows(jnp.where(first, y, x), sub ^ dist))
    return out


def walker_sums(items):
    for dist in (4, 2, 1):
        items = fold(items, dist)
    return items[0]


def gradient_kernel(
    walkers_total, part_ref, part2_ref, ent_ref, packed_ref, amp_ref, ci_ref, orb_ref, acc, pay_ref
):
    unpack_lists(packed_ref, pay_ref)
    nblk, _, width = pay_ref.shape
    per_block = width // TILE
    tiles = nblk * per_block
    packed = len(orb_ref.shape) == 3
    ci_rows = width // LANES * nblk // orb_ref.shape[0]
    amplitude = 1.0 + part_ref[...] + pltpu.roll(part2_ref[...], 4, 0)
    amp_ref[...] = amplitude
    weight = amplitude / (amplitude * amplitude + 1.0) / walkers_total
    sub = lax.broadcasted_iota(jnp.int32, (8, LANES), 0)
    slot = sub & 3
    upper = sub < 4
    limits = [
        jnp.maximum(slot, jnp.right_shift(sub, 2) + 2 * g).astype(jnp.float32) for g in range(2)
    ]
    others = [(sub & 4) + ((slot + shift) & 3) for shift in (1, 2, 3)]

    def backward(t, carry):
        occ, virt, rank_row, coef_row = load_lists(pay_ref, t)
        left = [[[] for _ in range(16)] for _ in range(4)]
        for h in range(TILE // LANES):
            lanes = slice(h * LANES, (h + 1) * LANES)
            rank = rows8(rank_row[:, lanes])
            coef = rows8(coef_row[:, lanes])
            entries = cell_rows(ent_ref, t * (TILE // LANES) + h)
            cells = masked_cells(entries, rank)
            low = [x * weight for x in pair_products(cells[2], cells[3])]
            top = pair_products(cells[0], cells[1])
            summed = all_rows_sum(determinant(top, low))
            source = t // per_block
            lane_tile = (t % per_block) * (TILE // LANES) + h
            if packed:
                dest = lane_tile // ci_rows * nblk + source
                orb_ref[dest, pl.ds(4 + lane_tile % ci_rows, 1), :] = summed[0:1]
            else:
                ci_ref[source, pl.ds(lane_tile, 1), :] = summed[0:1]
            top = [x * weight for x in top]
            d0, d1 = cofactor_rows(
                cells[0], cells[1], (low[5], -low[4], low[3], low[2], -low[1], low[0])
            )
            d2, d3 = cofactor_rows(
                cells[2], cells[3], (top[5], -top[4], top[3], top[2], -top[1], top[0])
            )
            grads = [d0, d1, d2, d3]
            occ_rows = jnp.concatenate([occ[:, lanes], occ[:, lanes]], axis=0)
            same = [occ_rows == along_rows(occ_rows, other) for other in others]
            sources = []
            for g in range(2):
                items = [grads[a][b] for b in (2 * g, 2 * g + 1) for a in range(4)]
                plain = jnp.where(rank > limits[g], walker_sums(items) * coef, 0.0)
                merged = plain
                for hit, other in zip(same, others):
                    merged = merged + jnp.where(hit, along_rows(plain, other), 0.0)
                high = merged.astype(jnp.bfloat16).astype(jnp.float32)
                both = (high, merged - high)
                sources.append([jnp.where(upper, x, 0.0) for x in both])
                sources.append([jnp.where(upper, pltpu.roll(x, 4, 0), 0.0) for x in both])
            slots = [rows8(occ[a : a + 1, lanes]) for a in range(4)]
            for k in range(8):
                index = []
                for block in (2 * k, 2 * k + 1):
                    place = sub + 8 * block
                    found = jnp.full((8, LANES), 4, jnp.int32)
                    for a in range(4):
                        found = jnp.where(slots[a] == place, a, found)
                    index.append(found)
                for b in range(4):
                    for part in range(2):
                        rows = [along_rows(sources[b][part], x) for x in index]
                        left[b][8 * part + k].append(
                            jnp.concatenate(rows, axis=0).astype(jnp.bfloat16)
                        )
        left = [[jnp.concatenate(x, axis=1) for x in left[b]] for b in range(4)]
        left = jnp.concatenate([jnp.concatenate(left[b], axis=0) for b in range(4)], axis=1)
        right = jnp.concatenate(
            [one_hot(rows16(virt[b : b + 1]), (1.0,)) for b in range(4)], axis=1
        )
        acc[...] += lax.dot_general(
            left, right, (((1,), (1,)), ((), ())), preferred_element_type=jnp.float32
        )
        return carry

    acc[...] = jnp.zeros_like(acc)
    if packed:
        orb_ref[...] = jnp.zeros_like(orb_ref)
    lax.fori_loop(0, tiles, backward, 0, unroll=32)
    total = acc[0:128, :] + acc[128:256, :]
    if packed:
        for dest in range(orb_ref.shape[0]):
            orb_ref[dest, 0:4, :] = total[4 * dest : 4 * dest + 4]
    else:
        orb_ref[...] = total


def sums_kernel(pieces_ref, orb_ref, ci_ref):
    everyone = pieces_ref.shape[0]
    blocks = orb_ref.shape[0] // 4
    totals = []
    for parity in range(2):
        picked = [
            pieces_ref[s] for s in range(everyone) if (s // blocks) % 2 == parity
        ]
        while len(picked) > 1:
            picked = [x + y for x, y in zip(picked[::2], picked[1::2])]
        totals.append(picked[0])
    both = totals[0] + totals[1]
    pair = jnp.concatenate([both[0:4], both[0:4]], axis=0)
    for k in range(blocks // 2):
        orb_ref[8 * k : 8 * k + 8, :] = pair
    ci_ref[...] = jnp.concatenate([totals[0][4:6], totals[1][4:6]], axis=0)


def per_device(
    inverse, virt_ref, new_rows, moved_electron, coefficient, occ_list, virt_list, exc_rank
):
    nocc = inverse.shape[1]
    nvirt = virt_ref.shape[1]
    walk_count = lax.axis_size("walk")
    blocks = lax.axis_size(DET_AXES)
    everyone = walk_count * blocks
    local = coefficient.shape[0]
    half = local // 2
    ndet = half * blocks
    walkers_total = inverse.shape[0] * everyone
    partner = [(u, u ^ 1) for u in range(walk_count)]
    vmem = pl.BlockSpec(memory_space=pltpu.VMEM)
    smem = pl.BlockSpec(memory_space=pltpu.SMEM)
    lists = pltpu.VMEM((blocks, 8, half), jnp.float32)
    params = pltpu.CompilerParams(vmem_limit_bytes=32 << 20)
    small = pltpu.CompilerParams(vmem_limit_bytes=8 << 20)

    payload = pl.pallas_call(
        payload_kernel,
        out_shape=jax.ShapeDtypeStruct((blocks, FIELDS * half // LANES, LANES), jnp.float32),
        in_specs=[vmem] * 4,
        out_specs=vmem,
    )(occ_list, virt_list, exc_rank[None], coefficient[None])
    gathered = lax.all_to_all(payload, DET_AXES, 0, 0)
    mine = pl.pallas_call(
        table_kernel,
        out_shape=jax.ShapeDtypeStruct(inverse.shape, jnp.bfloat16),
        in_specs=[smem] + [vmem] * 3,
        out_specs=vmem,
    )(moved_electron, inverse, new_rows, virt_ref)
    theirs = lax.ppermute(mine, "walk", partner)
    table, back = pl.pallas_call(
        code_kernel,
        out_shape=(
            jax.ShapeDtypeStruct((1024, 2 * LANES), jnp.float8_e4m3fn),
            jax.ShapeDtypeStruct((8, LANES), jnp.float32),
        ),
        in_specs=[vmem] * 2,
        out_specs=(vmem, vmem),
        compiler_params=params,
    )(mine, theirs)
    entries, part = pl.pallas_call(
        select_kernel,
        out_shape=(
            jax.ShapeDtypeStruct((ndet // LANES, 4, 32, LANES), jnp.float32),
            jax.ShapeDtypeStruct((8, LANES), jnp.float32),
        ),
        in_specs=[vmem] * 3,
        out_specs=(vmem, vmem),
        scratch_shapes=[lists],
        compiler_params=params,
    )(table, back, gathered)
    part2 = lax.ppermute(part, "walk", partner)

    ci_size = half // walk_count
    orb_size = nocc * nvirt // everyone
    packed = orb_size == 4 * LANES and ci_size == 2 * LANES and nvirt == LANES
    orb_shape = (everyone, 8, LANES) if packed else (nocc, nvirt)
    amp, ci_part, orb_part = pl.pallas_call(
        lambda *refs: gradient_kernel(float(walkers_total), *refs),
        out_shape=(
            jax.ShapeDtypeStruct((8, LANES), jnp.float32),
            jax.ShapeDtypeStruct((blocks, half // LANES, LANES), jnp.float32),
            jax.ShapeDtypeStruct(orb_shape, jnp.float32),
        ),
        in_specs=[vmem] * 4,
        out_specs=(vmem, vmem, vmem),
        scratch_shapes=[pltpu.VMEM((256, LANES), jnp.float32), lists],
        compiler_params=params,
    )(part, part2, entries, gathered)

    if packed:
        pieces = lax.all_to_all(orb_part, ALL_AXES, 0, 0)
        orb_rows, ci_mine = pl.pallas_call(
            sums_kernel,
            out_shape=(
                jax.ShapeDtypeStruct((blocks * 4, LANES), jnp.float32),
                jax.ShapeDtypeStruct((4, LANES), jnp.float32),
            ),
            in_specs=[vmem],
            out_specs=(vmem, vmem),
            compiler_params=small,
        )(pieces)
        ci_mine = ci_mine.reshape(2, ci_size)
        orb_all = lax.all_to_all(orb_rows, DET_AXES, 0, 0, tiled=True)
    else:
        ci_pieces = ci_part.reshape(blocks, walk_count, ci_size).transpose(1, 0, 2)
        orb_pieces = orb_part.reshape(walk_count, blocks, orb_size)
        pieces = jnp.concatenate([orb_pieces, ci_pieces], axis=2).reshape(everyone, -1)
        pieces = lax.all_to_all(pieces, ALL_AXES, 0, 0)
        pieces = pieces.reshape(walk_count // 2, 2, blocks, -1)
        orb_mine = jnp.sum(pieces[..., :orb_size], axis=(0, 1, 2))
        ci_mine = jnp.sum(pieces[..., orb_size:], axis=(0, 2))
        orb_all = lax.all_to_all(
            jnp.broadcast_to(orb_mine[None], (blocks, orb_size)), DET_AXES, 0, 0
        )
    ci_grad = lax.all_gather(ci_mine, "walk", axis=1).reshape(local)
    return (amp[:4, 0], ci_grad, orb_all.reshape(nocc // walk_count, nvirt))


def solution(mesh):
    return jax.shard_map(
        per_device,
        mesh=mesh,
        in_specs=(
            P(ALL_AXES, None, None),
            P(),
            P(ALL_AXES, None),
            P(ALL_AXES),
            P(DET_AXES),
            P(None, DET_AXES),
            P(None, DET_AXES),
            P(DET_AXES),
        ),
        out_specs=(P(ALL_AXES), P(DET_AXES), P("walk", None)),
        check_vma=False,
    )
```
